128 devices in a mesh: layer: 16 (over x, z), row: 2 (over y_hi), col: 4 (over y_lo, core).
Axes of the slice: x: 4, y: 4 (y_hi: 2, y_lo: 2; y = y_hi * 2 + y_lo), z: 4, core: 2. Of those that a mesh axis runs over, the one named last changes fastest.
Arguments:
- c_guess: float32 [16, 1, 64, 16, 512], P('layer', None, None, 'row', 'col'), may hold values from -6 to 6
- adjoint_guess: float32 [16, 1, 64, 16, 512], P('layer', None, None, 'row', 'col'), may hold values from -6 to 6
- weights: bfloat16 [128, 9, 64, 64], P('layer'), may hold values from -0.25 to 0.25
- biases: float32 [128, 64], P('layer'), may hold values from -2 to 2
- coarse_gain: float32 [16, 64], P('layer'), may hold values from 0 to 1
Outputs:
- c_states: float32 [16, 1, 64, 16, 512], P('layer', None, None, 'row', 'col')
- adjoint_ends: float32 [16, 1, 64, 16, 512], P('layer', None, None, 'row', 'col')
- weight_grad: float32 [128, 9, 64, 64], P('layer')
The draws below stay inside these ranges and needn't reach their ends.
All inputs are finite; a program needn't handle non-finite values.
Results may differ from the reference program's by a relative error of at most 0.0049.
Values may be sent and summed in bfloat16 or wider, within the bound.
A program may use at most 128 MiB of HBM per device.

```python
import math
import jax
import jax.numpy as jnp
from jax import lax

FEATURE_MAPS = 64
L_DEV = 8
IMAGES = 1
BLOCKS = 128
H = 16
W = 512
N_LAYER = 16


def draw_coarse_gain(key, part):
    processor_array = BLOCKS // L_DEV
    first, second, remaining_piece = jax.random.split(key, 3)
    log_decay_factor = jax.random.uniform(first, (FEATURE_MAPS,), jnp.float32, math.log(0.2), math.log(40.0))
    stencil_extent = jax.random.uniform(second, (processor_array, FEATURE_MAPS), jnp.float32, 0.6, 1.4)
    correction_sweep = jnp.where(jax.random.uniform(remaining_piece, (processor_array, FEATURE_MAPS), jnp.float32) < 0.08, 0.6, 1.0)
    return (jnp.exp(-jnp.exp(log_decay_factor)[None, :] * stencil_extent / processor_array) * correction_sweep).astype(jnp.float32)


def level_of(key, dims, cuts, low, top_value):
    gain, own = 1.0, jax.random.fold_in(key, 6)
    for dim, parts in cuts:
        draws = jnp.exp(jax.random.uniform(jax.random.fold_in(own, dim), (parts,), jnp.float32, low / len(cuts), top_value / len(cuts)))
        gain = gain * jnp.repeat(draws, dims[dim] // parts).reshape([-1 if axis == dim else 1 for axis in range(len(dims))])
    return gain


def centred(rng, extent, spread, bound, pieces=(), held_as=jnp.bfloat16):
    drawn = spread * jax.random.normal(rng, extent, jnp.float32)
    if pieces:
        drawn = drawn * level_of(rng, extent, pieces, -0.22, 0.18)
    return jnp.clip(drawn, -bound, bound).astype(held_as)


def setup_inputs(seed: int = 0) -> dict:
    streams_of = jax.random.split(jax.random.key(seed), 6)
    return {
        "c_guess": centred(streams_of[0], (N_LAYER, IMAGES, FEATURE_MAPS, H, W), 1.0, 6.0, ((0, 16), (3, 2), (4, 4)), jnp.float32),
        "adjoint_guess": centred(streams_of[1], (N_LAYER, IMAGES, FEATURE_MAPS, H, W), 1.0, 6.0, ((0, 16), (3, 2), (4, 4)), jnp.float32),
        "weights": centred(streams_of[2], (BLOCKS, 9, FEATURE_MAPS, FEATURE_MAPS), (9 * FEATURE_MAPS) ** -0.5, 0.25, ((0, 16),)),
        "biases": centred(streams_of[3], (BLOCKS, FEATURE_MAPS), 0.3, 2.0, ((0, 16),), jnp.float32),
        "coarse_gain": draw_coarse_gain(jax.random.fold_in(streams_of[5], 71), 0),
    }


step_size = 0.5

def pad_field(field):
    return jnp.pad(field, ((0, 0), (0, 0), (1, 1), (1, 1)))

def convolve(padded, kernel):
    rows = padded.shape[2] - 2
    cols = padded.shape[3] - 2
    total = jnp.zeros((padded.shape[0], kernel.shape[1], rows, cols), jnp.float32)
    for tap_idx in range(9):
        row_off = tap_idx // 3
        col_off = tap_idx % 3
        window = padded[:, :, row_off:row_off + rows, col_off:col_off + cols].astype(jnp.float32)
        total = total + jnp.einsum('oc,bchw->bohw', kernel[tap_idx].astype(jnp.float32), window)
    return total

def convolve_back(padded, kernel):
    rows = padded.shape[2] - 2
    cols = padded.shape[3] - 2
    total = jnp.zeros((padded.shape[0], kernel.shape[2], rows, cols), jnp.float32)
    for tap_idx in range(9):
        row_off = 2 - tap_idx // 3
        col_off = 2 - tap_idx % 3
        window = padded[:, :, row_off:row_off + rows, col_off:col_off + cols].astype(jnp.float32)
        total = total + jnp.einsum('oc,bohw->bchw', kernel[tap_idx].astype(jnp.float32), window)
    return total

def kernel_grad(cotan, padded):
    rows = cotan.shape[2]
    cols = cotan.shape[3]
    taps = []
    for tap_idx in range(9):
        row_off = tap_idx // 3
        col_off = tap_idx % 3
        window = padded[:, :, row_off:row_off + rows, col_off:col_off + cols].astype(jnp.float32)
        taps.append(jnp.einsum('bohw,bchw->oc', cotan.astype(jnp.float32), window))
    return step_size * jnp.stack(taps)

def relax(input_images):
    start, adjoint, kernels, offsets = input_images
    state = start
    states = []
    paddeds = []
    for block_idx in range(L_DEV):
        active = jnp.tanh(state).astype(jnp.bfloat16)
        padded = pad_field(active)
        states.append(state)
        paddeds.append(padded)
        state = state + step_size * (convolve(padded, kernels[block_idx]) + offsets[block_idx][None, :, None, None])
    cotan = adjoint
    grads = [None] * L_DEV
    for block_idx in reversed(range(L_DEV)):
        cot_bf = cotan.astype(jnp.bfloat16)
        grads[block_idx] = kernel_grad(cot_bf, paddeds[block_idx])
        back = convolve_back(pad_field(cot_bf), kernels[block_idx])
        slope = jnp.tanh(states[block_idx])
        cotan = cotan + step_size * (1.0 - slope * slope) * back
    return (state, cotan, jnp.stack(grads))

def reference(c_guess, adjoint_guess, weights, biases, coarse_gain):
    groups = c_guess.shape[0]
    kernels = weights.reshape(groups, L_DEV, 9, FEATURE_MAPS, FEATURE_MAPS)
    offsets = biases.reshape(groups, L_DEV, FEATURE_MAPS)
    phi, psi, grads = lax.map(relax, (c_guess, adjoint_guess, kernels, offsets))
    gains = coarse_gain[:, None, :, None, None]
    forward_rest = phi - gains * c_guess
    backward_rest = psi - gains * adjoint_guess
    states = [c_guess[0]]
    for group_idx in range(1, groups):
        states.append(gains[group_idx - 1] * states[-1] + forward_rest[group_idx - 1])
    ends = [None] * groups
    ends[groups - 1] = adjoint_guess[groups - 1]
    for group_idx in range(groups - 1, 0, -1):
        ends[group_idx - 1] = gains[group_idx] * ends[group_idx] + backward_rest[group_idx]
    weight_grad = grads.reshape(groups * L_DEV, 9, FEATURE_MAPS, FEATURE_MAPS)
    return (jnp.stack(states), jnp.stack(ends), weight_grad)
```

```python
import jax
import jax.numpy as jnp
from jax import lax
from jax.experimental import pallas as pl
from jax.experimental.pallas import tpu as pltpu
from jax.sharding import PartitionSpec as P

HALO = 32
OWN = 64
BF = jnp.bfloat16
F32 = jnp.float32


def relax_kernel(x_ref, a_ref, w_ref, wt_ref, b_ref, phi_ref, psi_ref, g_ref, z_s, sl_s):
    blocks = w_ref.shape[0]
    strip = 2 * lax.axis_index("col") + lax.axis_index("row")
    strips = 2 * lax.axis_size("col")
    lane = lax.broadcasted_iota(jnp.int32, (64, 128), 1)
    column = strip * OWN - HALO + lane
    inside = jnp.where((column >= 0) & (column < strips * OWN), 1.0, 0.0).astype(F32)
    own = jnp.where((lane >= HALO) & (lane < HALO + OWN), 1.0, 0.0).astype(F32)
    phi_ref[...] = x_ref[...]
    psi_ref[...] = a_ref[...] * inside[None]
    zero = jnp.zeros((64, 128), BF)

    def forward(l, carry):
        w = w_ref[l]
        bias = b_ref[l]
        z_s[l, 0] = zero
        z_s[l, 17] = zero
        later, last = None, None
        for m in range(8):
            pieces = []
            for h in (2 * m, 2 * m + 1):
                t = jnp.tanh(phi_ref[h]) * inside
                sl_s[l, h] = inside - t * t
                z_s[l, h + 1] = (t * own).astype(BF)
                pieces.append(
                    jnp.concatenate(
                        [
                            pltpu.roll(t, 1, 1).astype(BF),
                            t.astype(BF),
                            pltpu.roll(t, 127, 1).astype(BF),
                        ],
                        axis=0,
                    )
                )
            rhs = jnp.concatenate(pieces, axis=1)
            prod = jnp.dot(w, rhs, preferred_element_type=F32)
            p0, p1 = prod[:, :128], prod[:, 128:]
            if m > 0:
                phi_ref[2 * m - 1] = phi_ref[2 * m - 1] + bias + (later + p0[128:])
                first = last + p0[64:128] + p1[128:]
            else:
                first = p0[64:128] + p1[128:]
            phi_ref[2 * m] = phi_ref[2 * m] + bias + first
            later = p0[:64] + p1[64:128]
            last = p1[:64]
        phi_ref[15] = phi_ref[15] + bias + later
        return carry

    lax.fori_loop(0, blocks, forward, 0)

    def backward(step, carry):
        l = blocks - 1 - step
        wt = wt_ref[l]
        grad = jnp.zeros((192, 192), F32)
        later, last = None, None
        for m in range(8):
            pieces = []
            zs = []
            for h in (2 * m, 2 * m + 1):
                a = psi_ref[h]
                pieces.append(
                    jnp.concatenate(
                        [
                            pltpu.roll(a, 127, 1).astype(BF),
                            a.astype(BF),
                            pltpu.roll(a, 1, 1).astype(BF),
                        ],
                        axis=0,
                    )
                )
                zs.append(jnp.concatenate([z_s[l, h], z_s[l, h + 1], z_s[l, h + 2]], axis=0))
            rhs = jnp.concatenate(pieces, axis=1)
            zz = jnp.concatenate(zs, axis=1)
            prod = jnp.dot(wt, rhs, preferred_element_type=F32)
            grad = grad + lax.dot_general(
                rhs, zz, (((1,), (1,)), ((), ())), preferred_element_type=F32
            )
            p0, p1 = prod[:, :128], prod[:, 128:]
            if m > 0:
                psi_ref[2 * m - 1] = psi_ref[2 * m - 1] + sl_s[l, 2 * m - 1] * (later + p0[:64])
                first = last + p0[64:128] + p1[:64]
            else:
                first = p0[64:128] + p1[:64]
            psi_ref[2 * m] = psi_ref[2 * m] + sl_s[l, 2 * m] * first
            later = p0[128:] + p1[64:128]
            last = p1[128:]
        psi_ref[15] = psi_ref[15] + sl_s[l, 15] * later
        g_ref[l] = 0.5 * grad
        return carry

    lax.fori_loop(0, blocks, backward, 0)


def relax(x, a, w, wt, b):
    blocks = w.shape[0]
    return pl.pallas_call(
        relax_kernel,
        out_shape=(
            jax.ShapeDtypeStruct((16, 64, 128), F32),
            jax.ShapeDtypeStruct((16, 64, 128), F32),
            jax.ShapeDtypeStruct((blocks, 192, 192), F32),
        ),
        in_specs=[pl.BlockSpec(memory_space=pltpu.VMEM)] * 5,
        out_specs=[pl.BlockSpec(memory_space=pltpu.VMEM)] * 3,
        scratch_shapes=[
            pltpu.VMEM((blocks, 18, 64, 128), BF),
            pltpu.VMEM((blocks, 16, 64, 128), F32),
        ],
        compiler_params=pltpu.CompilerParams(vmem_limit_bytes=48 << 20),
    )(x, a, w, wt, b)


def local(c_guess, adjoint_guess, weights, biases, coarse_gain):
    blocks = weights.shape[0]
    row = lax.axis_index("row")
    cols = lax.axis_size("col")
    both = jnp.stack([c_guess[0, 0], adjoint_guess[0, 0]])
    both = both.transpose(0, 2, 1, 3)
    full = lax.all_gather(both, "row", axis=1, tiled=True)
    perm = [(c, (c + 1) % cols) for c in range(cols)]
    perm += [(cols + c, cols + (c - 1) % cols) for c in range(cols)]
    low = row == 0
    edge = jnp.where(low, full[..., 128 - HALO :], full[..., :HALO])
    side = lax.ppermute(edge, ("row", "col"), perm)
    strip = jnp.where(
        low,
        jnp.concatenate([side, full[..., : 128 - HALO]], axis=-1),
        jnp.concatenate([full[..., HALO:], side], axis=-1),
    )
    taps = weights.reshape(blocks, 3, 3, 64, 64) * jnp.asarray(0.5, BF)
    w = taps.transpose(0, 1, 3, 2, 4).reshape(blocks, 192, 192)
    wt = taps.transpose(0, 1, 4, 2, 3).reshape(blocks, 192, 192)
    b = jnp.broadcast_to(0.5 * biases[:, :, None], (blocks, 64, 128))
    phi, psi, grad = relax(strip[0], strip[1], w, wt, b)
    grad = grad.reshape(blocks, 3, 64, 3, 64).transpose(0, 3, 1, 2, 4).reshape(blocks, 9, 64, 64)
    weight_grad = lax.psum(grad, ("row", "col"))

    index = lax.axis_index("layer")
    count = lax.axis_size("layer")
    gain = coarse_gain[0][None, :, None]
    core = slice(HALO, HALO + OWN)
    r = phi[..., core] - jnp.where(index == 0, 0.0, gain) * strip[0][..., core]
    s = psi[..., core] - jnp.where(index == count - 1, 0.0, gain) * strip[1][..., core]
    rs = jnp.concatenate([r, s], axis=-1)
    rs = lax.all_to_all(rs, "layer", 0, 0, tiled=True)
    gains = lax.all_gather(coarse_gain[0], "layer")[:, :, None]
    fwd = [jnp.zeros_like(rs[0, :, :OWN])]
    for d in range(count - 1):
        fwd.append(gains[d] * fwd[-1] + rs[d, :, :OWN])
    bwd = [jnp.zeros_like(rs[0, :, OWN:])]
    for d in range(count - 1, 0, -1):
        bwd.append(gains[d] * bwd[-1] + rs[d, :, OWN:])
    out = jnp.concatenate([jnp.stack(fwd), jnp.stack(bwd[::-1])], axis=-1)
    out = lax.all_to_all(out, "layer", 0, 0, tiled=True)
    out = out.reshape(16, 64, 2, OWN)
    out = lax.all_to_all(out, "row", 0, 3, tiled=True)
    c_states = out[:, :, 0].transpose(1, 0, 2)
    ends = out[:, :, 1].transpose(1, 0, 2)
    c_states = jnp.where(index == 0, c_guess[0, 0], c_states)
    ends = jnp.where(index == count - 1, adjoint_guess[0, 0], ends)
    return (c_states[None, None], ends[None, None], weight_grad)


def solution(mesh):
    in_specs = (
        P("layer", None, None, "row", "col"),
        P("layer", None, None, "row", "col"),
        P("layer", None, None, None),
        P("layer", None),
        P("layer", None),
    )
    out_specs = (
        P("layer", None, None, "row", "col"),
        P("layer", None, None, "row", "col"),
        P("layer", None, None, None),
    )
    return jax.shard_map(local, mesh=mesh, in_specs=in_specs, out_specs=out_specs, check_vma=False)
```

```python
import jax
import jax.numpy as jnp
from jax import lax
from jax.experimental import pallas as pl
from jax.experimental.pallas import tpu as pltpu
from jax.sharding import PartitionSpec as P

HALO = 32
OWN = 64
BF = jnp.bfloat16
F32 = jnp.float32
MESH = pl.DeviceIdType.MESH


def remote(src, dst, send, recv, where):
    return pltpu.make_async_remote_copy(
        src_ref=src,
        dst_ref=dst,
        send_sem=send,
        recv_sem=recv,
        device_id=where,
        device_id_type=MESH,
    )


def fused_kernel(
    c_ref,
    a_ref,
    w_in,
    b_ref,
    gain_ref,
    pieces_out,
    grad_out,
    snd,
    rcv,
    edge_snd,
    edge_rcv,
    tmp,
    gain_snd,
    gain_rcv,
    gain_pk,
    gain_own,
    w_ref,
    wt_ref,
    b_s,
    phi_ref,
    psi_ref,
    z_s,
    sl_s,
    p1_snd,
    p1_rcv,
    p2_snd,
    p2_rcv,
    g_part,
    g_sib,
    g_half,
    g_chip,
    g_full,
    in_send,
    in_recv,
    gain_send,
    gain_recv,
    p1_send,
    p1_recv,
    p2_send,
    p2_recv,
    ga_send,
    ga_recv,
    gb_send,
    gb_recv,
    gc_send,
    gc_recv,
    gd_send,
    gd_recv,
):
    blocks = w_in.shape[0]
    layer = lax.axis_index("layer")
    row = lax.axis_index("row")
    col = lax.axis_index("col")
    layers = lax.axis_size("layer")
    cols = lax.axis_size("col")
    core = lax.rem(col, 2)
    chip = 2 * row + col // 2
    strip = 2 * col + row
    lane = lax.broadcasted_iota(jnp.int32, (64, 128), 1)
    lane32 = lax.broadcasted_iota(jnp.int32, (32, 128), 1)
    lane16 = lax.broadcasted_iota(jnp.int32, (16, 128), 1)
    column = strip * OWN - HALO + lane
    inside = jnp.where((column >= 0) & (column < 2 * cols * OWN), 1.0, 0.0).astype(F32)
    own = jnp.where((lane >= HALO) & (lane < HALO + OWN), 1.0, 0.0).astype(F32)
    top = row == 0

    barrier = pltpu.get_barrier_semaphore()

    def greet(n, carry):
        e, rho = n // 2, lax.rem(n, 2)

        @pl.when(jnp.logical_or(e != layer, rho != row))
        def _():
            pl.semaphore_signal(
                barrier, inc=1, device_id={"layer": e, "row": rho}, device_id_type=MESH
            )

        return carry

    lax.fori_loop(0, 2 * layers, greet, 0)
    for step in range(1, cols):
        for rho in range(2):
            pl.semaphore_signal(
                barrier,
                inc=1,
                device_id={"row": rho, "col": lax.rem(col + step, cols)},
                device_id_type=MESH,
            )

    def pack(src, n):
        def one(h, carry):
            x = src[pl.ds(h, 64, stride=8), :]
            snd[n, h] = x.astype(BF)
            for side in range(2):
                edge = jnp.zeros((16, 128), F32)
                for g in range(4):
                    part = x[16 * g : 16 * g + 16]
                    shift = (32 * g + (32 if side == 0 else 0)) % 128
                    if shift:
                        part = pltpu.roll(part, shift, 1)
                    edge = jnp.where(lane16 // 32 == g, part, edge)
                edge_snd[side, n, h] = edge.astype(BF)
            return carry

        lax.fori_loop(0, 8, one, 0)

    def exchange(n):
        yield remote(snd.at[n], rcv.at[n], in_send.at[n, 0], in_recv.at[n, 0], {"row": 1 - row})
        yield remote(
            edge_snd.at[0, n],
            edge_rcv.at[row, n],
            in_send.at[n, 1],
            in_recv.at[n, 1 + row],
            {"row": 0, "col": lax.rem(col + 1, cols)},
        )
        yield remote(
            edge_snd.at[1, n],
            edge_rcv.at[row, n],
            in_send.at[n, 2],
            in_recv.at[n, 1 + row],
            {"row": 1, "col": lax.rem(col + cols - 1, cols)},
        )

    def arrived(n):
        remote(snd.at[n], rcv.at[n], in_send.at[n, 0], in_recv.at[n, 0], {"row": 1 - row}).wait_recv()
        for rho in range(2):
            remote(
                edge_snd.at[0, n],
                edge_rcv.at[rho, n],
                in_send.at[n, 1],
                in_recv.at[n, 1 + rho],
                {"row": 1 - row},
            ).wait_recv()

    pack(c_ref, 0)
    pl.semaphore_wait(barrier, 2 * layers - 1 + 2 * (cols - 1))
    for copy in exchange(0):
        copy.start()
    pack(a_ref, 1)
    for copy in exchange(1):
        copy.start()

    def lay_weights(l, carry):
        for i in range(3):
            w_ref[l, 64 * i : 64 * i + 64, :] = jnp.concatenate(
                [w_in[l, 3 * i + j] * jnp.asarray(0.5, BF) for j in range(3)], axis=1
            )
            stack = w_in[l, 3 * i : 3 * i + 3].reshape(192, 64)
            wt_ref[l, 64 * i : 64 * i + 64, :] = (0.5 * stack.astype(F32)).T.astype(BF)
        return carry

    lax.fori_loop(0, blocks, lay_weights, 0)
    tmp[...] = jnp.zeros_like(tmp)
    tmp[0:blocks, 0:64] = 0.5 * b_ref[...]
    tmp[blocks : blocks + 1, 0:64] = gain_ref[...]
    turned = tmp[...].T
    for l in range(blocks):
        b_s[l] = jnp.broadcast_to(turned[0:64, l : l + 1], (64, 128))
    gain_own[...] = jnp.broadcast_to(turned[0:64, blocks : blocks + 1], (64, 128))
    gain_snd[...] = tmp[blocks : blocks + 8, :]

    def holder(h):
        return 2 * lax.rem(h, 8) + row, h // 8

    def stays(h):
        lam, rho = holder(h)
        return jnp.logical_and(lam == layer, rho == row)

    def gain_copy(h):
        lam, rho = holder(h)
        return remote(
            gain_snd,
            gain_rcv.at[layer],
            gain_send.at[h],
            gain_recv.at[layer],
            {"layer": lam, "row": rho},
        )

    def p1_copy(n, h):
        lam, rho = holder(h)
        return remote(
            p1_snd.at[n, h],
            p1_rcv.at[n, layer],
            p1_send.at[n, h],
            p1_recv.at[n, layer],
            {"layer": lam, "row": rho},
        )

    def comes(e):
        return jnp.logical_or(e != layer, lax.rem(layer, 2) != row)

    def send_gain(h, carry):
        @pl.when(stays(h))
        def _():
            gain_rcv[layer] = gain_snd[...]

        @pl.when(jnp.logical_not(stays(h)))
        def _():
            gain_copy(h).start()

        return carry

    lax.fori_loop(0, 16, send_gain, 0)

    def assemble(src, n, dst):
        shift = jnp.where(top, 32, 96)

        def halo(rho, h):
            packed = edge_rcv[rho, n, h].astype(F32)
            return jnp.concatenate(
                [
                    pltpu.roll(packed, jnp.where(top, (128 - 32 * g) % 128, (96 - 32 * g) % 128), 1)
                    for g in range(4)
                ],
                axis=0,
            )

        start = jnp.where(top, 0, 96)
        outer = (lane >= start) & (lane < start + 32)

        def one(h, carry):
            x = src[pl.ds(h, 64, stride=8), :]
            dst[8 * row + h] = jnp.where(outer, halo(row, h), pltpu.roll(x, shift, 1)) * inside
            y = rcv[n, h].astype(F32)
            dst[8 * (1 - row) + h] = (
                jnp.where(outer, halo(1 - row, h), pltpu.roll(y, shift, 1)) * inside
            )
            return carry

        lax.fori_loop(0, 8, one, 0)

    arrived(0)
    assemble(c_ref, 0, phi_ref)

    zero = jnp.zeros((64, 128), BF)

    def forward(l, carry):
        w = w_ref[l]
        bias = b_s[l]
        z_s[l, 0] = zero
        z_s[l, 17] = zero
        later, last = None, None
        for m in range(8):
            pieces = []
            for h in (2 * m, 2 * m + 1):
                t = jnp.tanh(phi_ref[h]) * inside
                sl_s[l, h] = inside - t * t
                z_s[l, h + 1] = (t * own).astype(BF)
                pieces.append(
                    jnp.concatenate(
                        [
                            pltpu.roll(t, 1, 1).astype(BF),
                            t.astype(BF),
                            pltpu.roll(t, 127, 1).astype(BF),
                        ],
                        axis=0,
                    )
                )
            rhs = jnp.concatenate(pieces, axis=1)
            prod = jnp.dot(w, rhs, preferred_element_type=F32)
            p0, p1 = prod[:, :128], prod[:, 128:]
            if m > 0:
                phi_ref[2 * m - 1] = phi_ref[2 * m - 1] + bias + (later + p0[128:])
                first = last + p0[64:128] + p1[128:]
            else:
                first = p0[64:128] + p1[128:]
            phi_ref[2 * m] = phi_ref[2 * m] + bias + first
            later = p0[:64] + p1[64:128]
            last = p1[:64]
        phi_ref[15] = phi_ref[15] + bias + later
        return carry

    lax.fori_loop(0, blocks, forward, 0)

    def send_pieces(n, field, guess_own, keep):
        gain = gain_own[...] * keep
        shift = jnp.where(top, 32, 96)

        def one(h, carry):
            rho, u = h // 8, lax.rem(h, 8)
            mine = pltpu.roll(guess_own[pl.ds(u, 64, stride=8), :], shift, 1)
            other = pltpu.roll(rcv[n, u].astype(F32), shift, 1)
            here = jnp.where(rho == row, 1.0, 0.0)
            r = field[h] - gain * (here * mine + (1.0 - here) * other)
            packed = jnp.where(lane32 < 64, pltpu.roll(r[:32], 96, 1), pltpu.roll(r[32:], 32, 1))

            @pl.when(stays(h))
            def _():
                p1_rcv[n, layer] = packed.astype(BF)

            @pl.when(jnp.logical_not(stays(h)))
            def _():
                p1_snd[n, h] = packed.astype(BF)
                p1_copy(n, h).start()

            return carry

        lax.fori_loop(0, 16, one, 0)

    def p2_copy(n, e):
        return remote(
            p2_snd.at[n, e],
            p2_rcv.at[n, layer],
            p2_send.at[n, e],
            p2_recv.at[n, layer],
            {"layer": e},
        )

    def solve(n):
        first = 0 if n == 0 else layers - 1
        stride = 1 if n == 0 else -1

        def one(k, state):
            e = first + stride * k

            @pl.when(comes(e))
            def _():
                remote(
                    p1_snd.at[n, 0],
                    p1_rcv.at[n, e],
                    p1_send.at[n, 0],
                    p1_recv.at[n, e],
                    {"layer": layer, "row": 1 - row},
                ).wait_recv()

            state = gain_pk[e] * state + p1_rcv[n, e].astype(F32)
            target = e + stride

            @pl.when(target == layer)
            def _():
                p2_rcv[n, layer] = state.astype(BF)

            @pl.when(target != layer)
            def _():
                p2_snd[n, target] = state.astype(BF)
                p2_copy(n, target).start()

            return state

        lax.fori_loop(0, layers - 1, one, jnp.zeros((32, 128), F32))
        unused = layers - 1 if n == 0 else 0

        @pl.when(comes(unused))
        def _():
            remote(
                p1_snd.at[n, 0],
                p1_rcv.at[n, unused],
                p1_send.at[n, 0],
                p1_recv.at[n, unused],
                {"layer": layer, "row": 1 - row},
            ).wait_recv()

    send_pieces(0, phi_ref, c_ref, jnp.where(layer == 0, 0.0, 1.0))

    def take_gain(e, carry):
        @pl.when(comes(e))
        def _():
            remote(
                gain_snd,
                gain_rcv.at[e],
                gain_send.at[0],
                gain_recv.at[e],
                {"layer": layer, "row": 1 - row},
            ).wait_recv()

        return carry

    lax.fori_loop(0, layers, take_gain, 0)
    for e in range(16):
        tmp[e : e + 1, :] = gain_rcv[e, 0:1, :]
    turned_all = tmp[...].T
    for e in range(16):
        gain_pk[e] = jnp.where(
            lane32 < 64,
            jnp.broadcast_to(turned_all[0:32, e : e + 1], (32, 128)),
            jnp.broadcast_to(turned_all[32:64, e : e + 1], (32, 128)),
        )

    half = pl.ds(pl.multiple_of(144 * core, 16), 144)
    other_half = pl.ds(pl.multiple_of(144 * (1 - core), 16), 144)
    beside = {"col": col + 1 - 2 * core}

    def ga_copy(l):
        return remote(g_part.at[l, other_half], g_sib.at[l], ga_send.at[l], ga_recv.at[l], beside)

    def at_chip(y):
        return {"row": y // 2, "col": 2 * lax.rem(y, 2) + core}

    def gb_copy(l):
        y = lax.rem(l, 4)
        return remote(
            g_half.at[l],
            g_chip.at[l // 4, chip],
            gb_send.at[l],
            gb_recv.at[l // 4, chip],
            at_chip(y),
        )

    def gc_copy(l, step):
        y = lax.rem(chip + step, 4)
        return remote(
            g_full.at[l, half],
            g_full.at[l, half],
            gc_send.at[l // 4, step - 1],
            gc_recv.at[l],
            at_chip(y),
        )

    def gd_copy(l):
        return remote(g_full.at[l, half], g_full.at[l, half], gd_send.at[l], gd_recv.at[l], beside)

    def to_owner(l):
        ga_copy(l).wait_recv()
        total = (g_part[l, half, :] + g_sib[l]).astype(BF)

        @pl.when(lax.rem(l, 4) == chip)
        def _():
            g_chip[l // 4, chip] = total

        @pl.when(lax.rem(l, 4) != chip)
        def _():
            g_half[l] = total
            gb_copy(l).start()

    def own_block(q):
        l = 4 * q + chip
        for step in range(1, 4):
            y = lax.rem(chip + step, 4)
            remote(
                g_half.at[l],
                g_chip.at[q, y],
                gb_send.at[l],
                gb_recv.at[q, y],
                at_chip(y),
            ).wait_recv()
        total = g_chip[q, 0].astype(F32) + g_chip[q, 1].astype(F32)
        total = total + g_chip[q, 2].astype(F32) + g_chip[q, 3].astype(F32)
        g_full[l, half, :] = total.astype(BF)
        for step in range(1, 4):
            gc_copy(l, step).start()

    arrived(1)
    assemble(a_ref, 1, psi_ref)

    def backward(step, carry):
        l = blocks - 1 - step
        wt = wt_ref[l]
        grad = jnp.zeros((192, 192), F32)
        later, last = None, None
        for m in range(8):
            pieces = []
            zs = []
            for h in (2 * m, 2 * m + 1):
                a = psi_ref[h]
                pieces.append(
                    jnp.concatenate(
                        [
                            pltpu.roll(a, 127, 1).astype(BF),
                            a.astype(BF),
                            pltpu.roll(a, 1, 1).astype(BF),
                        ],
                        axis=0,
                    )
                )
                zs.append(jnp.concatenate([z_s[l, h], z_s[l, h + 1], z_s[l, h + 2]], axis=0))
            rhs = jnp.concatenate(pieces, axis=1)
            zz = jnp.concatenate(zs, axis=1)
            prod = jnp.dot(wt, rhs, preferred_element_type=F32)
            grad = grad + lax.dot_general(
                rhs, zz, (((1,), (1,)), ((), ())), preferred_element_type=F32
            )
            p0, p1 = prod[:, :128], prod[:, 128:]
            if m > 0:
                psi_ref[2 * m - 1] = psi_ref[2 * m - 1] + sl_s[l, 2 * m - 1] * (later + p0[:64])
                first = last + p0[64:128] + p1[:64]
            else:
                first = p0[64:128] + p1[:64]
            psi_ref[2 * m] = psi_ref[2 * m] + sl_s[l, 2 * m] * first
            later = p0[128:] + p1[64:128]
            last = p1[128:]
        psi_ref[15] = psi_ref[15] + sl_s[l, 15] * later
        grad = 0.5 * grad
        g_part[l, 0:192, :] = grad[:, :128]
        g_part[l, 192:288, 0:64] = grad[:96, 128:192]
        g_part[l, 192:288, 64:128] = grad[96:, 128:192]
        ga_copy(l).start()

        @pl.when(step >= 2)
        def _():
            to_owner(l + 2)

        @pl.when(step == 5)
        def _():
            solve(0)

        return carry

    lax.fori_loop(0, blocks, backward, 0)

    send_pieces(1, psi_ref, a_ref, jnp.where(layer == layers - 1, 0.0, 1.0))
    own_block(1)
    to_owner(1)
    to_owner(0)
    solve(1)
    own_block(0)

    def forward_half(k, carry):
        l = blocks - 1 - k

        @pl.when(lax.rem(l, 4) != chip)
        def _():
            remote(
                g_full.at[l, half],
                g_full.at[l, half],
                gc_send.at[0, 0],
                gc_recv.at[l],
                at_chip(lax.rem(l, 4)),
            ).wait_recv()

        gd_copy(l).start()
        return carry

    lax.fori_loop(0, blocks, forward_half, 0)

    for n in range(2):
        for copy in exchange(n):
            copy.wait_send()

    def drain(h, carry):
        @pl.when(jnp.logical_not(stays(h)))
        def _():
            gain_copy(h).wait_send()
            for n in range(2):
                p1_copy(n, h).wait_send()

        for n in range(2):
            skipped = 0 if n == 0 else layers - 1

            @pl.when(jnp.logical_and(h != layer, h != skipped))
            def _():
                p2_copy(n, h).wait_send()

            @pl.when(jnp.logical_and(h != layer, layer != skipped))
            def _():
                remote(
                    p2_snd.at[n, 0],
                    p2_rcv.at[n, h],
                    p2_send.at[n, 0],
                    p2_recv.at[n, h],
                    {"row": 1 - row},
                ).wait_recv()

        return carry

    lax.fori_loop(0, 16, drain, 0)

    def drain_grads(l, carry):
        ga_copy(l).wait_send()

        @pl.when(lax.rem(l, 4) != chip)
        def _():
            gb_copy(l).wait_send()

        gd_copy(l).wait_send()
        remote(
            g_full.at[l, other_half],
            g_full.at[l, other_half],
            gd_send.at[l],
            gd_recv.at[l],
            beside,
        ).wait_recv()
        return carry

    lax.fori_loop(0, blocks, drain_grads, 0)
    for q in range(2):
        for step in range(1, 4):
            gc_copy(4 * q + chip, step).wait_send()
    for n in range(2):

        @pl.when(layer != (0 if n == 0 else layers - 1))
        def _():
            pieces_out[n] = p2_rcv[n]

    grad_out[...] = g_full[...]


def fused(c, a, w, b, gain):
    blocks = w.shape[0]
    vm = pltpu.VMEM
    dma = pltpu.SemaphoreType.DMA
    return pl.pallas_call(
        fused_kernel,
        out_shape=(
            jax.ShapeDtypeStruct((2, 16, 32, 128), BF),
            jax.ShapeDtypeStruct((blocks, 288, 128), BF),
        ),
        in_specs=[pl.BlockSpec(memory_space=vm)] * 5,
        out_specs=[pl.BlockSpec(memory_space=vm)] * 2,
        scratch_shapes=[
            vm((2, 8, 64, 128), BF),
            vm((2, 8, 64, 128), BF),
            vm((2, 2, 8, 16, 128), BF),
            vm((2, 2, 8, 16, 128), BF),
            vm((128, 128), F32),
            vm((8, 128), F32),
            vm((16, 8, 128), F32),
            vm((16, 32, 128), F32),
            vm((64, 128), F32),
            vm((blocks, 192, 192), BF),
            vm((blocks, 192, 192), BF),
            vm((blocks, 64, 128), F32),
            vm((16, 64, 128), F32),
            vm((16, 64, 128), F32),
            vm((blocks, 18, 64, 128), BF),
            vm((blocks, 16, 64, 128), F32),
            vm((2, 16, 32, 128), BF),
            vm((2, 16, 32, 128), BF),
            vm((2, 16, 32, 128), BF),
            vm((2, 16, 32, 128), BF),
            vm((blocks, 288, 128), F32),
            vm((blocks, 144, 128), F32),
            vm((blocks, 144, 128), BF),
            vm((2, 4, 144, 128), BF),
            vm((blocks, 288, 128), BF),
            dma((2, 3)),
            dma((2, 3)),
            dma((16,)),
            dma((16,)),
            dma((2, 16)),
            dma((2, 16)),
            dma((2, 16)),
            dma((2, 16)),
            dma((blocks,)),
            dma((blocks,)),
            dma((blocks,)),
            dma((2, 4)),
            dma((2, 3)),
            dma((blocks,)),
            dma((blocks,)),
            dma((blocks,)),
        ],
        compiler_params=pltpu.CompilerParams(
            vmem_limit_bytes=48 << 20, collective_id=0, has_side_effects=True
        ),
    )(c, a, w, b, gain)


def unpack_kernel(c_ref, a_ref, pieces_ref, grad_ref, c_out, a_out, g_out):
    layer = lax.axis_index("layer")
    layers = lax.axis_size("layer")
    lane32 = lax.broadcasted_iota(jnp.int32, (32, 128), 1)

    @pl.when(pl.program_id(0) == 0)
    def _():
        for n, src, dst, skipped in ((0, c_ref, c_out, 0), (1, a_ref, a_out, layers - 1)):

            @pl.when(layer == skipped)
            def _():
                dst[...] = src[...]

            @pl.when(layer != skipped)
            def _():
                for u in range(8):
                    left = pieces_ref[n, 2 * u].astype(F32)
                    right = pieces_ref[n, 2 * u + 1].astype(F32)
                    dst[pl.ds(u, 32, stride=8), :] = jnp.where(
                        lane32 < 64, left, pltpu.roll(right, 64, 1)
                    )
                    dst[pl.ds(256 + u, 32, stride=8), :] = jnp.where(
                        lane32 < 64, pltpu.roll(left, 64, 1), right
                    )

    for j in range(3):
        g_out[0, j] = grad_ref[0, 64 * j : 64 * j + 64, 0:64].astype(F32)
        g_out[0, 3 + j] = grad_ref[0, 64 * j : 64 * j + 64, 64:128].astype(F32)
    g_out[0, 6] = grad_ref[0, 192:256, 0:64].astype(F32)
    g_out[0, 7, 0:32] = grad_ref[0, 256:288, 0:64].astype(F32)
    g_out[0, 7, 32:64] = grad_ref[0, 192:224, 64:128].astype(F32)
    g_out[0, 8] = grad_ref[0, 224:288, 64:128].astype(F32)


def unpack(c, a, pieces, grad):
    blocks = grad.shape[0]
    whole = pl.BlockSpec((512, 128), lambda l: (0, 0))
    return pl.pallas_call(
        unpack_kernel,
        grid=(blocks,),
        out_shape=(
            jax.ShapeDtypeStruct((512, 128), F32),
            jax.ShapeDtypeStruct((512, 128), F32),
            jax.ShapeDtypeStruct((blocks, 9, 64, 64), F32),
        ),
        in_specs=[
            whole,
            whole,
            pl.BlockSpec((2, 16, 32, 128), lambda l: (0, 0, 0, 0)),
            pl.BlockSpec((1, 288, 128), lambda l: (l, 0, 0)),
        ],
        out_specs=[whole, whole, pl.BlockSpec((1, 9, 64, 64), lambda l: (l, 0, 0, 0))],
        compiler_params=pltpu.CompilerParams(vmem_limit_bytes=32 << 20),
    )(c, a, pieces, grad)


def local(c_guess, adjoint_guess, weights, biases, coarse_gain):
    c = c_guess.reshape(512, 128)
    a = adjoint_guess.reshape(512, 128)
    pieces, grad = fused(c, a, weights, biases, coarse_gain)
    c_states, ends, weight_grad = unpack(c, a, pieces, grad)
    return (c_states.reshape(c_guess.shape), ends.reshape(c_guess.shape), weight_grad)


def solution(mesh):
    in_specs = (
        P("layer", None, None, "row", "col"),
        P("layer", None, None, "row", "col"),
        P("layer", None, None, None),
        P("layer", None),
        P("layer", None),
    )
    out_specs = (
        P("layer", None, None, "row", "col"),
        P("layer", None, None, "row", "col"),
        P("layer", None, None, None),
    )
    return jax.shard_map(local, mesh=mesh, in_specs=in_specs, out_specs=out_specs, check_vma=False)
```

```python
import jax
import jax.numpy as jnp
from jax import lax
from jax.experimental import pallas as pl
from jax.experimental.pallas import tpu as pltpu
from jax.sharding import PartitionSpec as P

HALO = 32
OWN = 64
BF = jnp.bfloat16
F32 = jnp.float32
MESH = pl.DeviceIdType.MESH


def remote(src, dst, send, recv, where):
    return pltpu.make_async_remote_copy(
        src_ref=src,
        dst_ref=dst,
        send_sem=send,
        recv_sem=recv,
        device_id=where,
        device_id_type=MESH,
    )


def fused_kernel(
    c_hbm,
    a_hbm,
    w_hbm,
    b_hbm,
    gain_hbm,
    pieces_out,
    grad_out,
    snd,
    rcv,
    edge_snd,
    edge_rcv,
    tmp,
    gain_snd,
    gain_rcv,
    gain_pk,
    gain_own,
    w_ref,
    wt_ref,
    b_s,
    phi_ref,
    psi_ref,
    z_s,
    sl_s,
    p1_snd,
    p1_rcv,
    p2_snd,
    p2_rcv,
    g_part,
    g_sib,
    g_half,
    g_chip,
    g_full,
    in_send,
    in_recv,
    gain_send,
    gain_recv,
    p1_send,
    p1_recv,
    p2_send,
    p2_recv,
    ga_send,
    ga_recv,
    gb_send,
    gb_recv,
    gc_send,
    gc_recv,
    gd_send,
    gd_recv,
    c_ref,
    a_ref,
    w_in,
    b_ref,
    gain_ref,
    load_sem,
):
    blocks = w_in.shape[0]
    layer = lax.axis_index("layer")
    row = lax.axis_index("row")
    col = lax.axis_index("col")
    layers = lax.axis_size("layer")
    cols = lax.axis_size("col")
    core = lax.rem(col, 2)
    chip = 2 * row + col // 2
    strip = 2 * col + row
    lane = lax.broadcasted_iota(jnp.int32, (64, 128), 1)
    lane32 = lax.broadcasted_iota(jnp.int32, (32, 128), 1)
    lane16 = lax.broadcasted_iota(jnp.int32, (16, 128), 1)
    column = strip * OWN - HALO + lane
    inside = jnp.where((column >= 0) & (column < 2 * cols * OWN), 1.0, 0.0).astype(F32)
    own = jnp.where((lane >= HALO) & (lane < HALO + OWN), 1.0, 0.0).astype(F32)
    top = row == 0

    loads = [
        pltpu.make_async_copy(src, dst, load_sem.at[n])
        for n, (src, dst) in enumerate(
            (
                (c_hbm, c_ref),
                (a_hbm, a_ref),
                (w_hbm, w_in),
                (b_hbm, b_ref),
                (gain_hbm, gain_ref),
            )
        )
    ]
    for load in loads:
        load.start()

    barrier = pltpu.get_barrier_semaphore()

    def greet(n, carry):
        e, rho = n // 2, lax.rem(n, 2)

        @pl.when(jnp.logical_or(e != layer, rho != row))
        def _():
            pl.semaphore_signal(
                barrier, inc=1, device_id={"layer": e, "row": rho}, device_id_type=MESH
            )

        return carry

    lax.fori_loop(0, 2 * layers, greet, 0)
    for step in range(1, cols):
        for rho in range(2):
            pl.semaphore_signal(
                barrier,
                inc=1,
                device_id={"row": rho, "col": lax.rem(col + step, cols)},
                device_id_type=MESH,
            )

    def pack(src, n):
        def one(h, carry):
            x = src[pl.ds(h, 64, stride=8), :]
            snd[n, h] = x.astype(BF)
            for side in range(2):
                edge = jnp.zeros((16, 128), F32)
                for g in range(4):
                    part = x[16 * g : 16 * g + 16]
                    shift = (32 * g + (32 if side == 0 else 0)) % 128
                    if shift:
                        part = pltpu.roll(part, shift, 1)
                    edge = jnp.where(lane16 // 32 == g, part, edge)
                edge_snd[side, n, h] = edge.astype(BF)
            return carry

        lax.fori_loop(0, 8, one, 0)

    def exchange(n):
        yield remote(snd.at[n], rcv.at[n], in_send.at[n, 0], in_recv.at[n, 0], {"row": 1 - row})
        yield remote(
            edge_snd.at[0, n],
            edge_rcv.at[row, n],
            in_send.at[n, 1],
            in_recv.at[n, 1 + row],
            {"row": 0, "col": lax.rem(col + 1, cols)},
        )
        yield remote(
            edge_snd.at[1, n],
            edge_rcv.at[row, n],
            in_send.at[n, 2],
            in_recv.at[n, 1 + row],
            {"row": 1, "col": lax.rem(col + cols - 1, cols)},
        )

    def arrived(n):
        remote(snd.at[n], rcv.at[n], in_send.at[n, 0], in_recv.at[n, 0], {"row": 1 - row}).wait_recv()
        for rho in range(2):
            remote(
                edge_snd.at[0, n],
                edge_rcv.at[rho, n],
                in_send.at[n, 1],
                in_recv.at[n, 1 + rho],
                {"row": 1 - row},
            ).wait_recv()

    loads[0].wait()
    pack(c_ref, 0)
    pl.semaphore_wait(barrier, 2 * layers - 1 + 2 * (cols - 1))
    for copy in exchange(0):
        copy.start()
    loads[1].wait()
    pack(a_ref, 1)
    for copy in exchange(1):
        copy.start()

    def lay_weights(l, carry):
        for i in range(3):
            w_ref[l, 64 * i : 64 * i + 64, :] = jnp.concatenate(
                [w_in[l, 3 * i + j] * jnp.asarray(0.5, BF) for j in range(3)], axis=1
            )
            stack = w_in[l, 3 * i : 3 * i + 3].reshape(192, 64)
            wt_ref[l, 64 * i : 64 * i + 64, :] = (0.5 * stack.astype(F32)).T.astype(BF)
        return carry

    for load in loads[2:]:
        load.wait()
    lax.fori_loop(0, blocks, lay_weights, 0)
    tmp[...] = jnp.zeros_like(tmp)
    tmp[0:blocks, 0:64] = 0.5 * b_ref[...]
    tmp[blocks : blocks + 1, 0:64] = gain_ref[...]
    turned = tmp[...].T
    for l in range(blocks):
        b_s[l] = jnp.broadcast_to(turned[0:64, l : l + 1], (64, 128))
    gain_own[...] = jnp.broadcast_to(turned[0:64, blocks : blocks + 1], (64, 128))
    gain_snd[...] = tmp[blocks : blocks + 8, :]

    def holder(h):
        return 2 * lax.rem(h, 8) + row, h // 8

    def turn(k):
        return 8 * lax.rem(layer + k // 8, 2) + lax.rem(layer // 2 + k, 8)

    def stays(h):
        lam, rho = holder(h)
        return jnp.logical_and(lam == layer, rho == row)

    def gain_copy(h):
        lam, rho = holder(h)
        return remote(
            gain_snd,
            gain_rcv.at[layer],
            gain_send.at[h],
            gain_recv.at[layer],
            {"layer": lam, "row": rho},
        )

    def p1_copy(n, h):
        lam, rho = holder(h)
        return remote(
            p1_snd.at[n, h],
            p1_rcv.at[n, layer],
            p1_send.at[n, h],
            p1_recv.at[n, layer],
            {"layer": lam, "row": rho},
        )

    def comes(e):
        return jnp.logical_or(e != layer, lax.rem(layer, 2) != row)

    def send_gain(k, carry):
        h = turn(k)

        @pl.when(stays(h))
        def _():
            gain_rcv[layer] = gain_snd[...]

        @pl.when(jnp.logical_not(stays(h)))
        def _():
            gain_copy(h).start()

        return carry

    lax.fori_loop(0, 16, send_gain, 0)

    def assemble(src, n, dst):
        shift = jnp.where(top, 32, 96)

        def halo(rho, h):
            packed = edge_rcv[rho, n, h].astype(F32)
            return jnp.concatenate(
                [
                    pltpu.roll(packed, jnp.where(top, (128 - 32 * g) % 128, (96 - 32 * g) % 128), 1)
                    for g in range(4)
                ],
                axis=0,
            )

        start = jnp.where(top, 0, 96)
        outer = (lane >= start) & (lane < start + 32)

        def one(h, carry):
            x = src[pl.ds(h, 64, stride=8), :]
            dst[8 * row + h] = jnp.where(outer, halo(row, h), pltpu.roll(x, shift, 1)) * inside
            y = rcv[n, h].astype(F32)
            dst[8 * (1 - row) + h] = (
                jnp.where(outer, halo(1 - row, h), pltpu.roll(y, shift, 1)) * inside
            )
            return carry

        lax.fori_loop(0, 8, one, 0)

    arrived(0)
    assemble(c_ref, 0, phi_ref)

    zero = jnp.zeros((64, 128), BF)

    def forward(l, carry):
        w = w_ref[l]
        bias = b_s[l]
        z_s[l, 0] = zero
        z_s[l, 17] = zero
        later, last = None, None
        for m in range(8):
            pieces = []
            for h in (2 * m, 2 * m + 1):
                t = jnp.tanh(phi_ref[h]) * inside
                sl_s[l, h] = inside - t * t
                z_s[l, h + 1] = (t * own).astype(BF)
                pieces.append(
                    jnp.concatenate(
                        [
                            pltpu.roll(t, 1, 1).astype(BF),
                            t.astype(BF),
                            pltpu.roll(t, 127, 1).astype(BF),
                        ],
                        axis=0,
                    )
                )
            rhs = jnp.concatenate(pieces, axis=1)
            prod = jnp.dot(w, rhs, preferred_element_type=F32)
            p0, p1 = prod[:, :128], prod[:, 128:]
            if m > 0:
                phi_ref[2 * m - 1] = phi_ref[2 * m - 1] + bias + (later + p0[128:])
                first = last + p0[64:128] + p1[128:]
            else:
                first = p0[64:128] + p1[128:]
            phi_ref[2 * m] = phi_ref[2 * m] + bias + first
            later = p0[:64] + p1[64:128]
            last = p1[:64]
        phi_ref[15] = phi_ref[15] + bias + later
        return carry

    lax.fori_loop(0, blocks, forward, 0)

    def send_pieces(n, field, guess_own, keep):
        gain = gain_own[...] * keep
        shift = jnp.where(top, 32, 96)

        def one(k, carry):
            h = turn(k)
            rho, u = h // 8, lax.rem(h, 8)
            mine = pltpu.roll(guess_own[pl.ds(u, 64, stride=8), :], shift, 1)
            other = pltpu.roll(rcv[n, u].astype(F32), shift, 1)
            here = jnp.where(rho == row, 1.0, 0.0)
            r = field[h] - gain * (here * mine + (1.0 - here) * other)
            packed = jnp.where(lane32 < 64, pltpu.roll(r[:32], 96, 1), pltpu.roll(r[32:], 32, 1))

            @pl.when(stays(h))
            def _():
                p1_rcv[n, layer] = packed.astype(BF)

            @pl.when(jnp.logical_not(stays(h)))
            def _():
                p1_snd[n, h] = packed.astype(BF)
                p1_copy(n, h).start()

            return carry

        lax.fori_loop(0, 16, one, 0)

    def p2_copy(n, e):
        return remote(
            p2_snd.at[n, e],
            p2_rcv.at[n, layer],
            p2_send.at[n, e],
            p2_recv.at[n, layer],
            {"layer": e},
        )

    def solve(n):
        first = 0 if n == 0 else layers - 1
        stride = 1 if n == 0 else -1

        def take(e, carry):
            @pl.when(comes(e))
            def _():
                remote(
                    p1_snd.at[n, 0],
                    p1_rcv.at[n, e],
                    p1_send.at[n, 0],
                    p1_recv.at[n, e],
                    {"layer": layer, "row": 1 - row},
                ).wait_recv()

            return carry

        lax.fori_loop(0, layers, take, 0)
        state = jnp.zeros((32, 128), F32)
        for k in range(15):
            e = first + stride * k
            state = gain_pk[e] * state + p1_rcv[n, e].astype(F32)
            p2_snd[n, e + stride] = state.astype(BF)
        skipped = 0 if n == 0 else layers - 1

        def give(k, carry):
            e = lax.rem(layer + k, layers)

            @pl.when(e != skipped)
            def _():
                p2_copy(n, e).start()

            return carry

        lax.fori_loop(1, layers, give, 0)

        @pl.when(layer != skipped)
        def _():
            p2_rcv[n, layer] = p2_snd[n, layer]

    send_pieces(0, phi_ref, c_ref, jnp.where(layer == 0, 0.0, 1.0))

    def take_gain(e, carry):
        @pl.when(comes(e))
        def _():
            remote(
                gain_snd,
                gain_rcv.at[e],
                gain_send.at[0],
                gain_recv.at[e],
                {"layer": layer, "row": 1 - row},
            ).wait_recv()

        return carry

    lax.fori_loop(0, layers, take_gain, 0)
    for e in range(16):
        tmp[e : e + 1, :] = gain_rcv[e, 0:1, :]
    turned_all = tmp[...].T
    for e in range(16):
        gain_pk[e] = jnp.where(
            lane32 < 64,
            jnp.broadcast_to(turned_all[0:32, e : e + 1], (32, 128)),
            jnp.broadcast_to(turned_all[32:64, e : e + 1], (32, 128)),
        )

    half = pl.ds(pl.multiple_of(144 * core, 16), 144)
    other_half = pl.ds(pl.multiple_of(144 * (1 - core), 16), 144)
    beside = {"col": col + 1 - 2 * core}

    def ga_copy(l):
        return remote(g_part.at[l, other_half], g_sib.at[l], ga_send.at[l], ga_recv.at[l], beside)

    def at_chip(y):
        return {"row": y // 2, "col": 2 * lax.rem(y, 2) + core}

    def gb_copy(l):
        y = lax.rem(l, 4)
        return remote(
            g_half.at[l],
            g_chip.at[l // 4, chip],
            gb_send.at[l],
            gb_recv.at[l // 4, chip],
            at_chip(y),
        )

    def gc_copy(l, step):
        y = lax.rem(chip + step, 4)
        return remote(
            g_full.at[l, half],
            g_full.at[l, half],
            gc_send.at[l // 4, step - 1],
            gc_recv.at[l],
            at_chip(y),
        )

    def gd_copy(l):
        return remote(g_full.at[l, half], g_full.at[l, half], gd_send.at[l], gd_recv.at[l], beside)

    def to_owner(l):
        ga_copy(l).wait_recv()
        total = (g_part[l, half, :] + g_sib[l]).astype(BF)

        @pl.when(lax.rem(l, 4) == chip)
        def _():
            g_chip[l // 4, chip] = total

        @pl.when(lax.rem(l, 4) != chip)
        def _():
            g_half[l] = total
            gb_copy(l).start()

    def own_block(q):
        l = 4 * q + chip
        for step in range(1, 4):
            y = lax.rem(chip + step, 4)
            remote(
                g_half.at[l],
                g_chip.at[q, y],
                gb_send.at[l],
                gb_recv.at[q, y],
                at_chip(y),
            ).wait_recv()
        total = g_chip[q, 0].astype(F32) + g_chip[q, 1].astype(F32)
        total = total + g_chip[q, 2].astype(F32) + g_chip[q, 3].astype(F32)
        g_full[l, half, :] = total.astype(BF)
        for step in range(1, 4):
            gc_copy(l, step).start()

    arrived(1)
    assemble(a_ref, 1, psi_ref)

    def backward(step, carry):
        l = blocks - 1 - step
        wt = wt_ref[l]
        grad = jnp.zeros((192, 192), F32)
        later, last = None, None
        for m in range(8):
            pieces = []
            zs = []
            for h in (2 * m, 2 * m + 1):
                a = psi_ref[h]
                pieces.append(
                    jnp.concatenate(
                        [
                            pltpu.roll(a, 127, 1).astype(BF),
                            a.astype(BF),
                            pltpu.roll(a, 1, 1).astype(BF),
                        ],
                        axis=0,
                    )
                )
                zs.append(jnp.concatenate([z_s[l, h], z_s[l, h + 1], z_s[l, h + 2]], axis=0))
            rhs = jnp.concatenate(pieces, axis=1)
            zz = jnp.concatenate(zs, axis=1)
            prod = jnp.dot(wt, rhs, preferred_element_type=F32)
            grad = grad + lax.dot_general(
                rhs, zz, (((1,), (1,)), ((), ())), preferred_element_type=F32
            )
            p0, p1 = prod[:, :128], prod[:, 128:]
            if m > 0:
                psi_ref[2 * m - 1] = psi_ref[2 * m - 1] + sl_s[l, 2 * m - 1] * (later + p0[:64])
                first = last + p0[64:128] + p1[:64]
            else:
                first = p0[64:128] + p1[:64]
            psi_ref[2 * m] = psi_ref[2 * m] + sl_s[l, 2 * m] * first
            later = p0[128:] + p1[64:128]
            last = p1[128:]
        psi_ref[15] = psi_ref[15] + sl_s[l, 15] * later
        grad = 0.5 * grad
        g_part[l, 0:192, :] = grad[:, :128]
        g_part[l, 192:288, 0:64] = grad[:96, 128:192]
        g_part[l, 192:288, 64:128] = grad[96:, 128:192]
        ga_copy(l).start()

        @pl.when(step >= 2)
        def _():
            to_owner(l + 2)

        @pl.when(step == 5)
        def _():
            solve(0)

        return carry

    lax.fori_loop(0, blocks, backward, 0)

    send_pieces(1, psi_ref, a_ref, jnp.where(layer == layers - 1, 0.0, 1.0))
    own_block(1)
    to_owner(1)
    to_owner(0)
    solve(1)
    own_block(0)

    def forward_half(k, carry):
        l = blocks - 1 - k

        @pl.when(lax.rem(l, 4) != chip)
        def _():
            remote(
                g_full.at[l, half],
                g_full.at[l, half],
                gc_send.at[0, 0],
                gc_recv.at[l],
                at_chip(lax.rem(l, 4)),
            ).wait_recv()

        gd_copy(l).start()
        return carry

    lax.fori_loop(0, blocks, forward_half, 0)

    for n in range(2):
        for copy in exchange(n):
            copy.wait_send()

    def drain(h, carry):
        @pl.when(jnp.logical_not(stays(h)))
        def _():
            gain_copy(h).wait_send()
            for n in range(2):
                p1_copy(n, h).wait_send()

        for n in range(2):
            skipped = 0 if n == 0 else layers - 1

            @pl.when(jnp.logical_and(h != layer, h != skipped))
            def _():
                p2_copy(n, h).wait_send()

            @pl.when(jnp.logical_and(h != layer, layer != skipped))
            def _():
                remote(
                    p2_snd.at[n, 0],
                    p2_rcv.at[n, h],
                    p2_send.at[n, 0],
                    p2_recv.at[n, h],
                    {"row": 1 - row},
                ).wait_recv()

        return carry

    lax.fori_loop(0, 16, drain, 0)

    def drain_grads(l, carry):
        ga_copy(l).wait_send()

        @pl.when(lax.rem(l, 4) != chip)
        def _():
            gb_copy(l).wait_send()

        gd_copy(l).wait_send()
        remote(
            g_full.at[l, other_half],
            g_full.at[l, other_half],
            gd_send.at[l],
            gd_recv.at[l],
            beside,
        ).wait_recv()
        return carry

    lax.fori_loop(0, blocks, drain_grads, 0)
    for q in range(2):
        for step in range(1, 4):
            gc_copy(4 * q + chip, step).wait_send()
    for n in range(2):

        @pl.when(layer != (0 if n == 0 else layers - 1))
        def _():
            pieces_out[n] = p2_rcv[n]

    grad_out[...] = g_full[...]


def fused(c, a, w, b, gain):
    blocks = w.shape[0]
    vm = pltpu.VMEM
    dma = pltpu.SemaphoreType.DMA
    return pl.pallas_call(
        fused_kernel,
        out_shape=(
            jax.ShapeDtypeStruct((2, 16, 32, 128), BF),
            jax.ShapeDtypeStruct((blocks, 288, 128), BF),
        ),
        in_specs=[pl.BlockSpec(memory_space=pltpu.HBM)] * 5,
        out_specs=[pl.BlockSpec(memory_space=vm)] * 2,
        scratch_shapes=[
            vm((2, 8, 64, 128), BF),
            vm((2, 8, 64, 128), BF),
            vm((2, 2, 8, 16, 128), BF),
            vm((2, 2, 8, 16, 128), BF),
            vm((128, 128), F32),
            vm((8, 128), F32),
            vm((16, 8, 128), F32),
            vm((16, 32, 128), F32),
            vm((64, 128), F32),
            vm((blocks, 192, 192), BF),
            vm((blocks, 192, 192), BF),
            vm((blocks, 64, 128), F32),
            vm((16, 64, 128), F32),
            vm((16, 64, 128), F32),
            vm((blocks, 18, 64, 128), BF),
            vm((blocks, 16, 64, 128), F32),
            vm((2, 16, 32, 128), BF),
            vm((2, 16, 32, 128), BF),
            vm((2, 16, 32, 128), BF),
            vm((2, 16, 32, 128), BF),
            vm((blocks, 288, 128), F32),
            vm((blocks, 144, 128), F32),
            vm((blocks, 144, 128), BF),
            vm((2, 4, 144, 128), BF),
            vm((blocks, 288, 128), BF),
            dma((2, 3)),
            dma((2, 3)),
            dma((16,)),
            dma((16,)),
            dma((2, 16)),
            dma((2, 16)),
            dma((2, 16)),
            dma((2, 16)),
            dma((blocks,)),
            dma((blocks,)),
            dma((blocks,)),
            dma((2, 4)),
            dma((2, 3)),
            dma((blocks,)),
            dma((blocks,)),
            dma((blocks,)),
            vm(c.shape, F32),
            vm(a.shape, F32),
            vm(w.shape, BF),
            vm(b.shape, F32),
            vm(gain.shape, F32),
            dma((5,)),
        ],
        compiler_params=pltpu.CompilerParams(
            vmem_limit_bytes=48 << 20, collective_id=0, has_side_effects=True
        ),
    )(c, a, w, b, gain)


def unpack_kernel(c_ref, a_ref, pieces_ref, grad_ref, c_out, a_out, g_out, c_s, a_s, g_s, sem):
    layer = lax.axis_index("layer")
    layers = lax.axis_size("layer")
    blocks = grad_ref.shape[0]
    lane32 = lax.broadcasted_iota(jnp.int32, (32, 128), 1)

    def states(n, whole, part, out, skipped):
        @pl.when(layer == skipped)
        def _():
            pltpu.make_async_copy(whole, out, sem.at[blocks + n]).start()

        @pl.when(layer != skipped)
        def _():
            for u in range(8):
                left = pieces_ref[n, 2 * u].astype(F32)
                right = pieces_ref[n, 2 * u + 1].astype(F32)
                part[pl.ds(u, 32, stride=8), :] = jnp.where(
                    lane32 < 64, left, pltpu.roll(right, 64, 1)
                )
                part[pl.ds(256 + u, 32, stride=8), :] = jnp.where(
                    lane32 < 64, pltpu.roll(left, 64, 1), right
                )
            pltpu.make_async_copy(part, out, sem.at[blocks + n]).start()

    def one(l, carry):
        for j in range(3):
            g_s[l, j] = grad_ref[l, 64 * j : 64 * j + 64, 0:64].astype(F32)
            g_s[l, 3 + j] = grad_ref[l, 64 * j : 64 * j + 64, 64:128].astype(F32)
        g_s[l, 6] = grad_ref[l, 192:256, 0:64].astype(F32)
        g_s[l, 7, 0:32] = grad_ref[l, 256:288, 0:64].astype(F32)
        g_s[l, 7, 32:64] = grad_ref[l, 192:224, 64:128].astype(F32)
        g_s[l, 8] = grad_ref[l, 224:288, 64:128].astype(F32)
        pltpu.make_async_copy(g_s.at[l], g_out.at[l], sem.at[l]).start()
        return carry

    lax.fori_loop(0, blocks, one, 0)
    states(0, c_ref, c_s, c_out, 0)
    states(1, a_ref, a_s, a_out, layers - 1)
    for l in range(blocks):
        pltpu.make_async_copy(g_s.at[l], g_out.at[l], sem.at[l]).wait()
    pltpu.make_async_copy(c_s, c_out, sem.at[blocks]).wait()
    pltpu.make_async_copy(a_s, a_out, sem.at[blocks + 1]).wait()


def unpack(c, a, pieces, grad):
    blocks = grad.shape[0]
    vm = pltpu.VMEM
    far = pl.BlockSpec(memory_space=pltpu.HBM)
    return pl.pallas_call(
        unpack_kernel,
        out_shape=(
            jax.ShapeDtypeStruct((512, 128), F32),
            jax.ShapeDtypeStruct((512, 128), F32),
            jax.ShapeDtypeStruct((blocks, 9, 64, 64), F32),
        ),
        in_specs=[far, far, pl.BlockSpec(memory_space=vm), pl.BlockSpec(memory_space=vm)],
        out_specs=[far] * 3,
        scratch_shapes=[
            vm((512, 128), F32),
            vm((512, 128), F32),
            vm((blocks, 9, 64, 64), F32),
            pltpu.SemaphoreType.DMA((blocks + 2,)),
        ],
        compiler_params=pltpu.CompilerParams(vmem_limit_bytes=32 << 20),
    )(c, a, pieces, grad)


def local(c_guess, adjoint_guess, weights, biases, coarse_gain):
    c = c_guess.reshape(512, 128)
    a = adjoint_guess.reshape(512, 128)
    far = [
        pltpu.with_memory_space_constraint(x, pltpu.HBM)
        for x in (c, a, weights, biases, coarse_gain)
    ]
    pieces, grad = fused(*far)
    c_states, ends, weight_grad = unpack(far[0], far[1], pieces, grad)
    return (c_states.reshape(c_guess.shape), ends.reshape(c_guess.shape), weight_grad)


def solution(mesh):
    in_specs = (
        P("layer", None, None, "row", "col"),
        P("layer", None, None, "row", "col"),
        P("layer", None, None, None),
        P("layer", None),
        P("layer", None),
    )
    out_specs = (
        P("layer", None, None, "row", "col"),
        P("layer", None, None, "row", "col"),
        P("layer", None, None, None),
    )
    return jax.shard_map(local, mesh=mesh, in_specs=in_specs, out_specs=out_specs, check_vma=False)
```

```python
import jax
import jax.numpy as jnp
from jax import lax
from jax.experimental import pallas as pl
from jax.experimental.pallas import tpu as pltpu
from jax.sharding import PartitionSpec as P

HALO = 32
OWN = 64
BF = jnp.bfloat16
F32 = jnp.float32
MESH = pl.DeviceIdType.MESH


def remote(src, dst, send, recv, where):
    return pltpu.make_async_remote_copy(
        src_ref=src,
        dst_ref=dst,
        send_sem=send,
        recv_sem=recv,
        device_id=where,
        device_id_type=MESH,
    )


def fused_kernel(
    c_hbm,
    a_hbm,
    w_hbm,
    b_hbm,
    gain_hbm,
    pieces_out,
    grad_out,
    snd,
    rcv,
    edge_snd,
    edge_rcv,
    tmp,
    gain_snd,
    gain_rcv,
    gain_pk,
    gain_own,
    w_ref,
    wt_ref,
    b_s,
    phi_ref,
    psi_ref,
    z_s,
    sl_s,
    p1_snd,
    p1_rcv,
    p2_snd,
    p2_rcv,
    g_part,
    g_sib,
    g_half,
    g_chip,
    g_full,
    in_send,
    in_recv,
    gain_send,
    gain_recv,
    p1_send,
    p1_recv,
    p2_send,
    p2_recv,
    ga_send,
    ga_recv,
    gb_send,
    gb_recv,
    gc_send,
    gc_recv,
    gd_send,
    gd_recv,
    c_ref,
    a_ref,
    w_in,
    b_ref,
    gain_ref,
    load_sem,
    q_s,
):
    blocks = w_in.shape[0]
    layer = lax.axis_index("layer")
    row = lax.axis_index("row")
    col = lax.axis_index("col")
    layers = lax.axis_size("layer")
    cols = lax.axis_size("col")
    core = lax.rem(col, 2)
    chip = 2 * row + col // 2
    strip = 2 * col + row
    lane = lax.broadcasted_iota(jnp.int32, (64, 128), 1)
    lane32 = lax.broadcasted_iota(jnp.int32, (32, 128), 1)
    lane16 = lax.broadcasted_iota(jnp.int32, (16, 128), 1)
    column = strip * OWN - HALO + lane
    inside = jnp.where((column >= 0) & (column < 2 * cols * OWN), 1.0, 0.0).astype(F32)
    own = jnp.where((lane >= HALO) & (lane < HALO + OWN), 1.0, 0.0).astype(F32)
    top = row == 0

    loads = [
        pltpu.make_async_copy(src, dst, load_sem.at[n])
        for n, (src, dst) in enumerate(
            (
                (c_hbm, c_ref),
                (a_hbm, a_ref),
                (w_hbm, w_in),
                (b_hbm, b_ref),
                (gain_hbm, gain_ref),
            )
        )
    ]
    for load in loads:
        load.start()

    barrier = pltpu.get_barrier_semaphore()

    pl.semaphore_signal(barrier, inc=1, device_id={"row": 1 - row}, device_id_type=MESH)
    for step in range(1, cols):
        for rho in range(2):
            pl.semaphore_signal(
                barrier,
                inc=1,
                device_id={"row": rho, "col": lax.rem(col + step, cols)},
                device_id_type=MESH,
            )
    for step in range(1, layers):
        for rho in range(2):
            pl.semaphore_signal(
                barrier,
                inc=1,
                device_id={"layer": lax.rem(layer + step, layers), "row": rho},
                device_id_type=MESH,
            )

    def pack(src, n):
        def one(h, carry):
            x = src[pl.ds(h, 64, stride=8), :]
            snd[n, h] = x.astype(BF)
            for side in range(2):
                edge = jnp.zeros((16, 128), F32)
                for g in range(4):
                    part = x[16 * g : 16 * g + 16]
                    shift = (32 * g + (32 if side == 0 else 0)) % 128
                    if shift:
                        part = pltpu.roll(part, shift, 1)
                    edge = jnp.where(lane16 // 32 == g, part, edge)
                edge_snd[side, n, h] = edge.astype(BF)
            return carry

        lax.fori_loop(0, 8, one, 0)

    def exchange(n):
        yield remote(snd.at[n], rcv.at[n], in_send.at[n, 0], in_recv.at[n, 0], {"row": 1 - row})
        yield remote(
            edge_snd.at[0, n],
            edge_rcv.at[row, n],
            in_send.at[n, 1],
            in_recv.at[n, 1 + row],
            {"row": 0, "col": lax.rem(col + 1, cols)},
        )
        yield remote(
            edge_snd.at[1, n],
            edge_rcv.at[row, n],
            in_send.at[n, 2],
            in_recv.at[n, 1 + row],
            {"row": 1, "col": lax.rem(col + cols - 1, cols)},
        )

    def arrived(n):
        remote(snd.at[n], rcv.at[n], in_send.at[n, 0], in_recv.at[n, 0], {"row": 1 - row}).wait_recv()
        for rho in range(2):
            remote(
                edge_snd.at[0, n],
                edge_rcv.at[rho, n],
                in_send.at[n, 1],
                in_recv.at[n, 1 + rho],
                {"row": 1 - row},
            ).wait_recv()

    loads[0].wait()
    pack(c_ref, 0)
    pl.semaphore_wait(barrier, 2 * layers - 1 + 2 * (cols - 1))
    for copy in exchange(0):
        copy.start()
    loads[1].wait()
    pack(a_ref, 1)
    for copy in exchange(1):
        copy.start()

    def lay_weights(l, carry):
        for i in range(3):
            w_ref[l, 64 * i : 64 * i + 64, :] = jnp.concatenate(
                [w_in[l, 3 * i + j] * jnp.asarray(0.5, BF) for j in range(3)], axis=1
            )
            stack = w_in[l, 3 * i : 3 * i + 3].reshape(192, 64)
            wt_ref[l, 64 * i : 64 * i + 64, :] = (0.5 * stack.astype(F32)).T.astype(BF)
        return carry

    for load in loads[2:]:
        load.wait()
    lax.fori_loop(0, blocks, lay_weights, 0)
    tmp[...] = jnp.zeros_like(tmp)
    tmp[0:blocks, 0:64] = 0.5 * b_ref[...]
    tmp[blocks : blocks + 1, 0:64] = gain_ref[...]
    turned = tmp[...].T
    for l in range(blocks):
        b_s[l] = jnp.broadcast_to(turned[0:64, l : l + 1], (64, 128))
    gain_own[...] = jnp.broadcast_to(turned[0:64, blocks : blocks + 1], (64, 128))
    gain_snd[...] = tmp[blocks : blocks + 8, :]

    def holder(h):
        return 2 * lax.rem(h, 8) + row, h // 8

    def turn(k):
        return 8 * lax.rem(layer + k // 8, 2) + lax.rem(layer // 2 + k, 8)

    def stays(h):
        lam, rho = holder(h)
        return jnp.logical_and(lam == layer, rho == row)

    def gain_copy(h):
        lam, rho = holder(h)
        return remote(
            gain_snd,
            gain_rcv.at[layer],
            gain_send.at[h],
            gain_recv.at[layer],
            {"layer": lam, "row": rho},
        )

    def p1_copy(n, h):
        lam, rho = holder(h)
        return remote(
            p1_snd.at[n, h],
            p1_rcv.at[n, layer],
            p1_send.at[n, h],
            p1_recv.at[n, layer],
            {"layer": lam, "row": rho},
        )

    def comes(e):
        return jnp.logical_or(e != layer, lax.rem(layer, 2) != row)

    def send_gain(k, carry):
        h = turn(k)

        @pl.when(stays(h))
        def _():
            gain_rcv[layer] = gain_snd[...]

        @pl.when(jnp.logical_not(stays(h)))
        def _():
            gain_copy(h).start()

        return carry

    lax.fori_loop(0, 16, send_gain, 0)

    def assemble(src, n, dst):
        shift = jnp.where(top, 32, 96)

        def halo(rho, h):
            packed = edge_rcv[rho, n, h].astype(F32)
            return jnp.concatenate(
                [
                    pltpu.roll(packed, jnp.where(top, (128 - 32 * g) % 128, (96 - 32 * g) % 128), 1)
                    for g in range(4)
                ],
                axis=0,
            )

        start = jnp.where(top, 0, 96)
        outer = (lane >= start) & (lane < start + 32)

        def one(h, carry):
            x = src[pl.ds(h, 64, stride=8), :]
            dst[8 * row + h] = jnp.where(outer, halo(row, h), pltpu.roll(x, shift, 1)) * inside
            y = rcv[n, h].astype(F32)
            dst[8 * (1 - row) + h] = (
                jnp.where(outer, halo(1 - row, h), pltpu.roll(y, shift, 1)) * inside
            )
            return carry

        lax.fori_loop(0, 8, one, 0)

    arrived(0)
    assemble(c_ref, 0, phi_ref)

    zero = jnp.zeros((64, 128), BF)

    def forward(l, carry):
        w = w_ref[l]
        bias = b_s[l]
        z_s[l, 0] = zero
        z_s[l, 17] = zero
        later, last = None, None
        for m in range(8):
            pieces = []
            for h in (2 * m, 2 * m + 1):
                t = jnp.tanh(phi_ref[h]) * inside
                sl_s[l, h] = inside - t * t
                z_s[l, h + 1] = (t * own).astype(BF)
                pieces.append(
                    jnp.concatenate(
                        [
                            pltpu.roll(t, 1, 1).astype(BF),
                            t.astype(BF),
                            pltpu.roll(t, 127, 1).astype(BF),
                        ],
                        axis=0,
                    )
                )
            rhs = jnp.concatenate(pieces, axis=1)
            prod = jnp.dot(w, rhs, preferred_element_type=F32)
            p0, p1 = prod[:, :128], prod[:, 128:]
            if m > 0:
                phi_ref[2 * m - 1] = phi_ref[2 * m - 1] + bias + (later + p0[128:])
                first = last + p0[64:128] + p1[128:]
            else:
                first = p0[64:128] + p1[128:]
            phi_ref[2 * m] = phi_ref[2 * m] + bias + first
            later = p0[:64] + p1[64:128]
            last = p1[:64]
        phi_ref[15] = phi_ref[15] + bias + later
        return carry

    lax.fori_loop(0, blocks, forward, 0)

    def send_pieces(n, field, guess_own, keep):
        gain = gain_own[...] * keep
        shift = jnp.where(top, 32, 96)
        for u in range(8):
            for rho, guess in (
                (row, guess_own[pl.ds(u, 64, stride=8), :]),
                (1 - row, rcv[n, u].astype(F32)),
            ):
                r = field[8 * rho + u] - gain * pltpu.roll(guess, shift, 1)
                p1_snd[n, 8 * rho + u] = jnp.where(
                    lane32 < 64, pltpu.roll(r[:32], 96, 1), pltpu.roll(r[32:], 32, 1)
                ).astype(BF)

        def one(k, carry):
            h = turn(k)

            @pl.when(jnp.logical_not(stays(h)))
            def _():
                p1_copy(n, h).start()

            return carry

        lax.fori_loop(0, 16, one, 0)

        @pl.when(lax.rem(layer, 2) == row)
        def _():
            p1_rcv[n, layer] = p1_snd[n, 8 * row + layer // 2]

    def p2_copy(n, e):
        return remote(
            p2_snd.at[n, e],
            p2_rcv.at[n, layer],
            p2_send.at[n, e],
            p2_recv.at[n, layer],
            {"layer": e},
        )

    def solve(n):
        first = 0 if n == 0 else layers - 1
        stride = 1 if n == 0 else -1

        def take(e, carry):
            @pl.when(comes(e))
            def _():
                remote(
                    p1_snd.at[n, 0],
                    p1_rcv.at[n, e],
                    p1_send.at[n, 0],
                    p1_recv.at[n, e],
                    {"layer": layer, "row": 1 - row},
                ).wait_recv()

            return carry

        lax.fori_loop(0, layers, take, 0)
        state = jnp.zeros((32, 128), F32)
        for k in range(15):
            e = first + stride * k
            state = gain_pk[e] * state + p1_rcv[n, e].astype(F32)
            p2_snd[n, e + stride] = state.astype(BF)
        skipped = 0 if n == 0 else layers - 1

        def give(k, carry):
            e = lax.rem(layer + k, layers)

            @pl.when(e != skipped)
            def _():
                p2_copy(n, e).start()

            return carry

        lax.fori_loop(1, layers, give, 0)

        @pl.when(layer != skipped)
        def _():
            p2_rcv[n, layer] = p2_snd[n, layer]

    send_pieces(0, phi_ref, c_ref, jnp.where(layer == 0, 0.0, 1.0))

    def take_gain(e, carry):
        @pl.when(comes(e))
        def _():
            remote(
                gain_snd,
                gain_rcv.at[e],
                gain_send.at[0],
                gain_recv.at[e],
                {"layer": layer, "row": 1 - row},
            ).wait_recv()

        return carry

    lax.fori_loop(0, layers, take_gain, 0)
    for e in range(16):
        tmp[e : e + 1, :] = gain_rcv[e, 0:1, :]
    turned_all = tmp[...].T
    for e in range(16):
        gain_pk[e] = jnp.where(
            lane32 < 64,
            jnp.broadcast_to(turned_all[0:32, e : e + 1], (32, 128)),
            jnp.broadcast_to(turned_all[32:64, e : e + 1], (32, 128)),
        )

    half = pl.ds(pl.multiple_of(144 * core, 16), 144)
    other_half = pl.ds(pl.multiple_of(144 * (1 - core), 16), 144)
    beside = {"col": col + 1 - 2 * core}

    def ga_copy(l):
        return remote(g_part.at[l, other_half], g_sib.at[l], ga_send.at[l], ga_recv.at[l], beside)

    def at_chip(y):
        return {"row": y // 2, "col": 2 * lax.rem(y, 2) + core}

    def gb_copy(l):
        y = lax.rem(l, 4)
        return remote(
            g_half.at[l],
            g_chip.at[l // 4, chip],
            gb_send.at[l],
            gb_recv.at[l // 4, chip],
            at_chip(y),
        )

    def gc_copy(l, step):
        y = lax.rem(chip + step, 4)
        return remote(
            g_full.at[l, half],
            g_full.at[l, half],
            gc_send.at[l // 4, step - 1],
            gc_recv.at[l],
            at_chip(y),
        )

    def gd_copy(l):
        return remote(g_full.at[l, half], g_full.at[l, half], gd_send.at[l], gd_recv.at[l], beside)

    def to_owner(l):
        ga_copy(l).wait_recv()
        total = (g_part[l, half, :] + g_sib[l]).astype(BF)

        @pl.when(lax.rem(l, 4) == chip)
        def _():
            g_chip[l // 4, chip] = total

        @pl.when(lax.rem(l, 4) != chip)
        def _():
            g_half[l] = total
            gb_copy(l).start()

    def own_block(q):
        l = 4 * q + chip
        for step in range(1, 4):
            y = lax.rem(chip + step, 4)
            remote(
                g_half.at[l],
                g_chip.at[q, y],
                gb_send.at[l],
                gb_recv.at[q, y],
                at_chip(y),
            ).wait_recv()
        total = g_chip[q, 0].astype(F32) + g_chip[q, 1].astype(F32)
        total = total + g_chip[q, 2].astype(F32) + g_chip[q, 3].astype(F32)
        g_full[l, half, :] = total.astype(BF)
        for step in range(1, 4):
            gc_copy(l, step).start()

    arrived(1)
    assemble(a_ref, 1, psi_ref)

    def backward(step, carry):
        l = blocks - 1 - step
        wt = wt_ref[l]
        later, last = None, None
        for m in range(8):
            pieces = []
            for h in (2 * m, 2 * m + 1):
                a = psi_ref[h]
                pieces.append(
                    jnp.concatenate(
                        [
                            pltpu.roll(a, 127, 1).astype(BF),
                            a.astype(BF),
                            pltpu.roll(a, 1, 1).astype(BF),
                        ],
                        axis=0,
                    )
                )
            rhs = jnp.concatenate(pieces, axis=1)
            q_s[l, m] = rhs
            prod = jnp.dot(wt, rhs, preferred_element_type=F32)
            p0, p1 = prod[:, :128], prod[:, 128:]
            if m > 0:
                psi_ref[2 * m - 1] = psi_ref[2 * m - 1] + sl_s[l, 2 * m - 1] * (later + p0[:64])
                first = last + p0[64:128] + p1[:64]
            else:
                first = p0[64:128] + p1[:64]
            psi_ref[2 * m] = psi_ref[2 * m] + sl_s[l, 2 * m] * first
            later = p0[128:] + p1[64:128]
            last = p1[128:]
        psi_ref[15] = psi_ref[15] + sl_s[l, 15] * later
        return carry

    lax.fori_loop(0, blocks, backward, 0)
    send_pieces(1, psi_ref, a_ref, jnp.where(layer == layers - 1, 0.0, 1.0))

    def weight_grads(step, carry):
        l = blocks - 1 - step
        grad = jnp.zeros((192, 192), F32)
        for m in range(8):
            zz = jnp.concatenate(
                [
                    jnp.concatenate([z_s[l, h], z_s[l, h + 1], z_s[l, h + 2]], axis=0)
                    for h in (2 * m, 2 * m + 1)
                ],
                axis=1,
            )
            grad = grad + lax.dot_general(
                q_s[l, m], zz, (((1,), (1,)), ((), ())), preferred_element_type=F32
            )
        grad = 0.5 * grad
        g_part[l, 0:192, :] = grad[:, :128]
        g_part[l, 192:288, 0:64] = grad[:96, 128:192]
        g_part[l, 192:288, 64:128] = grad[96:, 128:192]
        ga_copy(l).start()

        @pl.when(step >= 3)
        def _():
            to_owner(l + 3)

        return carry

    lax.fori_loop(0, blocks, weight_grads, 0)
    for l in (2, 1, 0):
        to_owner(l)
    solve(0)
    own_block(1)
    solve(1)
    own_block(0)

    def forward_half(k, carry):
        l = blocks - 1 - k

        @pl.when(lax.rem(l, 4) != chip)
        def _():
            remote(
                g_full.at[l, half],
                g_full.at[l, half],
                gc_send.at[0, 0],
                gc_recv.at[l],
                at_chip(lax.rem(l, 4)),
            ).wait_recv()

        gd_copy(l).start()
        return carry

    lax.fori_loop(0, blocks, forward_half, 0)

    for n in range(2):
        for copy in exchange(n):
            copy.wait_send()

    def drain(h, carry):
        @pl.when(jnp.logical_not(stays(h)))
        def _():
            gain_copy(h).wait_send()
            for n in range(2):
                p1_copy(n, h).wait_send()

        for n in range(2):
            skipped = 0 if n == 0 else layers - 1

            @pl.when(jnp.logical_and(h != layer, h != skipped))
            def _():
                p2_copy(n, h).wait_send()

            @pl.when(jnp.logical_and(h != layer, layer != skipped))
            def _():
                remote(
                    p2_snd.at[n, 0],
                    p2_rcv.at[n, h],
                    p2_send.at[n, 0],
                    p2_recv.at[n, h],
                    {"row": 1 - row},
                ).wait_recv()

        return carry

    lax.fori_loop(0, 16, drain, 0)

    def drain_grads(l, carry):
        ga_copy(l).wait_send()

        @pl.when(lax.rem(l, 4) != chip)
        def _():
            gb_copy(l).wait_send()

        gd_copy(l).wait_send()
        remote(
            g_full.at[l, other_half],
            g_full.at[l, other_half],
            gd_send.at[l],
            gd_recv.at[l],
            beside,
        ).wait_recv()
        return carry

    lax.fori_loop(0, blocks, drain_grads, 0)
    for q in range(2):
        for step in range(1, 4):
            gc_copy(4 * q + chip, step).wait_send()
    for n in range(2):

        @pl.when(layer != (0 if n == 0 else layers - 1))
        def _():
            pieces_out[n] = p2_rcv[n]

    grad_out[...] = g_full[...]


def fused(c, a, w, b, gain):
    blocks = w.shape[0]
    vm = pltpu.VMEM
    dma = pltpu.SemaphoreType.DMA
    return pl.pallas_call(
        fused_kernel,
        out_shape=(
            jax.ShapeDtypeStruct((2, 16, 32, 128), BF),
            jax.ShapeDtypeStruct((blocks, 288, 128), BF),
        ),
        in_specs=[pl.BlockSpec(memory_space=pltpu.HBM)] * 5,
        out_specs=[pl.BlockSpec(memory_space=vm)] * 2,
        scratch_shapes=[
            vm((2, 8, 64, 128), BF),
            vm((2, 8, 64, 128), BF),
            vm((2, 2, 8, 16, 128), BF),
            vm((2, 2, 8, 16, 128), BF),
            vm((128, 128), F32),
            vm((8, 128), F32),
            vm((16, 8, 128), F32),
            vm((16, 32, 128), F32),
            vm((64, 128), F32),
            vm((blocks, 192, 192), BF),
            vm((blocks, 192, 192), BF),
            vm((blocks, 64, 128), F32),
            vm((16, 64, 128), F32),
            vm((16, 64, 128), F32),
            vm((blocks, 18, 64, 128), BF),
            vm((blocks, 16, 64, 128), F32),
            vm((2, 16, 32, 128), BF),
            vm((2, 16, 32, 128), BF),
            vm((2, 16, 32, 128), BF),
            vm((2, 16, 32, 128), BF),
            vm((blocks, 288, 128), F32),
            vm((blocks, 144, 128), F32),
            vm((blocks, 144, 128), BF),
            vm((2, 4, 144, 128), BF),
            vm((blocks, 288, 128), BF),
            dma((2, 3)),
            dma((2, 3)),
            dma((16,)),
            dma((16,)),
            dma((2, 16)),
            dma((2, 16)),
            dma((2, 16)),
            dma((2, 16)),
            dma((blocks,)),
            dma((blocks,)),
            dma((blocks,)),
            dma((2, 4)),
            dma((2, 3)),
            dma((blocks,)),
            dma((blocks,)),
            dma((blocks,)),
            vm(c.shape, F32),
            vm(a.shape, F32),
            vm(w.shape, BF),
            vm(b.shape, F32),
            vm(gain.shape, F32),
            dma((5,)),
            vm((blocks, 8, 192, 256), BF),
        ],
        compiler_params=pltpu.CompilerParams(
            vmem_limit_bytes=48 << 20, collective_id=0, has_side_effects=True
        ),
    )(c, a, w, b, gain)


def unpack_kernel(c_ref, a_ref, pieces_ref, grad_ref, c_out, a_out, g_out, c_s, a_s, g_s, sem):
    layer = lax.axis_index("layer")
    layers = lax.axis_size("layer")
    blocks = grad_ref.shape[0]
    lane32 = lax.broadcasted_iota(jnp.int32, (32, 128), 1)

    for n, whole, part, skipped in ((0, c_ref, c_s, 0), (1, a_ref, a_s, layers - 1)):

        @pl.when(layer == skipped)
        def _():
            pltpu.make_async_copy(whole, part, sem.at[blocks + 2 + n]).start()

    def states(n, whole, part, out, skipped):
        @pl.when(layer == skipped)
        def _():
            pltpu.make_async_copy(whole, part, sem.at[blocks + 2 + n]).wait()

        @pl.when(layer != skipped)
        def _():
            for u in range(8):
                left = pieces_ref[n, 2 * u].astype(F32)
                right = pieces_ref[n, 2 * u + 1].astype(F32)
                part[pl.ds(u, 32, stride=8), :] = jnp.where(
                    lane32 < 64, left, pltpu.roll(right, 64, 1)
                )
                part[pl.ds(256 + u, 32, stride=8), :] = jnp.where(
                    lane32 < 64, pltpu.roll(left, 64, 1), right
                )
        pltpu.make_async_copy(part, out, sem.at[blocks + n]).start()

    def one(l, carry):
        for j in range(3):
            g_s[l, j] = grad_ref[l, 64 * j : 64 * j + 64, 0:64].astype(F32)
            g_s[l, 3 + j] = grad_ref[l, 64 * j : 64 * j + 64, 64:128].astype(F32)
        g_s[l, 6] = grad_ref[l, 192:256, 0:64].astype(F32)
        g_s[l, 7, 0:32] = grad_ref[l, 256:288, 0:64].astype(F32)
        g_s[l, 7, 32:64] = grad_ref[l, 192:224, 64:128].astype(F32)
        g_s[l, 8] = grad_ref[l, 224:288, 64:128].astype(F32)
        pltpu.make_async_copy(g_s.at[l], g_out.at[l], sem.at[l]).start()
        return carry

    lax.fori_loop(0, blocks, one, 0)
    states(0, c_ref, c_s, c_out, 0)
    states(1, a_ref, a_s, a_out, layers - 1)
    for l in range(blocks):
        pltpu.make_async_copy(g_s.at[l], g_out.at[l], sem.at[l]).wait()
    pltpu.make_async_copy(c_s, c_out, sem.at[blocks]).wait()
    pltpu.make_async_copy(a_s, a_out, sem.at[blocks + 1]).wait()


def unpack(c, a, pieces, grad):
    blocks = grad.shape[0]
    vm = pltpu.VMEM
    far = pl.BlockSpec(memory_space=pltpu.HBM)
    return pl.pallas_call(
        unpack_kernel,
        out_shape=(
            jax.ShapeDtypeStruct((512, 128), F32),
            jax.ShapeDtypeStruct((512, 128), F32),
            jax.ShapeDtypeStruct((blocks, 9, 64, 64), F32),
        ),
        in_specs=[far, far, pl.BlockSpec(memory_space=vm), pl.BlockSpec(memory_space=vm)],
        out_specs=[far] * 3,
        scratch_shapes=[
            vm((512, 128), F32),
            vm((512, 128), F32),
            vm((blocks, 9, 64, 64), F32),
            pltpu.SemaphoreType.DMA((blocks + 4,)),
        ],
        compiler_params=pltpu.CompilerParams(vmem_limit_bytes=32 << 20),
    )(c, a, pieces, grad)


def local(c_guess, adjoint_guess, weights, biases, coarse_gain):
    c = c_guess.reshape(512, 128)
    a = adjoint_guess.reshape(512, 128)
    far = [
        pltpu.with_memory_space_constraint(x, pltpu.HBM)
        for x in (c, a, weights, biases, coarse_gain)
    ]
    pieces, grad = fused(*far)
    c_states, ends, weight_grad = unpack(far[0], far[1], pieces, grad)
    return (c_states.reshape(c_guess.shape), ends.reshape(c_guess.shape), weight_grad)


def solution(mesh):
    in_specs = (
        P("layer", None, None, "row", "col"),
        P("layer", None, None, "row", "col"),
        P("layer", None, None, None),
        P("layer", None),
        P("layer", None),
    )
    out_specs = (
        P("layer", None, None, "row", "col"),
        P("layer", None, None, "row", "col"),
        P("layer", None, None, None),
    )
    return jax.shard_map(local, mesh=mesh, in_specs=in_specs, out_specs=out_specs, check_vma=False)
```

```python
import jax
import jax.numpy as jnp
from jax import lax
from jax.experimental import pallas as pl
from jax.experimental.pallas import tpu as pltpu
from jax.sharding import PartitionSpec as P

HALO = 32
OWN = 64
BF = jnp.bfloat16
F32 = jnp.float32
MESH = pl.DeviceIdType.MESH


def remote(src, dst, send, recv, where):
    return pltpu.make_async_remote_copy(
        src_ref=src,
        dst_ref=dst,
        send_sem=send,
        recv_sem=recv,
        device_id=where,
        device_id_type=MESH,
    )


def fused_kernel(
    c_hbm,
    a_hbm,
    w_hbm,
    b_hbm,
    gain_hbm,
    pieces_out,
    grad_out,
    snd,
    rcv,
    edge_snd,
    edge_rcv,
    tmp,
    gain_snd,
    gain_rcv,
    gain_pk,
    gain_own,
    w_ref,
    wt_ref,
    b_s,
    phi_ref,
    psi_ref,
    z_s,
    sl_s,
    p1_snd,
    p1_rcv,
    p2_snd,
    p2_rcv,
    g_part,
    g_sib,
    g_half,
    g_chip,
    g_full,
    in_send,
    in_recv,
    gain_send,
    gain_recv,
    p1_send,
    p1_recv,
    p2_send,
    p2_recv,
    ga_send,
    ga_recv,
    gb_send,
    gb_recv,
    gc_send,
    gc_recv,
    gd_send,
    gd_recv,
    c_ref,
    a_ref,
    w_in,
    b_ref,
    gain_ref,
    load_sem,
    q_s,
):
    blocks = w_in.shape[0]
    layer = lax.axis_index("layer")
    row = lax.axis_index("row")
    col = lax.axis_index("col")
    layers = lax.axis_size("layer")
    cols = lax.axis_size("col")
    core = lax.rem(col, 2)
    chip = 2 * row + col // 2
    strip = 2 * col + row
    lane = lax.broadcasted_iota(jnp.int32, (64, 128), 1)
    lane32 = lax.broadcasted_iota(jnp.int32, (32, 128), 1)
    lane16 = lax.broadcasted_iota(jnp.int32, (16, 128), 1)
    column = strip * OWN - HALO + lane
    inside = jnp.where((column >= 0) & (column < 2 * cols * OWN), 1.0, 0.0).astype(F32)
    own = jnp.where((lane >= HALO) & (lane < HALO + OWN), 1.0, 0.0).astype(F32)
    top = row == 0

    loads = [
        pltpu.make_async_copy(src, dst, load_sem.at[n])
        for n, (src, dst) in enumerate(
            (
                (c_hbm, c_ref),
                (a_hbm, a_ref),
                (w_hbm, w_in),
                (b_hbm, b_ref),
                (gain_hbm, gain_ref),
            )
        )
    ]
    for load in loads:
        load.start()

    barrier = pltpu.get_barrier_semaphore()

    pl.semaphore_signal(barrier, inc=1, device_id={"row": 1 - row}, device_id_type=MESH)
    for step in range(1, cols):
        for rho in range(2):
            pl.semaphore_signal(
                barrier,
                inc=1,
                device_id={"row": rho, "col": lax.rem(col + step, cols)},
                device_id_type=MESH,
            )
    for step in range(1, layers):
        for rho in range(2):
            pl.semaphore_signal(
                barrier,
                inc=1,
                device_id={"layer": lax.rem(layer + step, layers), "row": rho},
                device_id_type=MESH,
            )

    def pack(src, n):
        def one(h, carry):
            x = src[pl.ds(h, 64, stride=8), :]
            snd[n, h] = x.astype(BF)
            for side in range(2):
                edge = jnp.zeros((16, 128), F32)
                for g in range(4):
                    part = x[16 * g : 16 * g + 16]
                    shift = (32 * g + (32 if side == 0 else 0)) % 128
                    if shift:
                        part = pltpu.roll(part, shift, 1)
                    edge = jnp.where(lane16 // 32 == g, part, edge)
                edge_snd[side, n, h] = edge.astype(BF)
            return carry

        lax.fori_loop(0, 8, one, 0)

    def exchange(n):
        yield remote(snd.at[n], rcv.at[n], in_send.at[n, 0], in_recv.at[n, 0], {"row": 1 - row})
        yield remote(
            edge_snd.at[0, n],
            edge_rcv.at[row, n],
            in_send.at[n, 1],
            in_recv.at[n, 1 + row],
            {"row": 0, "col": lax.rem(col + 1, cols)},
        )
        yield remote(
            edge_snd.at[1, n],
            edge_rcv.at[row, n],
            in_send.at[n, 2],
            in_recv.at[n, 1 + row],
            {"row": 1, "col": lax.rem(col + cols - 1, cols)},
        )

    def arrived(n):
        remote(snd.at[n], rcv.at[n], in_send.at[n, 0], in_recv.at[n, 0], {"row": 1 - row}).wait_recv()
        for rho in range(2):
            remote(
                edge_snd.at[0, n],
                edge_rcv.at[rho, n],
                in_send.at[n, 1],
                in_recv.at[n, 1 + rho],
                {"row": 1 - row},
            ).wait_recv()

    loads[0].wait()
    pack(c_ref, 0)
    pl.semaphore_wait(barrier, 2 * layers - 1 + 2 * (cols - 1))
    for copy in exchange(0):
        copy.start()
    loads[1].wait()
    pack(a_ref, 1)
    for copy in exchange(1):
        copy.start()

    def lay_weights(l, carry):
        for i in range(3):
            w_ref[l, 64 * i : 64 * i + 64, :] = jnp.concatenate(
                [w_in[l, 3 * i + j] * jnp.asarray(0.5, BF) for j in range(3)], axis=1
            )
            stack = w_in[l, 3 * i : 3 * i + 3].reshape(192, 64)
            wt_ref[l, 64 * i : 64 * i + 64, :] = (0.5 * stack.astype(F32)).T.astype(BF)
        return carry

    for load in loads[2:]:
        load.wait()
    lax.fori_loop(0, blocks, lay_weights, 0)
    tmp[...] = jnp.zeros_like(tmp)
    tmp[0:blocks, 0:64] = 0.5 * b_ref[...]
    tmp[blocks : blocks + 1, 0:64] = gain_ref[...]
    turned = tmp[...].T
    for l in range(blocks):
        b_s[l] = jnp.broadcast_to(turned[0:64, l : l + 1], (64, 128))
    gain_own[...] = jnp.broadcast_to(turned[0:64, blocks : blocks + 1], (64, 128))
    gain_snd[...] = tmp[blocks : blocks + 8, :]

    def holder(h):
        return 2 * lax.rem(h, 8) + row, h // 8

    rows_far_first = [
        8 * rho + lax.rem(layer // 2 + k, 8) for rho in (1 - row, row) for k in (5, 3, 4, 6, 2, 7, 1, 0)
    ]
    layers_far_first = [
        4 * lax.rem(layer // 4 + dx, 4) + lax.rem(layer + dz, 4)
        for dx, dz in (
            (2, 2), (2, 1), (2, 3), (1, 2), (3, 2), (1, 1), (3, 3), (1, 3), (3, 1),
            (2, 0), (0, 2), (1, 0), (3, 0), (0, 1), (0, 3),
        )
    ]

    def all_but_own(count, wait):
        for own_piece in (True, False):

            @pl.when((lax.rem(layer, 2) == row) == own_piece)
            def _():
                wait(count - 1 if own_piece else count)

    def stays(h):
        lam, rho = holder(h)
        return jnp.logical_and(lam == layer, rho == row)

    def gain_copy(h):
        lam, rho = holder(h)
        return remote(
            gain_snd,
            gain_rcv.at[layer],
            gain_send.at[0],
            gain_recv.at[0],
            {"layer": lam, "row": rho},
        )

    def p1_copy(n, h):
        lam, rho = holder(h)
        return remote(
            p1_snd.at[n, h],
            p1_rcv.at[n, layer],
            p1_send.at[n],
            p1_recv.at[n],
            {"layer": lam, "row": rho},
        )

    def start_unless_here(h, copy):
        @pl.when(jnp.logical_not(stays(h)))
        def _():
            copy.start()

    for h in rows_far_first:
        start_unless_here(h, gain_copy(h))

    @pl.when(lax.rem(layer, 2) == row)
    def _():
        gain_rcv[layer] = gain_snd[...]

    def assemble(src, n, dst):
        shift = jnp.where(top, 32, 96)

        def halo(rho, h):
            packed = edge_rcv[rho, n, h].astype(F32)
            return jnp.concatenate(
                [
                    pltpu.roll(packed, jnp.where(top, (128 - 32 * g) % 128, (96 - 32 * g) % 128), 1)
                    for g in range(4)
                ],
                axis=0,
            )

        start = jnp.where(top, 0, 96)
        outer = (lane >= start) & (lane < start + 32)

        def one(h, carry):
            x = src[pl.ds(h, 64, stride=8), :]
            dst[8 * row + h] = jnp.where(outer, halo(row, h), pltpu.roll(x, shift, 1)) * inside
            y = rcv[n, h].astype(F32)
            dst[8 * (1 - row) + h] = (
                jnp.where(outer, halo(1 - row, h), pltpu.roll(y, shift, 1)) * inside
            )
            return carry

        lax.fori_loop(0, 8, one, 0)

    arrived(0)
    assemble(c_ref, 0, phi_ref)

    zero = jnp.zeros((64, 128), BF)

    def forward(l, carry):
        w = w_ref[l]
        bias = b_s[l]
        z_s[l, 0] = zero
        z_s[l, 17] = zero
        later, last = None, None
        for m in range(8):
            pieces = []
            for h in (2 * m, 2 * m + 1):
                t = jnp.tanh(phi_ref[h]) * inside
                sl_s[l, h] = inside - t * t
                z_s[l, h + 1] = (t * own).astype(BF)
                pieces.append(
                    jnp.concatenate(
                        [
                            pltpu.roll(t, 1, 1).astype(BF),
                            t.astype(BF),
                            pltpu.roll(t, 127, 1).astype(BF),
                        ],
                        axis=0,
                    )
                )
            rhs = jnp.concatenate(pieces, axis=1)
            prod = jnp.dot(w, rhs, preferred_element_type=F32)
            p0, p1 = prod[:, :128], prod[:, 128:]
            if m > 0:
                phi_ref[2 * m - 1] = phi_ref[2 * m - 1] + bias + (later + p0[128:])
                first = last + p0[64:128] + p1[128:]
            else:
                first = p0[64:128] + p1[128:]
            phi_ref[2 * m] = phi_ref[2 * m] + bias + first
            later = p0[:64] + p1[64:128]
            last = p1[:64]
        phi_ref[15] = phi_ref[15] + bias + later
        return carry

    lax.fori_loop(0, blocks, forward, 0)

    def send_pieces(n, field, guess_own, keep):
        gain = gain_own[...] * keep
        shift = jnp.where(top, 32, 96)
        for u in range(8):
            for rho, guess in (
                (row, guess_own[pl.ds(u, 64, stride=8), :]),
                (1 - row, rcv[n, u].astype(F32)),
            ):
                r = field[8 * rho + u] - gain * pltpu.roll(guess, shift, 1)
                p1_snd[n, 8 * rho + u] = jnp.where(
                    lane32 < 64, pltpu.roll(r[:32], 96, 1), pltpu.roll(r[32:], 32, 1)
                ).astype(BF)

        for h in rows_far_first:
            start_unless_here(h, p1_copy(n, h))

        @pl.when(lax.rem(layer, 2) == row)
        def _():
            p1_rcv[n, layer] = p1_snd[n, 8 * row + layer // 2]

    def p2_copy(n, e):
        return remote(
            p2_snd.at[n, e],
            p2_rcv.at[n, layer],
            p2_send.at[n],
            p2_recv.at[n],
            {"layer": e},
        )

    def solve(n):
        first = 0 if n == 0 else layers - 1
        stride = 1 if n == 0 else -1

        all_but_own(
            16,
            lambda count: remote(
                p1_snd.at[n, pl.ds(0, count)],
                p1_rcv.at[n, pl.ds(0, count)],
                p1_send.at[n],
                p1_recv.at[n],
                {"row": 1 - row},
            ).wait_recv(),
        )
        state = jnp.zeros((32, 128), F32)
        for k in range(15):
            e = first + stride * k
            state = gain_pk[e] * state + p1_rcv[n, e].astype(F32)
            p2_snd[n, e + stride] = state.astype(BF)
        skipped = 0 if n == 0 else layers - 1

        for e in layers_far_first:

            @pl.when(e != skipped)
            def _():
                p2_copy(n, e).start()

        @pl.when(layer != skipped)
        def _():
            p2_rcv[n, layer] = p2_snd[n, layer]

    send_pieces(0, phi_ref, c_ref, jnp.where(layer == 0, 0.0, 1.0))

    all_but_own(
        16,
        lambda count: remote(
            gain_rcv.at[pl.ds(0, count)],
            gain_rcv.at[pl.ds(0, count)],
            gain_send.at[0],
            gain_recv.at[0],
            {"row": 1 - row},
        ).wait_recv(),
    )
    for e in range(16):
        tmp[e : e + 1, :] = gain_rcv[e, 0:1, :]
    turned_all = tmp[...].T
    for e in range(16):
        gain_pk[e] = jnp.where(
            lane32 < 64,
            jnp.broadcast_to(turned_all[0:32, e : e + 1], (32, 128)),
            jnp.broadcast_to(turned_all[32:64, e : e + 1], (32, 128)),
        )

    half = pl.ds(pl.multiple_of(144 * core, 16), 144)
    other_half = pl.ds(pl.multiple_of(144 * (1 - core), 16), 144)
    beside = {"col": col + 1 - 2 * core}

    def ga_copy(l):
        return remote(g_part.at[l, other_half], g_sib.at[l], ga_send.at[l], ga_recv.at[l], beside)

    def at_chip(y):
        return {"row": y // 2, "col": 2 * lax.rem(y, 2) + core}

    def gb_copy(l):
        y = lax.rem(l, 4)
        return remote(
            g_half.at[l],
            g_chip.at[l // 4, chip],
            gb_send.at[l],
            gb_recv.at[l // 4, chip],
            at_chip(y),
        )

    def gc_copy(l, step):
        y = lax.rem(chip + step, 4)
        return remote(
            g_full.at[l, half],
            g_full.at[l, half],
            gc_send.at[l // 4, step - 1],
            gc_recv.at[l],
            at_chip(y),
        )

    def gd_copy(l):
        return remote(g_full.at[l, half], g_full.at[l, half], gd_send.at[l], gd_recv.at[l], beside)

    def to_owner(l):
        ga_copy(l).wait_recv()
        total = (g_part[l, half, :] + g_sib[l]).astype(BF)

        @pl.when(lax.rem(l, 4) == chip)
        def _():
            g_chip[l // 4, chip] = total

        @pl.when(lax.rem(l, 4) != chip)
        def _():
            g_half[l] = total
            gb_copy(l).start()

    def own_block(q):
        l = 4 * q + chip
        for step in range(1, 4):
            y = lax.rem(chip + step, 4)
            remote(
                g_half.at[l],
                g_chip.at[q, y],
                gb_send.at[l],
                gb_recv.at[q, y],
                at_chip(y),
            ).wait_recv()
        total = g_chip[q, 0].astype(F32) + g_chip[q, 1].astype(F32)
        total = total + g_chip[q, 2].astype(F32) + g_chip[q, 3].astype(F32)
        g_full[l, half, :] = total.astype(BF)
        for step in range(1, 4):
            gc_copy(l, step).start()

    arrived(1)
    assemble(a_ref, 1, psi_ref)

    def backward(step, carry):
        l = blocks - 1 - step
        wt = wt_ref[l]
        later, last = None, None
        for m in range(8):
            pieces = []
            for h in (2 * m, 2 * m + 1):
                a = psi_ref[h]
                pieces.append(
                    jnp.concatenate(
                        [
                            pltpu.roll(a, 127, 1).astype(BF),
                            a.astype(BF),
                            pltpu.roll(a, 1, 1).astype(BF),
                        ],
                        axis=0,
                    )
                )
            rhs = jnp.concatenate(pieces, axis=1)
            q_s[l, :, 256 * m : 256 * m + 256] = rhs
            prod = jnp.dot(wt, rhs, preferred_element_type=F32)
            p0, p1 = prod[:, :128], prod[:, 128:]
            if m > 0:
                psi_ref[2 * m - 1] = psi_ref[2 * m - 1] + sl_s[l, 2 * m - 1] * (later + p0[:64])
                first = last + p0[64:128] + p1[:64]
            else:
                first = p0[64:128] + p1[:64]
            psi_ref[2 * m] = psi_ref[2 * m] + sl_s[l, 2 * m] * first
            later = p0[128:] + p1[64:128]
            last = p1[128:]
        psi_ref[15] = psi_ref[15] + sl_s[l, 15] * later
        return carry

    lax.fori_loop(0, blocks, backward, 0)
    send_pieces(1, psi_ref, a_ref, jnp.where(layer == layers - 1, 0.0, 1.0))

    def weight_grads(step, carry):
        l = blocks - 1 - step
        zz = jnp.concatenate(
            [
                jnp.concatenate([z_s[l, h], z_s[l, h + 1], z_s[l, h + 2]], axis=0)
                for h in range(16)
            ],
            axis=1,
        )
        grad = lax.dot_general(
            q_s[l], zz, (((1,), (1,)), ((), ())), preferred_element_type=F32
        )
        grad = 0.5 * grad
        g_part[l, 0:192, :] = grad[:, :128]
        g_part[l, 192:288, 0:64] = grad[:96, 128:192]
        g_part[l, 192:288, 64:128] = grad[96:, 128:192]
        ga_copy(l).start()

        @pl.when(step >= 3)
        def _():
            to_owner(l + 3)

        @pl.when(step == 5)
        def _():
            solve(0)

        return carry

    lax.fori_loop(0, blocks, weight_grads, 0)
    for l in (2, 1, 0):
        to_owner(l)
    solve(1)
    own_block(1)
    own_block(0)

    def forward_half(k, carry):
        l = blocks - 1 - k

        @pl.when(lax.rem(l, 4) != chip)
        def _():
            remote(
                g_full.at[l, half],
                g_full.at[l, half],
                gc_send.at[0, 0],
                gc_recv.at[l],
                at_chip(lax.rem(l, 4)),
            ).wait_recv()

        gd_copy(l).start()
        return carry

    lax.fori_loop(0, blocks, forward_half, 0)

    for n in range(2):
        for copy in exchange(n):
            copy.wait_send()

    def sent(count):
        remote(
            gain_rcv.at[pl.ds(0, count)],
            gain_rcv.at[pl.ds(0, count)],
            gain_send.at[0],
            gain_recv.at[0],
            {"row": 1 - row},
        ).wait_send()
        for n in range(2):
            remote(
                p1_snd.at[n, pl.ds(0, count)],
                p1_rcv.at[n, pl.ds(0, count)],
                p1_send.at[n],
                p1_recv.at[n],
                {"row": 1 - row},
            ).wait_send()

    all_but_own(16, sent)

    def p2_bytes(n, count):
        return remote(
            p2_snd.at[n, pl.ds(0, count)],
            p2_rcv.at[n, pl.ds(0, count)],
            p2_send.at[n],
            p2_recv.at[n],
            {"row": 1 - row},
        )

    for n in range(2):
        skipped = 0 if n == 0 else layers - 1

        @pl.when(layer == skipped)
        def _():
            p2_bytes(n, 15).wait_send()

        @pl.when(layer != skipped)
        def _():
            p2_bytes(n, 14).wait_send()
            p2_bytes(n, 15).wait_recv()
            pieces_out[n] = p2_rcv[n]

    def drain_grads(l, carry):
        ga_copy(l).wait_send()

        @pl.when(lax.rem(l, 4) != chip)
        def _():
            gb_copy(l).wait_send()

        gd_copy(l).wait_send()
        remote(
            g_full.at[l, other_half],
            g_full.at[l, other_half],
            gd_send.at[l],
            gd_recv.at[l],
            beside,
        ).wait_recv()
        return carry

    lax.fori_loop(0, blocks, drain_grads, 0)
    for q in range(2):
        for step in range(1, 4):
            gc_copy(4 * q + chip, step).wait_send()
    grad_out[...] = g_full[...]


def fused(c, a, w, b, gain):
    blocks = w.shape[0]
    vm = pltpu.VMEM
    dma = pltpu.SemaphoreType.DMA
    return pl.pallas_call(
        fused_kernel,
        out_shape=(
            jax.ShapeDtypeStruct((2, 16, 32, 128), BF),
            jax.ShapeDtypeStruct((blocks, 288, 128), BF),
        ),
        in_specs=[pl.BlockSpec(memory_space=pltpu.HBM)] * 5,
        out_specs=[pl.BlockSpec(memory_space=vm)] * 2,
        scratch_shapes=[
            vm((2, 8, 64, 128), BF),
            vm((2, 8, 64, 128), BF),
            vm((2, 2, 8, 16, 128), BF),
            vm((2, 2, 8, 16, 128), BF),
            vm((128, 128), F32),
            vm((8, 128), F32),
            vm((16, 8, 128), F32),
            vm((16, 32, 128), F32),
            vm((64, 128), F32),
            vm((blocks, 192, 192), BF),
            vm((blocks, 192, 192), BF),
            vm((blocks, 64, 128), F32),
            vm((16, 64, 128), F32),
            vm((16, 64, 128), F32),
            vm((blocks, 18, 64, 128), BF),
            vm((blocks, 16, 64, 128), F32),
            vm((2, 16, 32, 128), BF),
            vm((2, 16, 32, 128), BF),
            vm((2, 16, 32, 128), BF),
            vm((2, 16, 32, 128), BF),
            vm((blocks, 288, 128), F32),
            vm((blocks, 144, 128), F32),
            vm((blocks, 144, 128), BF),
            vm((2, 4, 144, 128), BF),
            vm((blocks, 288, 128), BF),
            dma((2, 3)),
            dma((2, 3)),
            dma((1,)),
            dma((1,)),
            dma((2,)),
            dma((2,)),
            dma((2,)),
            dma((2,)),
            dma((blocks,)),
            dma((blocks,)),
            dma((blocks,)),
            dma((2, 4)),
            dma((2, 3)),
            dma((blocks,)),
            dma((blocks,)),
            dma((blocks,)),
            vm(c.shape, F32),
            vm(a.shape, F32),
            vm(w.shape, BF),
            vm(b.shape, F32),
            vm(gain.shape, F32),
            dma((5,)),
            vm((blocks, 192, 2048), BF),
        ],
        compiler_params=pltpu.CompilerParams(
            vmem_limit_bytes=48 << 20, collective_id=0, has_side_effects=True
        ),
    )(c, a, w, b, gain)


def unpack_kernel(c_ref, a_ref, pieces_ref, grad_ref, c_out, a_out, g_out, c_s, a_s, g_s, sem):
    layer = lax.axis_index("layer")
    layers = lax.axis_size("layer")
    blocks = grad_ref.shape[0]
    lane32 = lax.broadcasted_iota(jnp.int32, (32, 128), 1)

    for n, whole, part, skipped in ((0, c_ref, c_s, 0), (1, a_ref, a_s, layers - 1)):

        @pl.when(layer == skipped)
        def _():
            pltpu.make_async_copy(whole, part, sem.at[blocks + 2 + n]).start()

    def states(n, whole, part, out, skipped):
        @pl.when(layer == skipped)
        def _():
            pltpu.make_async_copy(whole, part, sem.at[blocks + 2 + n]).wait()

        @pl.when(layer != skipped)
        def _():
            for u in range(8):
                left = pieces_ref[n, 2 * u].astype(F32)
                right = pieces_ref[n, 2 * u + 1].astype(F32)
                part[pl.ds(u, 32, stride=8), :] = jnp.where(
                    lane32 < 64, left, pltpu.roll(right, 64, 1)
                )
                part[pl.ds(256 + u, 32, stride=8), :] = jnp.where(
                    lane32 < 64, pltpu.roll(left, 64, 1), right
                )
        pltpu.make_async_copy(part, out, sem.at[blocks + n]).start()

    def one(l, carry):
        for j in range(3):
            g_s[l, j] = grad_ref[l, 64 * j : 64 * j + 64, 0:64].astype(F32)
            g_s[l, 3 + j] = grad_ref[l, 64 * j : 64 * j + 64, 64:128].astype(F32)
        g_s[l, 6] = grad_ref[l, 192:256, 0:64].astype(F32)
        g_s[l, 7, 0:32] = grad_ref[l, 256:288, 0:64].astype(F32)
        g_s[l, 7, 32:64] = grad_ref[l, 192:224, 64:128].astype(F32)
        g_s[l, 8] = grad_ref[l, 224:288, 64:128].astype(F32)
        pltpu.make_async_copy(g_s.at[l], g_out.at[l], sem.at[l]).start()
        return carry

    lax.fori_loop(0, blocks, one, 0)
    states(0, c_ref, c_s, c_out, 0)
    states(1, a_ref, a_s, a_out, layers - 1)
    for l in range(blocks):
        pltpu.make_async_copy(g_s.at[l], g_out.at[l], sem.at[l]).wait()
    pltpu.make_async_copy(c_s, c_out, sem.at[blocks]).wait()
    pltpu.make_async_copy(a_s, a_out, sem.at[blocks + 1]).wait()


def unpack(c, a, pieces, grad):
    blocks = grad.shape[0]
    vm = pltpu.VMEM
    far = pl.BlockSpec(memory_space=pltpu.HBM)
    return pl.pallas_call(
        unpack_kernel,
        out_shape=(
            jax.ShapeDtypeStruct((512, 128), F32),
            jax.ShapeDtypeStruct((512, 128), F32),
            jax.ShapeDtypeStruct((blocks, 9, 64, 64), F32),
        ),
        in_specs=[far, far, pl.BlockSpec(memory_space=vm), pl.BlockSpec(memory_space=vm)],
        out_specs=[far] * 3,
        scratch_shapes=[
            vm((512, 128), F32),
            vm((512, 128), F32),
            vm((blocks, 9, 64, 64), F32),
            pltpu.SemaphoreType.DMA((blocks + 4,)),
        ],
        compiler_params=pltpu.CompilerParams(vmem_limit_bytes=32 << 20),
    )(c, a, pieces, grad)


def local(c_guess, adjoint_guess, weights, biases, coarse_gain):
    c = c_guess.reshape(512, 128)
    a = adjoint_guess.reshape(512, 128)
    far = [
        pltpu.with_memory_space_constraint(x, pltpu.HBM)
        for x in (c, a, weights, biases, coarse_gain)
    ]
    pieces, grad = fused(*far)
    c_states, ends, weight_grad = unpack(far[0], far[1], pieces, grad)
    return (c_states.reshape(c_guess.shape), ends.reshape(c_guess.shape), weight_grad)


def solution(mesh):
    in_specs = (
        P("layer", None, None, "row", "col"),
        P("layer", None, None, "row", "col"),
        P("layer", None, None, None),
        P("layer", None),
        P("layer", None),
    )
    out_specs = (
        P("layer", None, None, "row", "col"),
        P("layer", None, None, "row", "col"),
        P("layer", None, None, None),
    )
    return jax.shard_map(local, mesh=mesh, in_specs=in_specs, out_specs=out_specs, check_vma=False)
```

```python
import jax
import jax.numpy as jnp
from jax import lax
from jax.experimental import pallas as pl
from jax.experimental.pallas import tpu as pltpu
from jax.sharding import PartitionSpec as P

HALO = 32
OWN = 64
SPLIT = 4
BF = jnp.bfloat16
F32 = jnp.float32
MESH = pl.DeviceIdType.MESH


def remote(src, dst, send, recv, where):
    return pltpu.make_async_remote_copy(
        src_ref=src,
        dst_ref=dst,
        send_sem=send,
        recv_sem=recv,
        device_id=where,
        device_id_type=MESH,
    )


def fused_kernel(
    c_hbm,
    a_hbm,
    w_hbm,
    b_hbm,
    gain_hbm,
    pieces_out,
    grad_out,
    snd,
    rcv,
    edge_snd,
    edge_rcv,
    tmp,
    gain_snd,
    gain_rcv,
    gain_pk,
    gain_own,
    w_ref,
    wt_ref,
    b_s,
    phi_ref,
    psi_ref,
    z_s,
    sl_s,
    p1_snd,
    p1_rcv,
    p2_snd,
    g_part,
    g_sib,
    g_half,
    g_chip,
    in_send,
    in_recv,
    gain_send,
    gain_recv,
    p1_send,
    p1_recv,
    p2_send,
    p2_recv,
    ga_send,
    ga_recv,
    gb_send,
    gb_recv,
    gc_send,
    gc_recv,
    gd_send,
    gd_recv,
    c_ref,
    a_ref,
    w_in,
    b_ref,
    gain_ref,
    load_sem,
    q_s,
):
    blocks = w_in.shape[0]
    layer = lax.axis_index("layer")
    row = lax.axis_index("row")
    col = lax.axis_index("col")
    layers = lax.axis_size("layer")
    cols = lax.axis_size("col")
    core = lax.rem(col, 2)
    chip = 2 * row + col // 2
    strip = 2 * col + row
    lane = lax.broadcasted_iota(jnp.int32, (64, 128), 1)
    lane32 = lax.broadcasted_iota(jnp.int32, (32, 128), 1)
    lane16 = lax.broadcasted_iota(jnp.int32, (16, 128), 1)
    column = strip * OWN - HALO + lane
    inside = jnp.where((column >= 0) & (column < 2 * cols * OWN), 1.0, 0.0).astype(F32)
    own = jnp.where((lane >= HALO) & (lane < HALO + OWN), 1.0, 0.0).astype(F32)
    top = row == 0

    loads = [
        pltpu.make_async_copy(src, dst, load_sem.at[n])
        for n, (src, dst) in enumerate(
            (
                (c_hbm, c_ref),
                (a_hbm, a_ref),
                (w_hbm, w_in),
                (b_hbm, b_ref),
                (gain_hbm, gain_ref),
            )
        )
    ]
    for load in loads:
        load.start()

    barrier = pltpu.get_barrier_semaphore()

    pl.semaphore_signal(barrier, inc=1, device_id={"row": 1 - row}, device_id_type=MESH)
    for step in range(1, cols):
        for rho in range(2):
            pl.semaphore_signal(
                barrier,
                inc=1,
                device_id={"row": rho, "col": lax.rem(col + step, cols)},
                device_id_type=MESH,
            )
    for step in range(1, layers):
        for rho in range(2):
            pl.semaphore_signal(
                barrier,
                inc=1,
                device_id={"layer": lax.rem(layer + step, layers), "row": rho},
                device_id_type=MESH,
            )

    def pack(src, n):
        def one(h, carry):
            x = src[pl.ds(h, 64, stride=8), :]
            snd[n, h] = x.astype(BF)
            for side in range(2):
                edge = jnp.zeros((16, 128), F32)
                for g in range(4):
                    part = x[16 * g : 16 * g + 16]
                    shift = (32 * g + (32 if side == 0 else 0)) % 128
                    if shift:
                        part = pltpu.roll(part, shift, 1)
                    edge = jnp.where(lane16 // 32 == g, part, edge)
                edge_snd[side, n, h] = edge.astype(BF)
            return carry

        lax.fori_loop(0, 8, one, 0)

    def exchange(n):
        yield remote(snd.at[n], rcv.at[n], in_send.at[n, 0], in_recv.at[n, 0], {"row": 1 - row})
        yield remote(
            edge_snd.at[0, n],
            edge_rcv.at[row, n],
            in_send.at[n, 1],
            in_recv.at[n, 1 + row],
            {"row": 0, "col": lax.rem(col + 1, cols)},
        )
        yield remote(
            edge_snd.at[1, n],
            edge_rcv.at[row, n],
            in_send.at[n, 2],
            in_recv.at[n, 1 + row],
            {"row": 1, "col": lax.rem(col + cols - 1, cols)},
        )

    def arrived(n):
        remote(snd.at[n], rcv.at[n], in_send.at[n, 0], in_recv.at[n, 0], {"row": 1 - row}).wait_recv()
        for rho in range(2):
            remote(
                edge_snd.at[0, n],
                edge_rcv.at[rho, n],
                in_send.at[n, 1],
                in_recv.at[n, 1 + rho],
                {"row": 1 - row},
            ).wait_recv()

    loads[0].wait()
    pack(c_ref, 0)
    pl.semaphore_wait(barrier, 2 * layers - 1 + 2 * (cols - 1))
    for copy in exchange(0):
        copy.start()
    loads[1].wait()
    pack(a_ref, 1)
    for copy in exchange(1):
        copy.start()

    def lay_weights(l, carry):
        for i in range(3):
            w_ref[l, 64 * i : 64 * i + 64, :] = jnp.concatenate(
                [w_in[l, 3 * i + j] * jnp.asarray(0.5, BF) for j in range(3)], axis=1
            )
            stack = w_in[l, 3 * i : 3 * i + 3].reshape(192, 64)
            wt_ref[l, 64 * i : 64 * i + 64, :] = (0.5 * stack.astype(F32)).T.astype(BF)
        return carry

    for load in loads[2:]:
        load.wait()
    lax.fori_loop(0, blocks, lay_weights, 0)
    tmp[...] = jnp.zeros_like(tmp)
    tmp[0:blocks, 0:64] = 0.5 * b_ref[...]
    tmp[blocks : blocks + 1, 0:64] = gain_ref[...]
    turned = tmp[...].T
    for l in range(blocks):
        b_s[l] = jnp.broadcast_to(turned[0:64, l : l + 1], (64, 128))
    gain_own[...] = jnp.broadcast_to(turned[0:64, blocks : blocks + 1], (64, 128))
    gain_snd[...] = tmp[blocks : blocks + 8, :]

    def holder(h):
        return 2 * lax.rem(h, 8) + row, h // 8

    rows_far_first = [
        8 * rho + lax.rem(layer // 2 + k, 8) for rho in (1 - row, row) for k in (5, 3, 4, 6, 2, 7, 1, 0)
    ]
    layers_far_first = [
        4 * lax.rem(layer // 4 + dx, 4) + lax.rem(layer + dz, 4)
        for dx, dz in (
            (2, 2), (2, 1), (2, 3), (1, 2), (3, 2), (1, 1), (3, 3), (1, 3), (3, 1),
            (2, 0), (0, 2), (1, 0), (3, 0), (0, 1), (0, 3),
        )
    ]

    def all_but_own(count, wait):
        for own_piece in (True, False):

            @pl.when((lax.rem(layer, 2) == row) == own_piece)
            def _():
                wait(count - 1 if own_piece else count)

    def stays(h):
        lam, rho = holder(h)
        return jnp.logical_and(lam == layer, rho == row)

    def gain_copy(h):
        lam, rho = holder(h)
        return remote(
            gain_snd,
            gain_rcv.at[layer],
            gain_send.at[0],
            gain_recv.at[0],
            {"layer": lam, "row": rho},
        )

    def p1_copy(n, h):
        lam, rho = holder(h)
        return remote(
            p1_snd.at[n, h],
            p1_rcv.at[n, layer],
            p1_send.at[n],
            p1_recv.at[n],
            {"layer": lam, "row": rho},
        )

    def start_unless_here(h, copy):
        @pl.when(jnp.logical_not(stays(h)))
        def _():
            copy.start()

    for h in rows_far_first:
        start_unless_here(h, gain_copy(h))

    @pl.when(lax.rem(layer, 2) == row)
    def _():
        gain_rcv[layer] = gain_snd[...]

    def assemble(src, n, dst):
        shift = jnp.where(top, 32, 96)

        def halo(rho, h):
            packed = edge_rcv[rho, n, h].astype(F32)
            return jnp.concatenate(
                [
                    pltpu.roll(packed, jnp.where(top, (128 - 32 * g) % 128, (96 - 32 * g) % 128), 1)
                    for g in range(4)
                ],
                axis=0,
            )

        start = jnp.where(top, 0, 96)
        outer = (lane >= start) & (lane < start + 32)

        def one(h, carry):
            x = src[pl.ds(h, 64, stride=8), :]
            dst[8 * row + h] = jnp.where(outer, halo(row, h), pltpu.roll(x, shift, 1)) * inside
            y = rcv[n, h].astype(F32)
            dst[8 * (1 - row) + h] = (
                jnp.where(outer, halo(1 - row, h), pltpu.roll(y, shift, 1)) * inside
            )
            return carry

        lax.fori_loop(0, 8, one, 0)

    arrived(0)
    assemble(c_ref, 0, phi_ref)

    zero = jnp.zeros((64, 128), BF)

    def forward(l, carry):
        w = w_ref[l]
        bias = b_s[l]
        z_s[l, 0] = zero
        z_s[l, 17] = zero
        later, last = None, None
        for m in range(8):
            pieces = []
            for h in (2 * m, 2 * m + 1):
                t = jnp.tanh(phi_ref[h]) * inside
                sl_s[l, h] = inside - t * t
                z_s[l, h + 1] = (t * own).astype(BF)
                pieces.append(
                    jnp.concatenate(
                        [
                            pltpu.roll(t, 1, 1).astype(BF),
                            t.astype(BF),
                            pltpu.roll(t, 127, 1).astype(BF),
                        ],
                        axis=0,
                    )
                )
            rhs = jnp.concatenate(pieces, axis=1)
            prod = jnp.dot(w, rhs, preferred_element_type=F32)
            p0, p1 = prod[:, :128], prod[:, 128:]
            if m > 0:
                phi_ref[2 * m - 1] = phi_ref[2 * m - 1] + bias + (later + p0[128:])
                first = last + p0[64:128] + p1[128:]
            else:
                first = p0[64:128] + p1[128:]
            phi_ref[2 * m] = phi_ref[2 * m] + bias + first
            later = p0[:64] + p1[64:128]
            last = p1[:64]
        phi_ref[15] = phi_ref[15] + bias + later
        return carry

    lax.fori_loop(0, blocks, forward, 0)

    def send_pieces(n, field, guess_own, keep):
        gain = gain_own[...] * keep
        shift = jnp.where(top, 32, 96)
        for u in range(8):
            for rho, guess in (
                (row, guess_own[pl.ds(u, 64, stride=8), :]),
                (1 - row, rcv[n, u].astype(F32)),
            ):
                r = field[8 * rho + u] - gain * pltpu.roll(guess, shift, 1)
                p1_snd[n, 8 * rho + u] = jnp.where(
                    lane32 < 64, pltpu.roll(r[:32], 96, 1), pltpu.roll(r[32:], 32, 1)
                ).astype(BF)

        for h in rows_far_first:
            start_unless_here(h, p1_copy(n, h))

        @pl.when(lax.rem(layer, 2) == row)
        def _():
            p1_rcv[n, layer] = p1_snd[n, 8 * row + layer // 2]

    def p2_copy(n, e):
        return remote(
            p2_snd.at[n, e],
            pieces_out.at[n, layer],
            p2_send.at[n],
            p2_recv.at[n],
            {"layer": e},
        )

    def solve(n):
        first = 0 if n == 0 else layers - 1
        stride = 1 if n == 0 else -1

        all_but_own(
            16,
            lambda count: remote(
                p1_snd.at[n, pl.ds(0, count)],
                p1_rcv.at[n, pl.ds(0, count)],
                p1_send.at[n],
                p1_recv.at[n],
                {"row": 1 - row},
            ).wait_recv(),
        )
        state = jnp.zeros((32, 128), F32)
        for k in range(15):
            e = first + stride * k
            state = gain_pk[e] * state + p1_rcv[n, e].astype(F32)
            p2_snd[n, e + stride] = state.astype(BF)
        skipped = 0 if n == 0 else layers - 1

        for e in layers_far_first:

            @pl.when(e != skipped)
            def _():
                p2_copy(n, e).start()

        @pl.when(layer != skipped)
        def _():
            pieces_out[n, layer] = p2_snd[n, layer]

    send_pieces(0, phi_ref, c_ref, jnp.where(layer == 0, 0.0, 1.0))

    all_but_own(
        16,
        lambda count: remote(
            gain_rcv.at[pl.ds(0, count)],
            gain_rcv.at[pl.ds(0, count)],
            gain_send.at[0],
            gain_recv.at[0],
            {"row": 1 - row},
        ).wait_recv(),
    )
    for e in range(16):
        tmp[e : e + 1, :] = gain_rcv[e, 0:1, :]
    turned_all = tmp[...].T
    for e in range(16):
        gain_pk[e] = jnp.where(
            lane32 < 64,
            jnp.broadcast_to(turned_all[0:32, e : e + 1], (32, 128)),
            jnp.broadcast_to(turned_all[32:64, e : e + 1], (32, 128)),
        )

    half = pl.ds(pl.multiple_of(144 * core, 16), 144)
    other_half = pl.ds(pl.multiple_of(144 * (1 - core), 16), 144)
    beside = {"col": col + 1 - 2 * core}

    def ga_copy(l):
        return remote(g_part.at[l, other_half], g_sib.at[l], ga_send.at[l], ga_recv.at[l], beside)

    def at_chip(y):
        return {"row": y // 2, "col": 2 * lax.rem(y, 2) + core}

    def gb_copy(l):
        y = lax.rem(l, 4)
        return remote(
            g_half.at[l],
            g_chip.at[l // 4, chip],
            gb_send.at[l],
            gb_recv.at[l // 4, chip],
            at_chip(y),
        )

    def gc_copy(l, step):
        y = lax.rem(chip + step, 4)
        return remote(
            grad_out.at[l, half],
            grad_out.at[l, half],
            gc_send.at[l // 4, step - 1],
            gc_recv.at[l],
            at_chip(y),
        )

    def gd_copy(l):
        return remote(grad_out.at[l, half], grad_out.at[l, half], gd_send.at[l], gd_recv.at[l], beside)

    def to_owner(l):
        ga_copy(l).wait_recv()
        total = (g_part[l, half, :] + g_sib[l]).astype(BF)

        @pl.when(lax.rem(l, 4) == chip)
        def _():
            g_chip[l // 4, chip] = total

        @pl.when(lax.rem(l, 4) != chip)
        def _():
            g_half[l] = total
            gb_copy(l).start()

    def own_block(q):
        l = 4 * q + chip
        for step in range(1, 4):
            y = lax.rem(chip + step, 4)
            remote(
                g_half.at[l],
                g_chip.at[q, y],
                gb_send.at[l],
                gb_recv.at[q, y],
                at_chip(y),
            ).wait_recv()
        total = g_chip[q, 0].astype(F32) + g_chip[q, 1].astype(F32)
        total = total + g_chip[q, 2].astype(F32) + g_chip[q, 3].astype(F32)
        grad_out[l, half, :] = total.astype(BF)
        for step in range(1, 4):
            gc_copy(l, step).start()

    arrived(1)
    assemble(a_ref, 1, psi_ref)

    def keep_grad(l, grad):
        grad = 0.5 * grad
        g_part[l, 0:192, :] = grad[:, :128]
        g_part[l, 192:288, 0:64] = grad[:96, 128:192]
        g_part[l, 192:288, 64:128] = grad[96:, 128:192]
        ga_copy(l).start()

    def rows_of(l, first, last):
        return jnp.concatenate(
            [
                jnp.concatenate([z_s[l, h], z_s[l, h + 1], z_s[l, h + 2]], axis=0)
                for h in range(first, last)
            ],
            axis=1,
        )

    def backward(step, with_grad):
        l = blocks - 1 - step
        grad = jnp.zeros((192, 192), F32)
        wt = wt_ref[l]
        later, last = None, None
        for m in range(8):
            pieces = []
            for h in (2 * m, 2 * m + 1):
                a = psi_ref[h]
                pieces.append(
                    jnp.concatenate(
                        [
                            pltpu.roll(a, 127, 1).astype(BF),
                            a.astype(BF),
                            pltpu.roll(a, 1, 1).astype(BF),
                        ],
                        axis=0,
                    )
                )
            rhs = jnp.concatenate(pieces, axis=1)
            if with_grad:
                grad = grad + lax.dot_general(
                    rhs,
                    rows_of(l, 2 * m, 2 * m + 2),
                    (((1,), (1,)), ((), ())),
                    preferred_element_type=F32,
                )
            else:
                q_s[l, :, 256 * m : 256 * m + 256] = rhs
            prod = jnp.dot(wt, rhs, preferred_element_type=F32)
            p0, p1 = prod[:, :128], prod[:, 128:]
            if m > 0:
                psi_ref[2 * m - 1] = psi_ref[2 * m - 1] + sl_s[l, 2 * m - 1] * (later + p0[:64])
                first = last + p0[64:128] + p1[:64]
            else:
                first = p0[64:128] + p1[:64]
            psi_ref[2 * m] = psi_ref[2 * m] + sl_s[l, 2 * m] * first
            later = p0[128:] + p1[64:128]
            last = p1[128:]
        psi_ref[15] = psi_ref[15] + sl_s[l, 15] * later
        if with_grad:
            keep_grad(l, grad)

    def sweep_grads(step, carry):
        backward(step, True)

        @pl.when(step >= 2)
        def _():
            to_owner(blocks + 1 - step)

        return carry

    def sweep(step, carry):
        backward(step, False)
        return carry

    lax.fori_loop(0, SPLIT, sweep_grads, 0)
    lax.fori_loop(SPLIT, blocks, sweep, 0)
    send_pieces(1, psi_ref, a_ref, jnp.where(layer == layers - 1, 0.0, 1.0))

    def weight_grads(step, carry):
        l = blocks - 1 - step
        keep_grad(
            l,
            lax.dot_general(
                q_s[l], rows_of(l, 0, 16), (((1,), (1,)), ((), ())), preferred_element_type=F32
            ),
        )

        @pl.when(step >= SPLIT + 1)
        def _():
            to_owner(l + 3)

        @pl.when(step == 5)
        def _():
            solve(0)

        return carry

    lax.fori_loop(SPLIT, blocks, weight_grads, 0)
    for l in (2, 1, 0):
        to_owner(l)
    solve(1)
    own_block(1)
    own_block(0)

    def forward_half(k, carry):
        l = blocks - 1 - k

        @pl.when(lax.rem(l, 4) != chip)
        def _():
            remote(
                grad_out.at[l, half],
                grad_out.at[l, half],
                gc_send.at[0, 0],
                gc_recv.at[l],
                at_chip(lax.rem(l, 4)),
            ).wait_recv()

        gd_copy(l).start()
        return carry

    lax.fori_loop(0, blocks, forward_half, 0)

    for n in range(2):
        for copy in exchange(n):
            copy.wait_send()

    def sent(count):
        remote(
            gain_rcv.at[pl.ds(0, count)],
            gain_rcv.at[pl.ds(0, count)],
            gain_send.at[0],
            gain_recv.at[0],
            {"row": 1 - row},
        ).wait_send()
        for n in range(2):
            remote(
                p1_snd.at[n, pl.ds(0, count)],
                p1_rcv.at[n, pl.ds(0, count)],
                p1_send.at[n],
                p1_recv.at[n],
                {"row": 1 - row},
            ).wait_send()

    all_but_own(16, sent)

    def p2_bytes(n, count):
        return remote(
            p2_snd.at[n, pl.ds(0, count)],
            pieces_out.at[n, pl.ds(0, count)],
            p2_send.at[n],
            p2_recv.at[n],
            {"row": 1 - row},
        )

    for n in range(2):
        skipped = 0 if n == 0 else layers - 1

        @pl.when(layer == skipped)
        def _():
            p2_bytes(n, 15).wait_send()

        @pl.when(layer != skipped)
        def _():
            p2_bytes(n, 14).wait_send()
            p2_bytes(n, 15).wait_recv()

    def drain_grads(l, carry):
        ga_copy(l).wait_send()

        @pl.when(lax.rem(l, 4) != chip)
        def _():
            gb_copy(l).wait_send()

        gd_copy(l).wait_send()
        remote(
            grad_out.at[l, other_half],
            grad_out.at[l, other_half],
            gd_send.at[l],
            gd_recv.at[l],
            beside,
        ).wait_recv()
        return carry

    lax.fori_loop(0, blocks, drain_grads, 0)
    for q in range(2):
        for step in range(1, 4):
            gc_copy(4 * q + chip, step).wait_send()


def fused(c, a, w, b, gain):
    blocks = w.shape[0]
    vm = pltpu.VMEM
    dma = pltpu.SemaphoreType.DMA
    return pl.pallas_call(
        fused_kernel,
        out_shape=(
            jax.ShapeDtypeStruct((2, 16, 32, 128), BF),
            jax.ShapeDtypeStruct((blocks, 288, 128), BF),
        ),
        in_specs=[pl.BlockSpec(memory_space=pltpu.HBM)] * 5,
        out_specs=[pl.BlockSpec(memory_space=vm)] * 2,
        scratch_shapes=[
            vm((2, 8, 64, 128), BF),
            vm((2, 8, 64, 128), BF),
            vm((2, 2, 8, 16, 128), BF),
            vm((2, 2, 8, 16, 128), BF),
            vm((128, 128), F32),
            vm((8, 128), F32),
            vm((16, 8, 128), F32),
            vm((16, 32, 128), F32),
            vm((64, 128), F32),
            vm((blocks, 192, 192), BF),
            vm((blocks, 192, 192), BF),
            vm((blocks, 64, 128), F32),
            vm((16, 64, 128), F32),
            vm((16, 64, 128), F32),
            vm((blocks, 18, 64, 128), BF),
            vm((blocks, 16, 64, 128), F32),
            vm((2, 16, 32, 128), BF),
            vm((2, 16, 32, 128), BF),
            vm((2, 16, 32, 128), BF),
            vm((blocks, 288, 128), F32),
            vm((blocks, 144, 128), F32),
            vm((blocks, 144, 128), BF),
            vm((2, 4, 144, 128), BF),
            dma((2, 3)),
            dma((2, 3)),
            dma((1,)),
            dma((1,)),
            dma((2,)),
            dma((2,)),
            dma((2,)),
            dma((2,)),
            dma((blocks,)),
            dma((blocks,)),
            dma((blocks,)),
            dma((2, 4)),
            dma((2, 3)),
            dma((blocks,)),
            dma((blocks,)),
            dma((blocks,)),
            vm(c.shape, F32),
            vm(a.shape, F32),
            vm(w.shape, BF),
            vm(b.shape, F32),
            vm(gain.shape, F32),
            dma((5,)),
            vm((blocks, 192, 2048), BF),
        ],
        compiler_params=pltpu.CompilerParams(
            vmem_limit_bytes=48 << 20, collective_id=0, has_side_effects=True
        ),
    )(c, a, w, b, gain)


def unpack_kernel(c_ref, a_ref, pieces_ref, grad_ref, c_out, a_out, g_out, c_s, a_s, g_s, sem):
    layer = lax.axis_index("layer")
    layers = lax.axis_size("layer")
    blocks = grad_ref.shape[0]
    lane32 = lax.broadcasted_iota(jnp.int32, (32, 128), 1)

    for n, whole, part, skipped in ((0, c_ref, c_s, 0), (1, a_ref, a_s, layers - 1)):

        @pl.when(layer == skipped)
        def _():
            pltpu.make_async_copy(whole, part, sem.at[blocks + 2 + n]).start()

    def states(n, whole, part, out, skipped):
        @pl.when(layer == skipped)
        def _():
            pltpu.make_async_copy(whole, part, sem.at[blocks + 2 + n]).wait()

        @pl.when(layer != skipped)
        def _():
            for u in range(8):
                left = pieces_ref[n, 2 * u].astype(F32)
                right = pieces_ref[n, 2 * u + 1].astype(F32)
                part[pl.ds(u, 32, stride=8), :] = jnp.where(
                    lane32 < 64, left, pltpu.roll(right, 64, 1)
                )
                part[pl.ds(256 + u, 32, stride=8), :] = jnp.where(
                    lane32 < 64, pltpu.roll(left, 64, 1), right
                )
        pltpu.make_async_copy(part, out, sem.at[blocks + n]).start()

    def one(l, carry):
        for j in range(3):
            g_s[l, j] = grad_ref[l, 64 * j : 64 * j + 64, 0:64].astype(F32)
            g_s[l, 3 + j] = grad_ref[l, 64 * j : 64 * j + 64, 64:128].astype(F32)
        g_s[l, 6] = grad_ref[l, 192:256, 0:64].astype(F32)
        g_s[l, 7, 0:32] = grad_ref[l, 256:288, 0:64].astype(F32)
        g_s[l, 7, 32:64] = grad_ref[l, 192:224, 64:128].astype(F32)
        g_s[l, 8] = grad_ref[l, 224:288, 64:128].astype(F32)
        pltpu.make_async_copy(g_s.at[l], g_out.at[l], sem.at[l]).start()
        return carry

    lax.fori_loop(0, blocks, one, 0)
    states(0, c_ref, c_s, c_out, 0)
    states(1, a_ref, a_s, a_out, layers - 1)
    for l in range(blocks):
        pltpu.make_async_copy(g_s.at[l], g_out.at[l], sem.at[l]).wait()
    pltpu.make_async_copy(c_s, c_out, sem.at[blocks]).wait()
    pltpu.make_async_copy(a_s, a_out, sem.at[blocks + 1]).wait()


def unpack(c, a, pieces, grad):
    blocks = grad.shape[0]
    vm = pltpu.VMEM
    far = pl.BlockSpec(memory_space=pltpu.HBM)
    return pl.pallas_call(
        unpack_kernel,
        out_shape=(
            jax.ShapeDtypeStruct((512, 128), F32),
            jax.ShapeDtypeStruct((512, 128), F32),
            jax.ShapeDtypeStruct((blocks, 9, 64, 64), F32),
        ),
        in_specs=[far, far, pl.BlockSpec(memory_space=vm), pl.BlockSpec(memory_space=vm)],
        out_specs=[far] * 3,
        scratch_shapes=[
            vm((512, 128), F32),
            vm((512, 128), F32),
            vm((blocks, 9, 64, 64), F32),
            pltpu.SemaphoreType.DMA((blocks + 4,)),
        ],
        compiler_params=pltpu.CompilerParams(vmem_limit_bytes=32 << 20),
    )(c, a, pieces, grad)


def local(c_guess, adjoint_guess, weights, biases, coarse_gain):
    c = c_guess.reshape(512, 128)
    a = adjoint_guess.reshape(512, 128)
    far = [
        pltpu.with_memory_space_constraint(x, pltpu.HBM)
        for x in (c, a, weights, biases, coarse_gain)
    ]
    pieces, grad = fused(*far)
    c_states, ends, weight_grad = unpack(far[0], far[1], pieces, grad)
    return (c_states.reshape(c_guess.shape), ends.reshape(c_guess.shape), weight_grad)


def solution(mesh):
    in_specs = (
        P("layer", None, None, "row", "col"),
        P("layer", None, None, "row", "col"),
        P("layer", None, None, None),
        P("layer", None),
        P("layer", None),
    )
    out_specs = (
        P("layer", None, None, "row", "col"),
        P("layer", None, None, "row", "col"),
        P("layer", None, None, None),
    )
    return jax.shard_map(local, mesh=mesh, in_specs=in_specs, out_specs=out_specs, check_vma=False)
```

```python
import jax
import jax.numpy as jnp
from jax import lax
from jax.experimental import pallas as pl
from jax.experimental.pallas import tpu as pltpu
from jax.sharding import PartitionSpec as P

HALO = 32
OWN = 64
SPLIT = 4
BF = jnp.bfloat16
F32 = jnp.float32
MESH = pl.DeviceIdType.MESH


def remote(src, dst, send, recv, where):
    return pltpu.make_async_remote_copy(
        src_ref=src,
        dst_ref=dst,
        send_sem=send,
        recv_sem=recv,
        device_id=where,
        device_id_type=MESH,
    )


def fused_kernel(
    c_hbm,
    a_hbm,
    w_hbm,
    b_hbm,
    gain_hbm,
    pieces_out,
    grad_out,
    snd,
    rcv,
    edge_snd,
    edge_rcv,
    tmp,
    gain_snd,
    gain_rcv,
    gain_pk,
    gain_own,
    w_ref,
    wt_ref,
    b_s,
    phi_ref,
    psi_ref,
    z_s,
    sl_s,
    p1_snd,
    p1_rcv,
    p2_snd,
    g_part,
    g_sib,
    g_half,
    g_chip,
    in_send,
    in_recv,
    gain_send,
    gain_recv,
    p1_send,
    p1_recv,
    p2_send,
    p2_recv,
    ga_send,
    ga_recv,
    gb_send,
    gb_recv,
    gc_send,
    gc_recv,
    gd_send,
    gd_recv,
    c_ref,
    a_ref,
    w_in,
    b_ref,
    gain_ref,
    load_sem,
    q_s,
):
    blocks = w_in.shape[0]
    layer = lax.axis_index("layer")
    row = lax.axis_index("row")
    col = lax.axis_index("col")
    layers = lax.axis_size("layer")
    cols = lax.axis_size("col")
    core = lax.rem(col, 2)
    chip = 2 * row + col // 2
    strip = 2 * col + row
    lane = lax.broadcasted_iota(jnp.int32, (64, 128), 1)
    lane32 = lax.broadcasted_iota(jnp.int32, (32, 128), 1)
    lane16 = lax.broadcasted_iota(jnp.int32, (16, 128), 1)
    column = strip * OWN - HALO + lane
    inside = jnp.where((column >= 0) & (column < 2 * cols * OWN), 1.0, 0.0).astype(F32)
    own = jnp.where((lane >= HALO) & (lane < HALO + OWN), 1.0, 0.0).astype(F32)
    top = row == 0

    loads = [
        pltpu.make_async_copy(src, dst, load_sem.at[n])
        for n, (src, dst) in enumerate(
            (
                (c_hbm, c_ref),
                (a_hbm, a_ref),
                (w_hbm, w_in),
                (b_hbm, b_ref),
                (gain_hbm, gain_ref),
            )
        )
    ]
    for load in loads:
        load.start()

    barrier = pltpu.get_barrier_semaphore()

    pl.semaphore_signal(barrier, inc=1, device_id={"row": 1 - row}, device_id_type=MESH)
    for step in range(1, cols):
        for rho in range(2):
            pl.semaphore_signal(
                barrier,
                inc=1,
                device_id={"row": rho, "col": lax.rem(col + step, cols)},
                device_id_type=MESH,
            )
    for step in range(1, layers):
        for rho in range(2):
            pl.semaphore_signal(
                barrier,
                inc=1,
                device_id={"layer": lax.rem(layer + step, layers), "row": rho},
                device_id_type=MESH,
            )

    def pack(src, n):
        def one(h, carry):
            x = src[pl.ds(h, 64, stride=8), :]
            turned_by = jnp.where(top, 64, 0)
            middle = jnp.where(
                lane32 < 64,
                pltpu.roll(x[:32], turned_by, 1),
                pltpu.roll(x[32:], 64 - turned_by, 1),
            )
            flank = jnp.zeros((16, 128), F32)
            for g in range(4):
                part = pltpu.roll(
                    x[16 * g : 16 * g + 16],
                    jnp.where(top, (32 * g + 96) % 128, (32 * g + 64) % 128),
                    1,
                )
                flank = jnp.where(lane16 // 32 == g, part, flank)
            snd[n, h] = jnp.concatenate([middle, flank], axis=0).astype(BF)
            for side in range(2):
                edge = jnp.zeros((16, 128), F32)
                for g in range(4):
                    part = x[16 * g : 16 * g + 16]
                    shift = (32 * g + (32 if side == 0 else 0)) % 128
                    if shift:
                        part = pltpu.roll(part, shift, 1)
                    edge = jnp.where(lane16 // 32 == g, part, edge)
                edge_snd[side, n, h] = edge.astype(BF)
            return carry

        lax.fori_loop(0, 8, one, 0)

    def exchange(n):
        yield remote(snd.at[n], rcv.at[n], in_send.at[n, 0], in_recv.at[n, 0], {"row": 1 - row})
        yield remote(
            edge_snd.at[0, n],
            edge_rcv.at[row, n],
            in_send.at[n, 1],
            in_recv.at[n, 1 + row],
            {"row": 0, "col": lax.rem(col + 1, cols)},
        )
        yield remote(
            edge_snd.at[1, n],
            edge_rcv.at[row, n],
            in_send.at[n, 2],
            in_recv.at[n, 1 + row],
            {"row": 1, "col": lax.rem(col + cols - 1, cols)},
        )

    def arrived(n):
        remote(snd.at[n], rcv.at[n], in_send.at[n, 0], in_recv.at[n, 0], {"row": 1 - row}).wait_recv()
        for rho in range(2):
            remote(
                edge_snd.at[0, n],
                edge_rcv.at[rho, n],
                in_send.at[n, 1],
                in_recv.at[n, 1 + rho],
                {"row": 1 - row},
            ).wait_recv()

    loads[0].wait()
    pack(c_ref, 0)
    pl.semaphore_wait(barrier, 2 * layers - 1 + 2 * (cols - 1))
    for copy in exchange(0):
        copy.start()
    loads[1].wait()
    pack(a_ref, 1)
    for copy in exchange(1):
        copy.start()

    def lay_weights(l, carry):
        for i in range(3):
            w_ref[l, 64 * i : 64 * i + 64, :] = jnp.concatenate(
                [w_in[l, 3 * i + j] * jnp.asarray(0.5, BF) for j in range(3)], axis=1
            )
            stack = w_in[l, 3 * i : 3 * i + 3].reshape(192, 64)
            wt_ref[l, 64 * i : 64 * i + 64, :] = (0.5 * stack.astype(F32)).T.astype(BF)
        return carry

    for load in loads[2:]:
        load.wait()
    lax.fori_loop(0, blocks, lay_weights, 0)
    tmp[...] = jnp.zeros_like(tmp)
    tmp[0:blocks, 0:64] = 0.5 * b_ref[...]
    tmp[blocks : blocks + 1, 0:64] = gain_ref[...]
    turned = tmp[...].T
    for l in range(blocks):
        b_s[l] = jnp.broadcast_to(turned[0:64, l : l + 1], (64, 128))
    gain_own[...] = jnp.broadcast_to(turned[0:64, blocks : blocks + 1], (64, 128))
    gain_snd[...] = tmp[blocks : blocks + 8, :]

    def holder(h):
        return 2 * lax.rem(h, 8) + row, h // 8

    rows_far_first = [
        8 * rho + lax.rem(layer // 2 + k, 8) for rho in (1 - row, row) for k in (5, 3, 4, 6, 2, 7, 1, 0)
    ]
    layers_far_first = [
        4 * lax.rem(layer // 4 + dx, 4) + lax.rem(layer + dz, 4)
        for dx, dz in (
            (2, 2), (2, 1), (2, 3), (1, 2), (3, 2), (1, 1), (3, 3), (1, 3), (3, 1),
            (2, 0), (0, 2), (1, 0), (3, 0), (0, 1), (0, 3),
        )
    ]

    def all_but_own(count, wait):
        for own_piece in (True, False):

            @pl.when((lax.rem(layer, 2) == row) == own_piece)
            def _():
                wait(count - 1 if own_piece else count)

    def stays(h):
        lam, rho = holder(h)
        return jnp.logical_and(lam == layer, rho == row)

    def gain_copy(h):
        lam, rho = holder(h)
        return remote(
            gain_snd,
            gain_rcv.at[layer],
            gain_send.at[0],
            gain_recv.at[0],
            {"layer": lam, "row": rho},
        )

    def p1_copy(n, h):
        lam, rho = holder(h)
        return remote(
            p1_snd.at[n, h],
            p1_rcv.at[n, layer],
            p1_send.at[n],
            p1_recv.at[n],
            {"layer": lam, "row": rho},
        )

    def start_unless_here(h, copy):
        @pl.when(jnp.logical_not(stays(h)))
        def _():
            copy.start()

    for h in rows_far_first:
        start_unless_here(h, gain_copy(h))

    @pl.when(lax.rem(layer, 2) == row)
    def _():
        gain_rcv[layer] = gain_snd[...]

    def spread(packed):
        return jnp.concatenate([pltpu.roll(packed, 32, 1), pltpu.roll(packed, 96, 1)], axis=0)

    def assemble(src, n, dst):
        shift = jnp.where(top, 32, 96)

        def halo(rho, h):
            packed = edge_rcv[rho, n, h].astype(F32)
            return jnp.concatenate(
                [
                    pltpu.roll(packed, jnp.where(top, (128 - 32 * g) % 128, (96 - 32 * g) % 128), 1)
                    for g in range(4)
                ],
                axis=0,
            )

        start = jnp.where(top, 0, 96)
        outer = (lane >= start) & (lane < start + 32)
        middle = (lane >= 32) & (lane < 96)

        def one(h, carry):
            x = src[pl.ds(h, 64, stride=8), :]
            dst[8 * row + h] = jnp.where(outer, halo(row, h), pltpu.roll(x, shift, 1)) * inside
            y = rcv[n, h].astype(F32)
            flank = jnp.concatenate(
                [
                    pltpu.roll(
                        y[32:48], jnp.where(top, (96 - 32 * g) % 128, (128 - 32 * g) % 128), 1
                    )
                    for g in range(4)
                ],
                axis=0,
            )
            dst[8 * (1 - row) + h] = (
                jnp.where(outer, halo(1 - row, h), jnp.where(middle, spread(y[:32]), flank))
                * inside
            )
            return carry

        lax.fori_loop(0, 8, one, 0)

    arrived(0)
    assemble(c_ref, 0, phi_ref)

    zero = jnp.zeros((64, 128), BF)

    def forward(l, carry):
        w = w_ref[l]
        bias = b_s[l]
        z_s[l, 0] = zero
        z_s[l, 17] = zero
        later, last = None, None
        for m in range(8):
            pieces = []
            for h in (2 * m, 2 * m + 1):
                t = jnp.tanh(phi_ref[h]) * inside
                sl_s[l, h] = inside - t * t
                z_s[l, h + 1] = (t * own).astype(BF)
                pieces.append(
                    jnp.concatenate(
                        [
                            pltpu.roll(t, 1, 1).astype(BF),
                            t.astype(BF),
                            pltpu.roll(t, 127, 1).astype(BF),
                        ],
                        axis=0,
                    )
                )
            rhs = jnp.concatenate(pieces, axis=1)
            prod = jnp.dot(w, rhs, preferred_element_type=F32)
            p0, p1 = prod[:, :128], prod[:, 128:]
            if m > 0:
                phi_ref[2 * m - 1] = phi_ref[2 * m - 1] + bias + (later + p0[128:])
                first = last + p0[64:128] + p1[128:]
            else:
                first = p0[64:128] + p1[128:]
            phi_ref[2 * m] = phi_ref[2 * m] + bias + first
            later = p0[:64] + p1[64:128]
            last = p1[:64]
        phi_ref[15] = phi_ref[15] + bias + later
        return carry

    lax.fori_loop(0, blocks, forward, 0)

    def send_pieces(n, field, guess_own, keep):
        gain = gain_own[...] * keep
        shift = jnp.where(top, 32, 96)
        for u in range(8):
            for rho, guess in (
                (row, pltpu.roll(guess_own[pl.ds(u, 64, stride=8), :], shift, 1)),
                (1 - row, spread(rcv[n, u, 0:32, :].astype(F32))),
            ):
                r = field[8 * rho + u] - gain * guess
                p1_snd[n, 8 * rho + u] = jnp.where(
                    lane32 < 64, pltpu.roll(r[:32], 96, 1), pltpu.roll(r[32:], 32, 1)
                ).astype(BF)

        for h in rows_far_first:
            start_unless_here(h, p1_copy(n, h))

        @pl.when(lax.rem(layer, 2) == row)
        def _():
            p1_rcv[n, layer] = p1_snd[n, 8 * row + layer // 2]

    def p2_copy(n, e):
        return remote(
            p2_snd.at[n, e],
            pieces_out.at[n, layer],
            p2_send.at[n],
            p2_recv.at[n],
            {"layer": e},
        )

    def solve(n):
        first = 0 if n == 0 else layers - 1
        stride = 1 if n == 0 else -1

        all_but_own(
            16,
            lambda count: remote(
                p1_snd.at[n, pl.ds(0, count)],
                p1_rcv.at[n, pl.ds(0, count)],
                p1_send.at[n],
                p1_recv.at[n],
                {"row": 1 - row},
            ).wait_recv(),
        )
        state = jnp.zeros((32, 128), F32)
        for k in range(15):
            e = first + stride * k
            state = gain_pk[e] * state + p1_rcv[n, e].astype(F32)
            p2_snd[n, e + stride] = state.astype(BF)
        skipped = 0 if n == 0 else layers - 1

        for e in layers_far_first:

            @pl.when(e != skipped)
            def _():
                p2_copy(n, e).start()

        @pl.when(layer != skipped)
        def _():
            pieces_out[n, layer] = p2_snd[n, layer]

    send_pieces(0, phi_ref, c_ref, jnp.where(layer == 0, 0.0, 1.0))

    all_but_own(
        16,
        lambda count: remote(
            gain_rcv.at[pl.ds(0, count)],
            gain_rcv.at[pl.ds(0, count)],
            gain_send.at[0],
            gain_recv.at[0],
            {"row": 1 - row},
        ).wait_recv(),
    )
    for e in range(16):
        tmp[e : e + 1, :] = gain_rcv[e, 0:1, :]
    turned_all = tmp[...].T
    for e in range(16):
        gain_pk[e] = jnp.where(
            lane32 < 64,
            jnp.broadcast_to(turned_all[0:32, e : e + 1], (32, 128)),
            jnp.broadcast_to(turned_all[32:64, e : e + 1], (32, 128)),
        )

    half = pl.ds(pl.multiple_of(144 * core, 16), 144)
    other_half = pl.ds(pl.multiple_of(144 * (1 - core), 16), 144)
    beside = {"col": col + 1 - 2 * core}

    def ga_copy(l):
        return remote(g_part.at[l, other_half], g_sib.at[l], ga_send.at[l], ga_recv.at[l], beside)

    def at_chip(y):
        return {"row": y // 2, "col": 2 * lax.rem(y, 2) + core}

    def gb_copy(l):
        y = lax.rem(l, 4)
        return remote(
            g_half.at[l],
            g_chip.at[l // 4, chip],
            gb_send.at[l],
            gb_recv.at[l // 4, chip],
            at_chip(y),
        )

    def gc_copy(l, step):
        y = lax.rem(chip + step, 4)
        return remote(
            grad_out.at[l, half],
            grad_out.at[l, half],
            gc_send.at[l // 4, step - 1],
            gc_recv.at[l],
            at_chip(y),
        )

    def gd_copy(l):
        return remote(grad_out.at[l, half], grad_out.at[l, half], gd_send.at[l], gd_recv.at[l], beside)

    def to_owner(l):
        ga_copy(l).wait_recv()
        total = (g_part[l, half, :] + g_sib[l]).astype(BF)

        @pl.when(lax.rem(l, 4) == chip)
        def _():
            g_chip[l // 4, chip] = total

        @pl.when(lax.rem(l, 4) != chip)
        def _():
            g_half[l] = total
            gb_copy(l).start()

    def own_block(q):
        l = 4 * q + chip
        for step in range(1, 4):
            y = lax.rem(chip + step, 4)
            remote(
                g_half.at[l],
                g_chip.at[q, y],
                gb_send.at[l],
                gb_recv.at[q, y],
                at_chip(y),
            ).wait_recv()
        total = g_chip[q, 0].astype(F32) + g_chip[q, 1].astype(F32)
        total = total + g_chip[q, 2].astype(F32) + g_chip[q, 3].astype(F32)
        grad_out[l, half, :] = total.astype(BF)
        for step in range(1, 4):
            gc_copy(l, step).start()

    arrived(1)
    assemble(a_ref, 1, psi_ref)

    def keep_grad(l, grad):
        grad = 0.5 * grad
        g_part[l, 0:192, :] = grad[:, :128]
        g_part[l, 192:288, 0:64] = grad[:96, 128:192]
        g_part[l, 192:288, 64:128] = grad[96:, 128:192]
        ga_copy(l).start()

    def rows_of(l, first, last):
        return jnp.concatenate(
            [
                jnp.concatenate([z_s[l, h], z_s[l, h + 1], z_s[l, h + 2]], axis=0)
                for h in range(first, last)
            ],
            axis=1,
        )

    def backward(step, with_grad):
        l = blocks - 1 - step
        grad = jnp.zeros((192, 192), F32)
        wt = wt_ref[l]
        later, last = None, None
        for m in range(8):
            pieces = []
            for h in (2 * m, 2 * m + 1):
                a = psi_ref[h]
                pieces.append(
                    jnp.concatenate(
                        [
                            pltpu.roll(a, 127, 1).astype(BF),
                            a.astype(BF),
                            pltpu.roll(a, 1, 1).astype(BF),
                        ],
                        axis=0,
                    )
                )
            rhs = jnp.concatenate(pieces, axis=1)
            if with_grad:
                grad = grad + lax.dot_general(
                    rhs,
                    rows_of(l, 2 * m, 2 * m + 2),
                    (((1,), (1,)), ((), ())),
                    preferred_element_type=F32,
                )
            else:
                q_s[l, :, 256 * m : 256 * m + 256] = rhs
            prod = jnp.dot(wt, rhs, preferred_element_type=F32)
            p0, p1 = prod[:, :128], prod[:, 128:]
            if m > 0:
                psi_ref[2 * m - 1] = psi_ref[2 * m - 1] + sl_s[l, 2 * m - 1] * (later + p0[:64])
                first = last + p0[64:128] + p1[:64]
            else:
                first = p0[64:128] + p1[:64]
            psi_ref[2 * m] = psi_ref[2 * m] + sl_s[l, 2 * m] * first
            later = p0[128:] + p1[64:128]
            last = p1[128:]
        psi_ref[15] = psi_ref[15] + sl_s[l, 15] * later
        if with_grad:
            keep_grad(l, grad)

    def sweep_grads(step, carry):
        backward(step, True)

        @pl.when(step >= 2)
        def _():
            to_owner(blocks + 1 - step)

        return carry

    def sweep(step, carry):
        backward(step, False)
        return carry

    lax.fori_loop(0, SPLIT, sweep_grads, 0)
    lax.fori_loop(SPLIT, blocks, sweep, 0)
    send_pieces(1, psi_ref, a_ref, jnp.where(layer == layers - 1, 0.0, 1.0))

    def weight_grads(step, carry):
        l = blocks - 1 - step
        keep_grad(
            l,
            lax.dot_general(
                q_s[l], rows_of(l, 0, 16), (((1,), (1,)), ((), ())), preferred_element_type=F32
            ),
        )

        @pl.when(step >= SPLIT + 1)
        def _():
            to_owner(l + 3)

        @pl.when(step == 5)
        def _():
            solve(0)

        return carry

    lax.fori_loop(SPLIT, blocks, weight_grads, 0)
    for l in (2, 1, 0):
        to_owner(l)
    solve(1)
    own_block(1)
    own_block(0)

    def forward_half(k, carry):
        l = blocks - 1 - k

        @pl.when(lax.rem(l, 4) != chip)
        def _():
            remote(
                grad_out.at[l, half],
                grad_out.at[l, half],
                gc_send.at[0, 0],
                gc_recv.at[l],
                at_chip(lax.rem(l, 4)),
            ).wait_recv()

        gd_copy(l).start()
        return carry

    lax.fori_loop(0, blocks, forward_half, 0)

    for n in range(2):
        for copy in exchange(n):
            copy.wait_send()

    def sent(count):
        remote(
            gain_rcv.at[pl.ds(0, count)],
            gain_rcv.at[pl.ds(0, count)],
            gain_send.at[0],
            gain_recv.at[0],
            {"row": 1 - row},
        ).wait_send()
        for n in range(2):
            remote(
                p1_snd.at[n, pl.ds(0, count)],
                p1_rcv.at[n, pl.ds(0, count)],
                p1_send.at[n],
                p1_recv.at[n],
                {"row": 1 - row},
            ).wait_send()

    all_but_own(16, sent)

    def p2_bytes(n, count):
        return remote(
            p2_snd.at[n, pl.ds(0, count)],
            pieces_out.at[n, pl.ds(0, count)],
            p2_send.at[n],
            p2_recv.at[n],
            {"row": 1 - row},
        )

    for n in range(2):
        skipped = 0 if n == 0 else layers - 1

        @pl.when(layer == skipped)
        def _():
            p2_bytes(n, 15).wait_send()

        @pl.when(layer != skipped)
        def _():
            p2_bytes(n, 14).wait_send()
            p2_bytes(n, 15).wait_recv()

    def drain_grads(l, carry):
        ga_copy(l).wait_send()

        @pl.when(lax.rem(l, 4) != chip)
        def _():
            gb_copy(l).wait_send()

        gd_copy(l).wait_send()
        remote(
            grad_out.at[l, other_half],
            grad_out.at[l, other_half],
            gd_send.at[l],
            gd_recv.at[l],
            beside,
        ).wait_recv()
        return carry

    lax.fori_loop(0, blocks, drain_grads, 0)
    for q in range(2):
        for step in range(1, 4):
            gc_copy(4 * q + chip, step).wait_send()


def fused(c, a, w, b, gain):
    blocks = w.shape[0]
    vm = pltpu.VMEM
    dma = pltpu.SemaphoreType.DMA
    return pl.pallas_call(
        fused_kernel,
        out_shape=(
            jax.ShapeDtypeStruct((2, 16, 32, 128), BF),
            jax.ShapeDtypeStruct((blocks, 288, 128), BF),
        ),
        in_specs=[pl.BlockSpec(memory_space=pltpu.HBM)] * 5,
        out_specs=[pl.BlockSpec(memory_space=vm)] * 2,
        scratch_shapes=[
            vm((2, 8, 48, 128), BF),
            vm((2, 8, 48, 128), BF),
            vm((2, 2, 8, 16, 128), BF),
            vm((2, 2, 8, 16, 128), BF),
            vm((128, 128), F32),
            vm((8, 128), F32),
            vm((16, 8, 128), F32),
            vm((16, 32, 128), F32),
            vm((64, 128), F32),
            vm((blocks, 192, 192), BF),
            vm((blocks, 192, 192), BF),
            vm((blocks, 64, 128), F32),
            vm((16, 64, 128), F32),
            vm((16, 64, 128), F32),
            vm((blocks, 18, 64, 128), BF),
            vm((blocks, 16, 64, 128), F32),
            vm((2, 16, 32, 128), BF),
            vm((2, 16, 32, 128), BF),
            vm((2, 16, 32, 128), BF),
            vm((blocks, 288, 128), F32),
            vm((blocks, 144, 128), F32),
            vm((blocks, 144, 128), BF),
            vm((2, 4, 144, 128), BF),
            dma((2, 3)),
            dma((2, 3)),
            dma((1,)),
            dma((1,)),
            dma((2,)),
            dma((2,)),
            dma((2,)),
            dma((2,)),
            dma((blocks,)),
            dma((blocks,)),
            dma((blocks,)),
            dma((2, 4)),
            dma((2, 3)),
            dma((blocks,)),
            dma((blocks,)),
            dma((blocks,)),
            vm(c.shape, F32),
            vm(a.shape, F32),
            vm(w.shape, BF),
            vm(b.shape, F32),
            vm(gain.shape, F32),
            dma((5,)),
            vm((blocks, 192, 2048), BF),
        ],
        compiler_params=pltpu.CompilerParams(
            vmem_limit_bytes=48 << 20, collective_id=0, has_side_effects=True
        ),
    )(c, a, w, b, gain)


def unpack_kernel(c_ref, a_ref, pieces_ref, grad_ref, c_out, a_out, g_out, c_s, a_s, g_s, sem):
    layer = lax.axis_index("layer")
    layers = lax.axis_size("layer")
    blocks = grad_ref.shape[0]
    lane32 = lax.broadcasted_iota(jnp.int32, (32, 128), 1)

    for n, whole, part, skipped in ((0, c_ref, c_s, 0), (1, a_ref, a_s, layers - 1)):

        @pl.when(layer == skipped)
        def _():
            pltpu.make_async_copy(whole, part, sem.at[blocks + 2 + n]).start()

    def states(n, whole, part, out, skipped):
        @pl.when(layer == skipped)
        def _():
            pltpu.make_async_copy(whole, part, sem.at[blocks + 2 + n]).wait()

        @pl.when(layer != skipped)
        def _():
            for u in range(8):
                left = pieces_ref[n, 2 * u].astype(F32)
                right = pieces_ref[n, 2 * u + 1].astype(F32)
                part[pl.ds(u, 32, stride=8), :] = jnp.where(
                    lane32 < 64, left, pltpu.roll(right, 64, 1)
                )
                part[pl.ds(256 + u, 32, stride=8), :] = jnp.where(
                    lane32 < 64, pltpu.roll(left, 64, 1), right
                )
        pltpu.make_async_copy(part, out, sem.at[blocks + n]).start()

    def one(l, carry):
        for j in range(3):
            g_s[l, j] = grad_ref[l, 64 * j : 64 * j + 64, 0:64].astype(F32)
            g_s[l, 3 + j] = grad_ref[l, 64 * j : 64 * j + 64, 64:128].astype(F32)
        g_s[l, 6] = grad_ref[l, 192:256, 0:64].astype(F32)
        g_s[l, 7, 0:32] = grad_ref[l, 256:288, 0:64].astype(F32)
        g_s[l, 7, 32:64] = grad_ref[l, 192:224, 64:128].astype(F32)
        g_s[l, 8] = grad_ref[l, 224:288, 64:128].astype(F32)
        pltpu.make_async_copy(g_s.at[l], g_out.at[l], sem.at[l]).start()
        return carry

    lax.fori_loop(0, blocks, one, 0)
    states(0, c_ref, c_s, c_out, 0)
    states(1, a_ref, a_s, a_out, layers - 1)
    for l in range(blocks):
        pltpu.make_async_copy(g_s.at[l], g_out.at[l], sem.at[l]).wait()
    pltpu.make_async_copy(c_s, c_out, sem.at[blocks]).wait()
    pltpu.make_async_copy(a_s, a_out, sem.at[blocks + 1]).wait()


def unpack(c, a, pieces, grad):
    blocks = grad.shape[0]
    vm = pltpu.VMEM
    far = pl.BlockSpec(memory_space=pltpu.HBM)
    return pl.pallas_call(
        unpack_kernel,
        out_shape=(
            jax.ShapeDtypeStruct((512, 128), F32),
            jax.ShapeDtypeStruct((512, 128), F32),
            jax.ShapeDtypeStruct((blocks, 9, 64, 64), F32),
        ),
        in_specs=[far, far, pl.BlockSpec(memory_space=vm), pl.BlockSpec(memory_space=vm)],
        out_specs=[far] * 3,
        scratch_shapes=[
            vm((512, 128), F32),
            vm((512, 128), F32),
            vm((blocks, 9, 64, 64), F32),
            pltpu.SemaphoreType.DMA((blocks + 4,)),
        ],
        compiler_params=pltpu.CompilerParams(vmem_limit_bytes=32 << 20),
    )(c, a, pieces, grad)


def local(c_guess, adjoint_guess, weights, biases, coarse_gain):
    c = c_guess.reshape(512, 128)
    a = adjoint_guess.reshape(512, 128)
    far = [
        pltpu.with_memory_space_constraint(x, pltpu.HBM)
        for x in (c, a, weights, biases, coarse_gain)
    ]
    pieces, grad = fused(*far)
    c_states, ends, weight_grad = unpack(far[0], far[1], pieces, grad)
    return (c_states.reshape(c_guess.shape), ends.reshape(c_guess.shape), weight_grad)


def solution(mesh):
    in_specs = (
        P("layer", None, None, "row", "col"),
        P("layer", None, None, "row", "col"),
        P("layer", None, None, None),
        P("layer", None),
        P("layer", None),
    )
    out_specs = (
        P("layer", None, None, "row", "col"),
        P("layer", None, None, "row", "col"),
        P("layer", None, None, None),
    )
    return jax.shard_map(local, mesh=mesh, in_specs=in_specs, out_specs=out_specs, check_vma=False)
```

```python
import jax
import jax.numpy as jnp
from jax import lax
from jax.experimental import pallas as pl
from jax.experimental.pallas import tpu as pltpu
from jax.sharding import PartitionSpec as P

HALO = 32
OWN = 64
SPLIT = 4
BF = jnp.bfloat16
F32 = jnp.float32
MESH = pl.DeviceIdType.MESH


def remote(src, dst, send, recv, where):
    return pltpu.make_async_remote_copy(
        src_ref=src,
        dst_ref=dst,
        send_sem=send,
        recv_sem=recv,
        device_id=where,
        device_id_type=MESH,
    )


def fused_kernel(
    c_hbm,
    a_hbm,
    w_hbm,
    b_hbm,
    gain_hbm,
    pieces_out,
    grad_out,
    snd,
    rcv,
    edge_snd,
    edge_rcv,
    tmp,
    gain_snd,
    gain_rcv,
    gain_pk,
    gain_own,
    w_ref,
    wt_ref,
    b_s,
    phi_ref,
    psi_ref,
    z_s,
    sl_s,
    p1_snd,
    p1_rcv,
    p2_snd,
    g_part,
    g_sib,
    g_half,
    g_chip,
    in_send,
    in_recv,
    gain_send,
    gain_recv,
    p1_send,
    p1_recv,
    p2_send,
    p2_recv,
    ga_send,
    ga_recv,
    gb_send,
    gb_recv,
    gc_send,
    gc_recv,
    gd_send,
    gd_recv,
    c_ref,
    a_ref,
    w_in,
    b_ref,
    gain_ref,
    load_sem,
    q_s,
):
    blocks = w_in.shape[0]
    layer = lax.axis_index("layer")
    row = lax.axis_index("row")
    col = lax.axis_index("col")
    layers = lax.axis_size("layer")
    cols = lax.axis_size("col")
    core = lax.rem(col, 2)
    chip = 2 * row + col // 2
    strip = 2 * col + row
    lane = lax.broadcasted_iota(jnp.int32, (64, 128), 1)
    lane32 = lax.broadcasted_iota(jnp.int32, (32, 128), 1)
    lane16 = lax.broadcasted_iota(jnp.int32, (16, 128), 1)
    column = strip * OWN - HALO + lane
    inside = jnp.where((column >= 0) & (column < 2 * cols * OWN), 1.0, 0.0).astype(F32)
    own = jnp.where((lane >= HALO) & (lane < HALO + OWN), 1.0, 0.0).astype(F32)
    top = row == 0

    loads = [
        pltpu.make_async_copy(src, dst, load_sem.at[n])
        for n, (src, dst) in enumerate(
            (
                (c_hbm, c_ref),
                (a_hbm, a_ref),
                (w_hbm, w_in),
                (b_hbm, b_ref),
                (gain_hbm, gain_ref),
            )
        )
    ]
    for load in loads:
        load.start()

    barrier = pltpu.get_barrier_semaphore()

    pl.semaphore_signal(barrier, inc=1, device_id={"row": 1 - row}, device_id_type=MESH)
    for step in range(1, cols):
        for rho in range(2):
            pl.semaphore_signal(
                barrier,
                inc=1,
                device_id={"row": rho, "col": lax.rem(col + step, cols)},
                device_id_type=MESH,
            )
    for step in range(1, layers):
        for rho in range(2):
            pl.semaphore_signal(
                barrier,
                inc=1,
                device_id={"layer": lax.rem(layer + step, layers), "row": rho},
                device_id_type=MESH,
            )

    def pack(src, n):
        def one(h, carry):
            x = src[pl.ds(h, 64, stride=8), :]
            turned_by = jnp.where(top, 64, 0)
            middle = jnp.where(
                lane32 < 64,
                pltpu.roll(x[:32], turned_by, 1),
                pltpu.roll(x[32:], 64 - turned_by, 1),
            )
            flank = jnp.zeros((16, 128), F32)
            for g in range(4):
                part = pltpu.roll(
                    x[16 * g : 16 * g + 16],
                    jnp.where(top, (32 * g + 96) % 128, (32 * g + 64) % 128),
                    1,
                )
                flank = jnp.where(lane16 // 32 == g, part, flank)
            snd[n, h] = jnp.concatenate([middle, flank], axis=0).astype(BF)
            for side in range(2):
                edge = jnp.zeros((16, 128), F32)
                for g in range(4):
                    part = x[16 * g : 16 * g + 16]
                    shift = (32 * g + (32 if side == 0 else 0)) % 128
                    if shift:
                        part = pltpu.roll(part, shift, 1)
                    edge = jnp.where(lane16 // 32 == g, part, edge)
                edge_snd[side, n, h] = edge.astype(BF)
            return carry

        lax.fori_loop(0, 8, one, 0)

    def exchange(n):
        yield remote(snd.at[n], rcv.at[n], in_send.at[n, 0], in_recv.at[n, 0], {"row": 1 - row})
        yield remote(
            edge_snd.at[0, n],
            edge_rcv.at[row, n],
            in_send.at[n, 1],
            in_recv.at[n, 1 + row],
            {"row": 0, "col": lax.rem(col + 1, cols)},
        )
        yield remote(
            edge_snd.at[1, n],
            edge_rcv.at[row, n],
            in_send.at[n, 2],
            in_recv.at[n, 1 + row],
            {"row": 1, "col": lax.rem(col + cols - 1, cols)},
        )

    def arrived(n):
        remote(snd.at[n], rcv.at[n], in_send.at[n, 0], in_recv.at[n, 0], {"row": 1 - row}).wait_recv()
        for rho in range(2):
            remote(
                edge_snd.at[0, n],
                edge_rcv.at[rho, n],
                in_send.at[n, 1],
                in_recv.at[n, 1 + rho],
                {"row": 1 - row},
            ).wait_recv()

    loads[0].wait()
    pack(c_ref, 0)
    pl.semaphore_wait(barrier, 2 * layers - 1 + 2 * (cols - 1))
    for copy in exchange(0):
        copy.start()
    loads[1].wait()
    pack(a_ref, 1)
    for copy in exchange(1):
        copy.start()

    def lay_weights(l, carry):
        for i in range(3):
            w_ref[l, 64 * i : 64 * i + 64, :] = jnp.concatenate(
                [w_in[l, 3 * i + j] * jnp.asarray(0.5, BF) for j in range(3)], axis=1
            )
            stack = w_in[l, 3 * i : 3 * i + 3].reshape(192, 64)
            wt_ref[l, 64 * i : 64 * i + 64, :] = (0.5 * stack.astype(F32)).T.astype(BF)
        return carry

    for load in loads[2:]:
        load.wait()
    lax.fori_loop(0, blocks, lay_weights, 0)
    tmp[...] = jnp.zeros_like(tmp)
    tmp[0:blocks, 0:64] = 0.5 * b_ref[...]
    tmp[blocks : blocks + 1, 0:64] = gain_ref[...]
    turned = tmp[...].T
    for l in range(blocks):
        b_s[l] = jnp.broadcast_to(turned[0:64, l : l + 1], (64, 128))
    gain_own[...] = jnp.broadcast_to(turned[0:64, blocks : blocks + 1], (64, 128))
    gain_snd[...] = tmp[blocks : blocks + 8, :]

    def holder(h):
        return 2 * lax.rem(h, 8) + row, h // 8

    rows_far_first = [
        8 * rho + lax.rem(layer // 2 + k, 8) for rho in (1 - row, row) for k in (5, 3, 4, 6, 2, 7, 1, 0)
    ]
    layers_far_first = [
        4 * lax.rem(layer // 4 + dx, 4) + lax.rem(layer + dz, 4)
        for dx, dz in (
            (2, 2), (2, 1), (2, 3), (1, 2), (3, 2), (1, 1), (3, 3), (1, 3), (3, 1),
            (2, 0), (0, 2), (1, 0), (3, 0), (0, 1), (0, 3),
        )
    ]

    def all_but_own(count, wait):
        for own_piece in (True, False):

            @pl.when((lax.rem(layer, 2) == row) == own_piece)
            def _():
                wait(count - 1 if own_piece else count)

    def stays(h):
        lam, rho = holder(h)
        return jnp.logical_and(lam == layer, rho == row)

    def gain_copy(h):
        lam, rho = holder(h)
        return remote(
            gain_snd,
            gain_rcv.at[layer],
            gain_send.at[0],
            gain_recv.at[0],
            {"layer": lam, "row": rho},
        )

    def p1_copy(n, h):
        lam, rho = holder(h)
        return remote(
            p1_snd.at[n, h],
            p1_rcv.at[n, layer],
            p1_send.at[n],
            p1_recv.at[n],
            {"layer": lam, "row": rho},
        )

    def start_unless_here(h, copy):
        @pl.when(jnp.logical_not(stays(h)))
        def _():
            copy.start()

    for h in rows_far_first:
        start_unless_here(h, gain_copy(h))

    @pl.when(lax.rem(layer, 2) == row)
    def _():
        gain_rcv[layer] = gain_snd[...]

    def spread(packed):
        return jnp.concatenate([pltpu.roll(packed, 32, 1), pltpu.roll(packed, 96, 1)], axis=0)

    def assemble(src, n, dst):
        shift = jnp.where(top, 32, 96)

        def halo(rho, h):
            packed = edge_rcv[rho, n, h].astype(F32)
            return jnp.concatenate(
                [
                    pltpu.roll(packed, jnp.where(top, (128 - 32 * g) % 128, (96 - 32 * g) % 128), 1)
                    for g in range(4)
                ],
                axis=0,
            )

        start = jnp.where(top, 0, 96)
        outer = (lane >= start) & (lane < start + 32)
        middle = (lane >= 32) & (lane < 96)

        def one(h, carry):
            x = src[pl.ds(h, 64, stride=8), :]
            dst[8 * row + h] = jnp.where(outer, halo(row, h), pltpu.roll(x, shift, 1)) * inside
            y = rcv[n, h].astype(F32)
            flank = jnp.concatenate(
                [
                    pltpu.roll(
                        y[32:48], jnp.where(top, (96 - 32 * g) % 128, (128 - 32 * g) % 128), 1
                    )
                    for g in range(4)
                ],
                axis=0,
            )
            dst[8 * (1 - row) + h] = (
                jnp.where(outer, halo(1 - row, h), jnp.where(middle, spread(y[:32]), flank))
                * inside
            )
            return carry

        lax.fori_loop(0, 8, one, 0)

    arrived(0)
    assemble(c_ref, 0, phi_ref)

    zero = jnp.zeros((64, 128), BF)

    def forward(l, carry):
        w = w_ref[l]
        bias = b_s[l]
        z_s[l, 0] = zero
        z_s[l, 17] = zero
        later, last = None, None
        for m in range(8):
            pieces = []
            for h in (2 * m, 2 * m + 1):
                t = jnp.tanh(phi_ref[h]) * inside
                sl_s[l, h] = inside - t * t
                z_s[l, h + 1] = (t * own).astype(BF)
                pieces.append(
                    jnp.concatenate(
                        [
                            pltpu.roll(t, 1, 1).astype(BF),
                            t.astype(BF),
                            pltpu.roll(t, 127, 1).astype(BF),
                        ],
                        axis=0,
                    )
                )
            rhs = jnp.concatenate(pieces, axis=1)
            prod = jnp.dot(w, rhs, preferred_element_type=F32)
            p0, p1 = prod[:, :128], prod[:, 128:]
            if m > 0:
                phi_ref[2 * m - 1] = phi_ref[2 * m - 1] + bias + (later + p0[128:])
                first = last + p0[64:128] + p1[128:]
            else:
                first = p0[64:128] + p1[128:]
            phi_ref[2 * m] = phi_ref[2 * m] + bias + first
            later = p0[:64] + p1[64:128]
            last = p1[:64]
        phi_ref[15] = phi_ref[15] + bias + later
        return carry

    lax.fori_loop(0, blocks, forward, 0)

    def send_pieces(n, field, guess_own, keep):
        gain = gain_own[...] * keep
        shift = jnp.where(top, 32, 96)
        for u in range(8):
            for rho, guess in (
                (row, pltpu.roll(guess_own[pl.ds(u, 64, stride=8), :], shift, 1)),
                (1 - row, spread(rcv[n, u, 0:32, :].astype(F32))),
            ):
                r = field[8 * rho + u] - gain * guess
                p1_snd[n, 8 * rho + u] = jnp.where(
                    lane32 < 64, pltpu.roll(r[:32], 96, 1), pltpu.roll(r[32:], 32, 1)
                ).astype(BF)

        for h in rows_far_first:
            start_unless_here(h, p1_copy(n, h))

        @pl.when(lax.rem(layer, 2) == row)
        def _():
            p1_rcv[n, layer] = p1_snd[n, 8 * row + layer // 2]

    def p2_copy(n, e):
        return remote(
            p2_snd.at[n, e],
            pieces_out.at[n, layer],
            p2_send.at[n],
            p2_recv.at[n],
            {"layer": e},
        )

    def solve(n):
        first = 0 if n == 0 else layers - 1
        stride = 1 if n == 0 else -1

        all_but_own(
            16,
            lambda count: remote(
                p1_snd.at[n, pl.ds(0, count)],
                p1_rcv.at[n, pl.ds(0, count)],
                p1_send.at[n],
                p1_recv.at[n],
                {"row": 1 - row},
            ).wait_recv(),
        )
        state = jnp.zeros((32, 128), F32)
        for k in range(15):
            e = first + stride * k
            state = gain_pk[e] * state + p1_rcv[n, e].astype(F32)
            p2_snd[n, e + stride] = state.astype(BF)
        skipped = 0 if n == 0 else layers - 1

        for e in layers_far_first:

            @pl.when(e != skipped)
            def _():
                p2_copy(n, e).start()

        @pl.when(layer != skipped)
        def _():
            pieces_out[n, layer] = p2_snd[n, layer]

    send_pieces(0, phi_ref, c_ref, jnp.where(layer == 0, 0.0, 1.0))

    all_but_own(
        16,
        lambda count: remote(
            gain_rcv.at[pl.ds(0, count)],
            gain_rcv.at[pl.ds(0, count)],
            gain_send.at[0],
            gain_recv.at[0],
            {"row": 1 - row},
        ).wait_recv(),
    )
    for e in range(16):
        tmp[e : e + 1, :] = gain_rcv[e, 0:1, :]
    turned_all = tmp[...].T
    for e in range(16):
        gain_pk[e] = jnp.where(
            lane32 < 64,
            jnp.broadcast_to(turned_all[0:32, e : e + 1], (32, 128)),
            jnp.broadcast_to(turned_all[32:64, e : e + 1], (32, 128)),
        )

    half = pl.ds(pl.multiple_of(144 * core, 16), 144)
    other_half = pl.ds(pl.multiple_of(144 * (1 - core), 16), 144)
    beside = {"col": col + 1 - 2 * core}

    def ga_copy(l):
        return remote(g_part.at[l, other_half], g_sib.at[l], ga_send.at[l], ga_recv.at[l], beside)

    def at_chip(y):
        return {"row": y // 2, "col": 2 * lax.rem(y, 2) + core}

    def gb_copy(l):
        y = lax.rem(l, 4)
        return remote(
            g_half.at[l],
            g_chip.at[l // 4, chip],
            gb_send.at[l],
            gb_recv.at[l // 4, chip],
            at_chip(y),
        )

    def gc_copy(l, step):
        y = lax.rem(chip + step, 4)
        return remote(
            grad_out.at[l, half],
            grad_out.at[l, half],
            gc_send.at[l // 4, step - 1],
            gc_recv.at[l],
            at_chip(y),
        )

    def gd_copy(l):
        return remote(grad_out.at[l, half], grad_out.at[l, half], gd_send.at[l], gd_recv.at[l], beside)

    def to_owner(l):
        ga_copy(l).wait_recv()
        total = (g_part[l, half, :] + g_sib[l]).astype(BF)

        @pl.when(lax.rem(l, 4) == chip)
        def _():
            g_chip[l // 4, chip] = total

        @pl.when(lax.rem(l, 4) != chip)
        def _():
            g_half[l] = total
            gb_copy(l).start()

    def own_block(q):
        l = 4 * q + chip
        for step in range(1, 4):
            y = lax.rem(chip + step, 4)
            remote(
                g_half.at[l],
                g_chip.at[q, y],
                gb_send.at[l],
                gb_recv.at[q, y],
                at_chip(y),
            ).wait_recv()
        total = g_chip[q, 0].astype(F32) + g_chip[q, 1].astype(F32)
        total = total + g_chip[q, 2].astype(F32) + g_chip[q, 3].astype(F32)
        grad_out[l, half, :] = total.astype(BF)
        for step in range(1, 4):
            gc_copy(l, step).start()

    arrived(1)
    assemble(a_ref, 1, psi_ref)

    def keep_grad(l, grad):
        grad = 0.5 * grad
        g_part[l, 0:192, :] = grad[:, :128]
        g_part[l, 192:288, 0:64] = grad[:96, 128:192]
        g_part[l, 192:288, 64:128] = grad[96:, 128:192]
        ga_copy(l).start()

    def rows_of(l, first, last):
        return jnp.concatenate(
            [
                jnp.concatenate([z_s[l, h], z_s[l, h + 1], z_s[l, h + 2]], axis=0)
                for h in range(first, last)
            ],
            axis=1,
        )

    def backward(step, with_grad):
        l = blocks - 1 - step
        grad = jnp.zeros((192, 192), F32)
        wt = wt_ref[l]
        later, last = None, None
        for m in range(8):
            pieces = []
            for h in (2 * m, 2 * m + 1):
                a = psi_ref[h]
                pieces.append(
                    jnp.concatenate(
                        [
                            pltpu.roll(a, 127, 1).astype(BF),
                            a.astype(BF),
                            pltpu.roll(a, 1, 1).astype(BF),
                        ],
                        axis=0,
                    )
                )
            rhs = jnp.concatenate(pieces, axis=1)
            if with_grad:
                grad = grad + lax.dot_general(
                    rhs,
                    rows_of(l, 2 * m, 2 * m + 2),
                    (((1,), (1,)), ((), ())),
                    preferred_element_type=F32,
                )
            else:
                q_s[l, :, 256 * m : 256 * m + 256] = rhs
            prod = jnp.dot(wt, rhs, preferred_element_type=F32)
            p0, p1 = prod[:, :128], prod[:, 128:]
            if m > 0:
                psi_ref[2 * m - 1] = psi_ref[2 * m - 1] + sl_s[l, 2 * m - 1] * (later + p0[:64])
                first = last + p0[64:128] + p1[:64]
            else:
                first = p0[64:128] + p1[:64]
            psi_ref[2 * m] = psi_ref[2 * m] + sl_s[l, 2 * m] * first
            later = p0[128:] + p1[64:128]
            last = p1[128:]
        psi_ref[15] = psi_ref[15] + sl_s[l, 15] * later
        if with_grad:
            keep_grad(l, grad)

    def sweep_grads(step, carry):
        backward(step, True)

        @pl.when(step >= 2)
        def _():
            to_owner(blocks + 1 - step)

        return carry

    def sweep(step, carry):
        backward(step, False)
        return carry

    lax.fori_loop(0, SPLIT, sweep_grads, 0)
    lax.fori_loop(SPLIT, blocks, sweep, 0)
    send_pieces(1, psi_ref, a_ref, jnp.where(layer == layers - 1, 0.0, 1.0))

    def weight_grads(step, carry):
        l = blocks - 1 - step
        keep_grad(
            l,
            lax.dot_general(
                q_s[l], rows_of(l, 0, 16), (((1,), (1,)), ((), ())), preferred_element_type=F32
            ),
        )

        @pl.when(step >= SPLIT)
        def _():
            to_owner(l + 2)

        @pl.when(step == 5)
        def _():
            solve(0)

        return carry

    lax.fori_loop(SPLIT, blocks, weight_grads, 0)
    for l in (1, 0):
        to_owner(l)
    solve(1)
    own_block(1)
    own_block(0)

    def forward_half(k, carry):
        l = blocks - 1 - k

        @pl.when(lax.rem(l, 4) != chip)
        def _():
            remote(
                grad_out.at[l, half],
                grad_out.at[l, half],
                gc_send.at[0, 0],
                gc_recv.at[l],
                at_chip(lax.rem(l, 4)),
            ).wait_recv()

        gd_copy(l).start()
        return carry

    for n in range(2):
        for copy in exchange(n):
            copy.wait_send()

    def sent(count):
        remote(
            gain_rcv.at[pl.ds(0, count)],
            gain_rcv.at[pl.ds(0, count)],
            gain_send.at[0],
            gain_recv.at[0],
            {"row": 1 - row},
        ).wait_send()
        for n in range(2):
            remote(
                p1_snd.at[n, pl.ds(0, count)],
                p1_rcv.at[n, pl.ds(0, count)],
                p1_send.at[n],
                p1_recv.at[n],
                {"row": 1 - row},
            ).wait_send()

    all_but_own(16, sent)

    def drain_parts(l, carry):
        ga_copy(l).wait_send()

        @pl.when(lax.rem(l, 4) != chip)
        def _():
            gb_copy(l).wait_send()

        return carry

    lax.fori_loop(0, blocks, drain_parts, 0)
    lax.fori_loop(0, blocks, forward_half, 0)

    def p2_bytes(n, count):
        return remote(
            p2_snd.at[n, pl.ds(0, count)],
            pieces_out.at[n, pl.ds(0, count)],
            p2_send.at[n],
            p2_recv.at[n],
            {"row": 1 - row},
        )

    for n in range(2):
        skipped = 0 if n == 0 else layers - 1

        @pl.when(layer == skipped)
        def _():
            p2_bytes(n, 15).wait_send()

        @pl.when(layer != skipped)
        def _():
            p2_bytes(n, 14).wait_send()
            p2_bytes(n, 15).wait_recv()

    def drain_grads(l, carry):
        gd_copy(l).wait_send()
        remote(
            grad_out.at[l, other_half],
            grad_out.at[l, other_half],
            gd_send.at[l],
            gd_recv.at[l],
            beside,
        ).wait_recv()
        return carry

    lax.fori_loop(0, blocks, drain_grads, 0)
    for q in range(2):
        for step in range(1, 4):
            gc_copy(4 * q + chip, step).wait_send()


def fused(c, a, w, b, gain):
    blocks = w.shape[0]
    vm = pltpu.VMEM
    dma = pltpu.SemaphoreType.DMA
    return pl.pallas_call(
        fused_kernel,
        out_shape=(
            jax.ShapeDtypeStruct((2, 16, 32, 128), BF),
            jax.ShapeDtypeStruct((blocks, 288, 128), BF),
        ),
        in_specs=[pl.BlockSpec(memory_space=pltpu.HBM)] * 5,
        out_specs=[pl.BlockSpec(memory_space=vm)] * 2,
        scratch_shapes=[
            vm((2, 8, 48, 128), BF),
            vm((2, 8, 48, 128), BF),
            vm((2, 2, 8, 16, 128), BF),
            vm((2, 2, 8, 16, 128), BF),
            vm((128, 128), F32),
            vm((8, 128), F32),
            vm((16, 8, 128), F32),
            vm((16, 32, 128), F32),
            vm((64, 128), F32),
            vm((blocks, 192, 192), BF),
            vm((blocks, 192, 192), BF),
            vm((blocks, 64, 128), F32),
            vm((16, 64, 128), F32),
            vm((16, 64, 128), F32),
            vm((blocks, 18, 64, 128), BF),
            vm((blocks, 16, 64, 128), F32),
            vm((2, 16, 32, 128), BF),
            vm((2, 16, 32, 128), BF),
            vm((2, 16, 32, 128), BF),
            vm((blocks, 288, 128), F32),
            vm((blocks, 144, 128), F32),
            vm((blocks, 144, 128), BF),
            vm((2, 4, 144, 128), BF),
            dma((2, 3)),
            dma((2, 3)),
            dma((1,)),
            dma((1,)),
            dma((2,)),
            dma((2,)),
            dma((2,)),
            dma((2,)),
            dma((blocks,)),
            dma((blocks,)),
            dma((blocks,)),
            dma((2, 4)),
            dma((2, 3)),
            dma((blocks,)),
            dma((blocks,)),
            dma((blocks,)),
            vm(c.shape, F32),
            vm(a.shape, F32),
            vm(w.shape, BF),
            vm(b.shape, F32),
            vm(gain.shape, F32),
            dma((5,)),
            vm((blocks, 192, 2048), BF),
        ],
        compiler_params=pltpu.CompilerParams(
            vmem_limit_bytes=48 << 20, collective_id=0, has_side_effects=True
        ),
    )(c, a, w, b, gain)


def unpack_kernel(c_ref, a_ref, pieces_ref, grad_ref, c_out, a_out, g_out, c_s, a_s, g_s, sem):
    layer = lax.axis_index("layer")
    layers = lax.axis_size("layer")
    blocks = grad_ref.shape[0]
    lane32 = lax.broadcasted_iota(jnp.int32, (32, 128), 1)

    for n, whole, part, skipped in ((0, c_ref, c_s, 0), (1, a_ref, a_s, layers - 1)):

        @pl.when(layer == skipped)
        def _():
            pltpu.make_async_copy(whole, part, sem.at[blocks + 2 + n]).start()

    def states(n, whole, part, out, skipped):
        @pl.when(layer == skipped)
        def _():
            pltpu.make_async_copy(whole, part, sem.at[blocks + 2 + n]).wait()

        @pl.when(layer != skipped)
        def _():
            for u in range(8):
                left = pieces_ref[n, 2 * u].astype(F32)
                right = pieces_ref[n, 2 * u + 1].astype(F32)
                part[pl.ds(u, 32, stride=8), :] = jnp.where(
                    lane32 < 64, left, pltpu.roll(right, 64, 1)
                )
                part[pl.ds(256 + u, 32, stride=8), :] = jnp.where(
                    lane32 < 64, pltpu.roll(left, 64, 1), right
                )
        pltpu.make_async_copy(part, out, sem.at[blocks + n]).start()

    def one(l, carry):
        for j in range(3):
            g_s[l, j] = grad_ref[l, 64 * j : 64 * j + 64, 0:64].astype(F32)
            g_s[l, 3 + j] = grad_ref[l, 64 * j : 64 * j + 64, 64:128].astype(F32)
        g_s[l, 6] = grad_ref[l, 192:256, 0:64].astype(F32)
        g_s[l, 7, 0:32] = grad_ref[l, 256:288, 0:64].astype(F32)
        g_s[l, 7, 32:64] = grad_ref[l, 192:224, 64:128].astype(F32)
        g_s[l, 8] = grad_ref[l, 224:288, 64:128].astype(F32)
        pltpu.make_async_copy(g_s.at[l], g_out.at[l], sem.at[l]).start()
        return carry

    lax.fori_loop(0, blocks, one, 0)
    states(0, c_ref, c_s, c_out, 0)
    states(1, a_ref, a_s, a_out, layers - 1)
    for l in range(blocks):
        pltpu.make_async_copy(g_s.at[l], g_out.at[l], sem.at[l]).wait()
    pltpu.make_async_copy(c_s, c_out, sem.at[blocks]).wait()
    pltpu.make_async_copy(a_s, a_out, sem.at[blocks + 1]).wait()


def unpack(c, a, pieces, grad):
    blocks = grad.shape[0]
    vm = pltpu.VMEM
    far = pl.BlockSpec(memory_space=pltpu.HBM)
    return pl.pallas_call(
        unpack_kernel,
        out_shape=(
            jax.ShapeDtypeStruct((512, 128), F32),
            jax.ShapeDtypeStruct((512, 128), F32),
            jax.ShapeDtypeStruct((blocks, 9, 64, 64), F32),
        ),
        in_specs=[far, far, pl.BlockSpec(memory_space=vm), pl.BlockSpec(memory_space=vm)],
        out_specs=[far] * 3,
        scratch_shapes=[
            vm((512, 128), F32),
            vm((512, 128), F32),
            vm((blocks, 9, 64, 64), F32),
            pltpu.SemaphoreType.DMA((blocks + 4,)),
        ],
        compiler_params=pltpu.CompilerParams(vmem_limit_bytes=32 << 20),
    )(c, a, pieces, grad)


def local(c_guess, adjoint_guess, weights, biases, coarse_gain):
    c = c_guess.reshape(512, 128)
    a = adjoint_guess.reshape(512, 128)
    far = [
        pltpu.with_memory_space_constraint(x, pltpu.HBM)
        for x in (c, a, weights, biases, coarse_gain)
    ]
    pieces, grad = fused(*far)
    c_states, ends, weight_grad = unpack(far[0], far[1], pieces, grad)
    return (c_states.reshape(c_guess.shape), ends.reshape(c_guess.shape), weight_grad)


def solution(mesh):
    in_specs = (
        P("layer", None, None, "row", "col"),
        P("layer", None, None, "row", "col"),
        P("layer", None, None, None),
        P("layer", None),
        P("layer", None),
    )
    out_specs = (
        P("layer", None, None, "row", "col"),
        P("layer", None, None, "row", "col"),
        P("layer", None, None, None),
    )
    return jax.shard_map(local, mesh=mesh, in_specs=in_specs, out_specs=out_specs, check_vma=False)
```

```python
import jax
import jax.numpy as jnp
from jax import lax
from jax.experimental import pallas as pl
from jax.experimental.pallas import tpu as pltpu
from jax.sharding import PartitionSpec as P

HALO = 32
OWN = 64
SPLIT = 4
BF = jnp.bfloat16
F32 = jnp.float32
MESH = pl.DeviceIdType.MESH


def remote(src, dst, send, recv, where):
    return pltpu.make_async_remote_copy(
        src_ref=src,
        dst_ref=dst,
        send_sem=send,
        recv_sem=recv,
        device_id=where,
        device_id_type=MESH,
    )


def fused_kernel(
    c_hbm,
    a_hbm,
    w_hbm,
    b_hbm,
    gain_hbm,
    pieces_out,
    grad_out,
    snd,
    rcv,
    edge_snd,
    edge_rcv,
    tmp,
    gain_snd,
    gain_rcv,
    gain_pk,
    gain_own,
    w_ref,
    wt_ref,
    b_s,
    phi_ref,
    psi_ref,
    z_s,
    sl_s,
    p1_snd,
    p1_rcv,
    p2_snd,
    g_part,
    g_sib,
    g_half,
    g_chip,
    in_send,
    in_recv,
    gain_send,
    gain_recv,
    p1_send,
    p1_recv,
    p2_send,
    p2_recv,
    ga_send,
    ga_recv,
    gb_send,
    gb_recv,
    gc_send,
    gc_recv,
    gd_send,
    gd_recv,
    c_ref,
    a_ref,
    w_in,
    b_ref,
    gain_ref,
    load_sem,
    q_s,
):
    blocks = w_in.shape[0]
    layer = lax.axis_index("layer")
    row = lax.axis_index("row")
    col = lax.axis_index("col")
    layers = lax.axis_size("layer")
    cols = lax.axis_size("col")
    core = lax.rem(col, 2)
    chip = 2 * row + col // 2
    strip = 2 * col + row
    lane = lax.broadcasted_iota(jnp.int32, (64, 128), 1)
    lane32 = lax.broadcasted_iota(jnp.int32, (32, 128), 1)
    lane16 = lax.broadcasted_iota(jnp.int32, (16, 128), 1)
    column = strip * OWN - HALO + lane
    inside = jnp.where((column >= 0) & (column < 2 * cols * OWN), 1.0, 0.0).astype(F32)
    own = jnp.where((lane >= HALO) & (lane < HALO + OWN), 1.0, 0.0).astype(F32)
    top = row == 0

    loads = [
        pltpu.make_async_copy(src, dst, load_sem.at[n])
        for n, (src, dst) in enumerate(
            (
                (c_hbm, c_ref),
                (a_hbm, a_ref),
                (w_hbm, w_in),
                (b_hbm, b_ref),
                (gain_hbm, gain_ref),
            )
        )
    ]
    for load in loads:
        load.start()

    barrier = pltpu.get_barrier_semaphore()

    pl.semaphore_signal(barrier, inc=1, device_id={"row": 1 - row}, device_id_type=MESH)
    for step in range(1, cols):
        for rho in range(2):
            pl.semaphore_signal(
                barrier,
                inc=1,
                device_id={"row": rho, "col": lax.rem(col + step, cols)},
                device_id_type=MESH,
            )
    for step in range(1, layers):
        for rho in range(2):
            pl.semaphore_signal(
                barrier,
                inc=1,
                device_id={"layer": lax.rem(layer + step, layers), "row": rho},
                device_id_type=MESH,
            )

    def pack(src, n):
        def one(h, carry):
            x = src[pl.ds(h, 64, stride=8), :]
            turned_by = jnp.where(top, 64, 0)
            middle = jnp.where(
                lane32 < 64,
                pltpu.roll(x[:32], turned_by, 1),
                pltpu.roll(x[32:], 64 - turned_by, 1),
            )
            flank = jnp.zeros((16, 128), F32)
            for g in range(4):
                part = pltpu.roll(
                    x[16 * g : 16 * g + 16],
                    jnp.where(top, (32 * g + 96) % 128, (32 * g + 64) % 128),
                    1,
                )
                flank = jnp.where(lane16 // 32 == g, part, flank)
            snd[n, h] = jnp.concatenate([middle, flank], axis=0).astype(BF)
            for side in range(2):
                edge = jnp.zeros((16, 128), F32)
                for g in range(4):
                    part = x[16 * g : 16 * g + 16]
                    shift = (32 * g + (32 if side == 0 else 0)) % 128
                    if shift:
                        part = pltpu.roll(part, shift, 1)
                    edge = jnp.where(lane16 // 32 == g, part, edge)
                edge_snd[side, n, h] = edge.astype(BF)
            return carry

        for h in range(8):
            one(h, 0)

    def exchange(n):
        yield remote(snd.at[n], rcv.at[n], in_send.at[n, 0], in_recv.at[n, 0], {"row": 1 - row})
        yield remote(
            edge_snd.at[0, n],
            edge_rcv.at[row, n],
            in_send.at[n, 1],
            in_recv.at[n, 1 + row],
            {"row": 0, "col": lax.rem(col + 1, cols)},
        )
        yield remote(
            edge_snd.at[1, n],
            edge_rcv.at[row, n],
            in_send.at[n, 2],
            in_recv.at[n, 1 + row],
            {"row": 1, "col": lax.rem(col + cols - 1, cols)},
        )

    def arrived(n):
        remote(snd.at[n], rcv.at[n], in_send.at[n, 0], in_recv.at[n, 0], {"row": 1 - row}).wait_recv()
        for rho in range(2):
            remote(
                edge_snd.at[0, n],
                edge_rcv.at[rho, n],
                in_send.at[n, 1],
                in_recv.at[n, 1 + rho],
                {"row": 1 - row},
            ).wait_recv()

    loads[0].wait()
    pack(c_ref, 0)
    pl.semaphore_wait(barrier, 2 * layers - 1 + 2 * (cols - 1))
    for copy in exchange(0):
        copy.start()
    loads[1].wait()
    pack(a_ref, 1)
    for copy in exchange(1):
        copy.start()

    def lay_weights(l, carry):
        for i in range(3):
            w_ref[l, 64 * i : 64 * i + 64, :] = jnp.concatenate(
                [w_in[l, 3 * i + j] * jnp.asarray(0.5, BF) for j in range(3)], axis=1
            )
            stack = w_in[l, 3 * i : 3 * i + 3].reshape(192, 64)
            wt_ref[l, 64 * i : 64 * i + 64, :] = (0.5 * stack.astype(F32)).T.astype(BF)
        return carry

    for load in loads[2:]:
        load.wait()
    lax.fori_loop(0, blocks, lay_weights, 0)
    tmp[...] = jnp.zeros_like(tmp)
    tmp[0:blocks, 0:64] = 0.5 * b_ref[...]
    tmp[blocks : blocks + 1, 0:64] = gain_ref[...]
    turned = tmp[...].T
    for l in range(blocks):
        b_s[l] = jnp.broadcast_to(turned[0:64, l : l + 1], (64, 128))
    gain_own[...] = jnp.broadcast_to(turned[0:64, blocks : blocks + 1], (64, 128))
    gain_snd[...] = tmp[blocks : blocks + 8, :]

    def holder(h):
        return 2 * lax.rem(h, 8) + row, h // 8

    rows_far_first = [
        8 * rho + lax.rem(layer // 2 + k, 8) for rho in (1 - row, row) for k in (5, 3, 4, 6, 2, 7, 1, 0)
    ]
    layers_far_first = [
        4 * lax.rem(layer // 4 + dx, 4) + lax.rem(layer + dz, 4)
        for dx, dz in (
            (2, 2), (2, 1), (2, 3), (1, 2), (3, 2), (1, 1), (3, 3), (1, 3), (3, 1),
            (2, 0), (0, 2), (1, 0), (3, 0), (0, 1), (0, 3),
        )
    ]

    def all_but_own(count, wait):
        for own_piece in (True, False):

            @pl.when((lax.rem(layer, 2) == row) == own_piece)
            def _():
                wait(count - 1 if own_piece else count)

    def stays(h):
        lam, rho = holder(h)
        return jnp.logical_and(lam == layer, rho == row)

    def gain_copy(h):
        lam, rho = holder(h)
        return remote(
            gain_snd,
            gain_rcv.at[layer],
            gain_send.at[0],
            gain_recv.at[0],
            {"layer": lam, "row": rho},
        )

    def p1_copy(n, h):
        lam, rho = holder(h)
        return remote(
            p1_snd.at[n, h],
            p1_rcv.at[n, layer],
            p1_send.at[n],
            p1_recv.at[n],
            {"layer": lam, "row": rho},
        )

    def start_unless_here(h, copy):
        @pl.when(jnp.logical_not(stays(h)))
        def _():
            copy.start()

    for h in rows_far_first:
        start_unless_here(h, gain_copy(h))

    @pl.when(lax.rem(layer, 2) == row)
    def _():
        gain_rcv[layer] = gain_snd[...]

    def spread(packed):
        return jnp.concatenate([pltpu.roll(packed, 32, 1), pltpu.roll(packed, 96, 1)], axis=0)

    def assemble(src, n, dst):
        shift = jnp.where(top, 32, 96)

        def halo(rho, h):
            packed = edge_rcv[rho, n, h].astype(F32)
            return jnp.concatenate(
                [
                    pltpu.roll(packed, jnp.where(top, (128 - 32 * g) % 128, (96 - 32 * g) % 128), 1)
                    for g in range(4)
                ],
                axis=0,
            )

        start = jnp.where(top, 0, 96)
        outer = (lane >= start) & (lane < start + 32)
        middle = (lane >= 32) & (lane < 96)

        def one(h, carry):
            x = src[pl.ds(h, 64, stride=8), :]
            dst[8 * row + h] = jnp.where(outer, halo(row, h), pltpu.roll(x, shift, 1)) * inside
            y = rcv[n, h].astype(F32)
            flank = jnp.concatenate(
                [
                    pltpu.roll(
                        y[32:48], jnp.where(top, (96 - 32 * g) % 128, (128 - 32 * g) % 128), 1
                    )
                    for g in range(4)
                ],
                axis=0,
            )
            dst[8 * (1 - row) + h] = (
                jnp.where(outer, halo(1 - row, h), jnp.where(middle, spread(y[:32]), flank))
                * inside
            )
            return carry

        for h in range(8):
            one(h, 0)

    arrived(0)
    assemble(c_ref, 0, phi_ref)

    zero = jnp.zeros((64, 128), BF)

    def forward(l, carry):
        w = w_ref[l]
        bias = b_s[l]
        z_s[l, 0] = zero
        z_s[l, 17] = zero
        later, last = None, None
        for m in range(8):
            pieces = []
            for h in (2 * m, 2 * m + 1):
                t = jnp.tanh(phi_ref[h]) * inside
                sl_s[l, h] = inside - t * t
                z_s[l, h + 1] = (t * own).astype(BF)
                pieces.append(
                    jnp.concatenate(
                        [
                            pltpu.roll(t, 1, 1).astype(BF),
                            t.astype(BF),
                            pltpu.roll(t, 127, 1).astype(BF),
                        ],
                        axis=0,
                    )
                )
            rhs = jnp.concatenate(pieces, axis=1)
            prod = jnp.dot(w, rhs, preferred_element_type=F32)
            p0, p1 = prod[:, :128], prod[:, 128:]
            if m > 0:
                phi_ref[2 * m - 1] = phi_ref[2 * m - 1] + bias + (later + p0[128:])
                first = last + p0[64:128] + p1[128:]
            else:
                first = p0[64:128] + p1[128:]
            phi_ref[2 * m] = phi_ref[2 * m] + bias + first
            later = p0[:64] + p1[64:128]
            last = p1[:64]
        phi_ref[15] = phi_ref[15] + bias + later
        return carry

    lax.fori_loop(0, blocks, forward, 0)

    def send_pieces(n, field, guess_own, keep):
        gain = gain_own[...] * keep
        shift = jnp.where(top, 32, 96)
        for u in range(8):
            for rho, guess in (
                (row, pltpu.roll(guess_own[pl.ds(u, 64, stride=8), :], shift, 1)),
                (1 - row, spread(rcv[n, u, 0:32, :].astype(F32))),
            ):
                r = field[8 * rho + u] - gain * guess
                p1_snd[n, 8 * rho + u] = jnp.where(
                    lane32 < 64, pltpu.roll(r[:32], 96, 1), pltpu.roll(r[32:], 32, 1)
                ).astype(BF)

        for h in rows_far_first:
            start_unless_here(h, p1_copy(n, h))

        @pl.when(lax.rem(layer, 2) == row)
        def _():
            p1_rcv[n, layer] = p1_snd[n, 8 * row + layer // 2]

    def p2_copy(n, e):
        return remote(
            p2_snd.at[n, e],
            pieces_out.at[n, layer],
            p2_send.at[n],
            p2_recv.at[n],
            {"layer": e},
        )

    def solve(n):
        first = 0 if n == 0 else layers - 1
        stride = 1 if n == 0 else -1

        all_but_own(
            16,
            lambda count: remote(
                p1_snd.at[n, pl.ds(0, count)],
                p1_rcv.at[n, pl.ds(0, count)],
                p1_send.at[n],
                p1_recv.at[n],
                {"row": 1 - row},
            ).wait_recv(),
        )
        state = jnp.zeros((32, 128), F32)
        for k in range(15):
            e = first + stride * k
            state = gain_pk[e] * state + p1_rcv[n, e].astype(F32)
            p2_snd[n, e + stride] = state.astype(BF)
        skipped = 0 if n == 0 else layers - 1

        for e in layers_far_first:

            @pl.when(e != skipped)
            def _():
                p2_copy(n, e).start()

        @pl.when(layer != skipped)
        def _():
            pieces_out[n, layer] = p2_snd[n, layer]

    send_pieces(0, phi_ref, c_ref, jnp.where(layer == 0, 0.0, 1.0))

    all_but_own(
        16,
        lambda count: remote(
            gain_rcv.at[pl.ds(0, count)],
            gain_rcv.at[pl.ds(0, count)],
            gain_send.at[0],
            gain_recv.at[0],
            {"row": 1 - row},
        ).wait_recv(),
    )
    for e in range(16):
        tmp[e : e + 1, :] = gain_rcv[e, 0:1, :]
    turned_all = tmp[...].T
    for e in range(16):
        gain_pk[e] = jnp.where(
            lane32 < 64,
            jnp.broadcast_to(turned_all[0:32, e : e + 1], (32, 128)),
            jnp.broadcast_to(turned_all[32:64, e : e + 1], (32, 128)),
        )

    half = pl.ds(pl.multiple_of(144 * core, 16), 144)
    other_half = pl.ds(pl.multiple_of(144 * (1 - core), 16), 144)
    beside = {"col": col + 1 - 2 * core}

    def ga_copy(l):
        return remote(g_part.at[l, other_half], g_sib.at[l], ga_send.at[l], ga_recv.at[l], beside)

    def at_chip(y):
        return {"row": y // 2, "col": 2 * lax.rem(y, 2) + core}

    def gb_copy(l):
        y = lax.rem(l, 4)
        return remote(
            g_half.at[l],
            g_chip.at[l // 4, chip],
            gb_send.at[l],
            gb_recv.at[l // 4, chip],
            at_chip(y),
        )

    def gc_copy(l, step):
        y = lax.rem(chip + step, 4)
        return remote(
            grad_out.at[l, half],
            grad_out.at[l, half],
            gc_send.at[l // 4, step - 1],
            gc_recv.at[l],
            at_chip(y),
        )

    def gd_copy(l):
        return remote(grad_out.at[l, half], grad_out.at[l, half], gd_send.at[l], gd_recv.at[l], beside)

    def to_owner(l):
        ga_copy(l).wait_recv()
        total = (g_part[l, half, :] + g_sib[l]).astype(BF)

        @pl.when(lax.rem(l, 4) == chip)
        def _():
            g_chip[l // 4, chip] = total

        @pl.when(lax.rem(l, 4) != chip)
        def _():
            g_half[l] = total
            gb_copy(l).start()

    def own_block(q):
        l = 4 * q + chip
        for step in range(1, 4):
            y = lax.rem(chip + step, 4)
            remote(
                g_half.at[l],
                g_chip.at[q, y],
                gb_send.at[l],
                gb_recv.at[q, y],
                at_chip(y),
            ).wait_recv()
        total = g_chip[q, 0].astype(F32) + g_chip[q, 1].astype(F32)
        total = total + g_chip[q, 2].astype(F32) + g_chip[q, 3].astype(F32)
        grad_out[l, half, :] = total.astype(BF)
        for step in range(1, 4):
            gc_copy(l, step).start()

    arrived(1)
    assemble(a_ref, 1, psi_ref)

    def keep_grad(l, grad):
        grad = 0.5 * grad
        g_part[l, 0:192, :] = grad[:, :128]
        g_part[l, 192:288, 0:64] = grad[:96, 128:192]
        g_part[l, 192:288, 64:128] = grad[96:, 128:192]
        ga_copy(l).start()

    def rows_of(l, first, last):
        return jnp.concatenate(
            [
                jnp.concatenate([z_s[l, h], z_s[l, h + 1], z_s[l, h + 2]], axis=0)
                for h in range(first, last)
            ],
            axis=1,
        )

    def backward(step, with_grad):
        l = blocks - 1 - step
        grad = jnp.zeros((192, 192), F32)
        wt = wt_ref[l]
        later, last = None, None
        for m in range(8):
            pieces = []
            for h in (2 * m, 2 * m + 1):
                a = psi_ref[h]
                pieces.append(
                    jnp.concatenate(
                        [
                            pltpu.roll(a, 127, 1).astype(BF),
                            a.astype(BF),
                            pltpu.roll(a, 1, 1).astype(BF),
                        ],
                        axis=0,
                    )
                )
            rhs = jnp.concatenate(pieces, axis=1)
            if with_grad:
                grad = grad + lax.dot_general(
                    rhs,
                    rows_of(l, 2 * m, 2 * m + 2),
                    (((1,), (1,)), ((), ())),
                    preferred_element_type=F32,
                )
            else:
                q_s[l, :, 256 * m : 256 * m + 256] = rhs
            prod = jnp.dot(wt, rhs, preferred_element_type=F32)
            p0, p1 = prod[:, :128], prod[:, 128:]
            if m > 0:
                psi_ref[2 * m - 1] = psi_ref[2 * m - 1] + sl_s[l, 2 * m - 1] * (later + p0[:64])
                first = last + p0[64:128] + p1[:64]
            else:
                first = p0[64:128] + p1[:64]
            psi_ref[2 * m] = psi_ref[2 * m] + sl_s[l, 2 * m] * first
            later = p0[128:] + p1[64:128]
            last = p1[128:]
        psi_ref[15] = psi_ref[15] + sl_s[l, 15] * later
        if with_grad:
            keep_grad(l, grad)

    def sweep_grads(step, carry):
        backward(step, True)

        @pl.when(step >= 2)
        def _():
            to_owner(blocks + 1 - step)

        return carry

    def sweep(step, carry):
        backward(step, False)
        return carry

    lax.fori_loop(0, SPLIT, sweep_grads, 0)
    lax.fori_loop(SPLIT, blocks, sweep, 0)
    send_pieces(1, psi_ref, a_ref, jnp.where(layer == layers - 1, 0.0, 1.0))

    def weight_grads(step, carry):
        l = blocks - 1 - step
        keep_grad(
            l,
            lax.dot_general(
                q_s[l], rows_of(l, 0, 16), (((1,), (1,)), ((), ())), preferred_element_type=F32
            ),
        )

        @pl.when(step >= SPLIT)
        def _():
            to_owner(l + 2)

        @pl.when(step == 5)
        def _():
            solve(0)

        return carry

    lax.fori_loop(SPLIT, blocks, weight_grads, 0)
    for l in (1, 0):
        to_owner(l)
    solve(1)
    own_block(1)
    own_block(0)

    def forward_half(k, carry):
        l = blocks - 1 - k

        @pl.when(lax.rem(l, 4) != chip)
        def _():
            remote(
                grad_out.at[l, half],
                grad_out.at[l, half],
                gc_send.at[0, 0],
                gc_recv.at[l],
                at_chip(lax.rem(l, 4)),
            ).wait_recv()

        gd_copy(l).start()
        return carry

    for n in range(2):
        for copy in exchange(n):
            copy.wait_send()

    def sent(count):
        remote(
            gain_rcv.at[pl.ds(0, count)],
            gain_rcv.at[pl.ds(0, count)],
            gain_send.at[0],
            gain_recv.at[0],
            {"row": 1 - row},
        ).wait_send()
        for n in range(2):
            remote(
                p1_snd.at[n, pl.ds(0, count)],
                p1_rcv.at[n, pl.ds(0, count)],
                p1_send.at[n],
                p1_recv.at[n],
                {"row": 1 - row},
            ).wait_send()

    all_but_own(16, sent)

    def drain_parts(l, carry):
        ga_copy(l).wait_send()

        @pl.when(lax.rem(l, 4) != chip)
        def _():
            gb_copy(l).wait_send()

        return carry

    lax.fori_loop(0, blocks, drain_parts, 0)
    lax.fori_loop(0, blocks, forward_half, 0)

    def p2_bytes(n, count):
        return remote(
            p2_snd.at[n, pl.ds(0, count)],
            pieces_out.at[n, pl.ds(0, count)],
            p2_send.at[n],
            p2_recv.at[n],
            {"row": 1 - row},
        )

    for n in range(2):
        skipped = 0 if n == 0 else layers - 1

        @pl.when(layer == skipped)
        def _():
            p2_bytes(n, 15).wait_send()

        @pl.when(layer != skipped)
        def _():
            p2_bytes(n, 14).wait_send()
            p2_bytes(n, 15).wait_recv()

    def drain_grads(l, carry):
        gd_copy(l).wait_send()
        remote(
            grad_out.at[l, other_half],
            grad_out.at[l, other_half],
            gd_send.at[l],
            gd_recv.at[l],
            beside,
        ).wait_recv()
        return carry

    lax.fori_loop(0, blocks, drain_grads, 0)
    for q in range(2):
        for step in range(1, 4):
            gc_copy(4 * q + chip, step).wait_send()


def fused(c, a, w, b, gain):
    blocks = w.shape[0]
    vm = pltpu.VMEM
    dma = pltpu.SemaphoreType.DMA
    return pl.pallas_call(
        fused_kernel,
        out_shape=(
            jax.ShapeDtypeStruct((2, 16, 32, 128), BF),
            jax.ShapeDtypeStruct((blocks, 288, 128), BF),
        ),
        in_specs=[pl.BlockSpec(memory_space=pltpu.HBM)] * 5,
        out_specs=[pl.BlockSpec(memory_space=vm)] * 2,
        scratch_shapes=[
            vm((2, 8, 48, 128), BF),
            vm((2, 8, 48, 128), BF),
            vm((2, 2, 8, 16, 128), BF),
            vm((2, 2, 8, 16, 128), BF),
            vm((128, 128), F32),
            vm((8, 128), F32),
            vm((16, 8, 128), F32),
            vm((16, 32, 128), F32),
            vm((64, 128), F32),
            vm((blocks, 192, 192), BF),
            vm((blocks, 192, 192), BF),
            vm((blocks, 64, 128), F32),
            vm((16, 64, 128), F32),
            vm((16, 64, 128), F32),
            vm((blocks, 18, 64, 128), BF),
            vm((blocks, 16, 64, 128), F32),
            vm((2, 16, 32, 128), BF),
            vm((2, 16, 32, 128), BF),
            vm((2, 16, 32, 128), BF),
            vm((blocks, 288, 128), F32),
            vm((blocks, 144, 128), F32),
            vm((blocks, 144, 128), BF),
            vm((2, 4, 144, 128), BF),
            dma((2, 3)),
            dma((2, 3)),
            dma((1,)),
            dma((1,)),
            dma((2,)),
            dma((2,)),
            dma((2,)),
            dma((2,)),
            dma((blocks,)),
            dma((blocks,)),
            dma((blocks,)),
            dma((2, 4)),
            dma((2, 3)),
            dma((blocks,)),
            dma((blocks,)),
            dma((blocks,)),
            vm(c.shape, F32),
            vm(a.shape, F32),
            vm(w.shape, BF),
            vm(b.shape, F32),
            vm(gain.shape, F32),
            dma((5,)),
            vm((blocks, 192, 2048), BF),
        ],
        compiler_params=pltpu.CompilerParams(
            vmem_limit_bytes=48 << 20, collective_id=0, has_side_effects=True
        ),
    )(c, a, w, b, gain)


def unpack_kernel(c_ref, a_ref, pieces_ref, grad_ref, c_out, a_out, g_out, c_s, a_s, g_s, sem):
    layer = lax.axis_index("layer")
    layers = lax.axis_size("layer")
    blocks = grad_ref.shape[0]
    lane32 = lax.broadcasted_iota(jnp.int32, (32, 128), 1)

    for n, whole, part, skipped in ((0, c_ref, c_s, 0), (1, a_ref, a_s, layers - 1)):

        @pl.when(layer == skipped)
        def _():
            pltpu.make_async_copy(whole, part, sem.at[blocks + 2 + n]).start()

    def states(n, whole, part, out, skipped):
        @pl.when(layer == skipped)
        def _():
            pltpu.make_async_copy(whole, part, sem.at[blocks + 2 + n]).wait()

        @pl.when(layer != skipped)
        def _():
            for u in range(8):
                left = pieces_ref[n, 2 * u].astype(F32)
                right = pieces_ref[n, 2 * u + 1].astype(F32)
                part[pl.ds(u, 32, stride=8), :] = jnp.where(
                    lane32 < 64, left, pltpu.roll(right, 64, 1)
                )
                part[pl.ds(256 + u, 32, stride=8), :] = jnp.where(
                    lane32 < 64, pltpu.roll(left, 64, 1), right
                )
        pltpu.make_async_copy(part, out, sem.at[blocks + n]).start()

    def one(l, carry):
        for j in range(3):
            g_s[l, j] = grad_ref[l, 64 * j : 64 * j + 64, 0:64].astype(F32)
            g_s[l, 3 + j] = grad_ref[l, 64 * j : 64 * j + 64, 64:128].astype(F32)
        g_s[l, 6] = grad_ref[l, 192:256, 0:64].astype(F32)
        g_s[l, 7, 0:32] = grad_ref[l, 256:288, 0:64].astype(F32)
        g_s[l, 7, 32:64] = grad_ref[l, 192:224, 64:128].astype(F32)
        g_s[l, 8] = grad_ref[l, 224:288, 64:128].astype(F32)
        pltpu.make_async_copy(g_s.at[l], g_out.at[l], sem.at[l]).start()
        return carry

    lax.fori_loop(0, blocks, one, 0)
    states(0, c_ref, c_s, c_out, 0)
    states(1, a_ref, a_s, a_out, layers - 1)
    for l in range(blocks):
        pltpu.make_async_copy(g_s.at[l], g_out.at[l], sem.at[l]).wait()
    pltpu.make_async_copy(c_s, c_out, sem.at[blocks]).wait()
    pltpu.make_async_copy(a_s, a_out, sem.at[blocks + 1]).wait()


def unpack(c, a, pieces, grad):
    blocks = grad.shape[0]
    vm = pltpu.VMEM
    far = pl.BlockSpec(memory_space=pltpu.HBM)
    return pl.pallas_call(
        unpack_kernel,
        out_shape=(
            jax.ShapeDtypeStruct((512, 128), F32),
            jax.ShapeDtypeStruct((512, 128), F32),
            jax.ShapeDtypeStruct((blocks, 9, 64, 64), F32),
        ),
        in_specs=[far, far, pl.BlockSpec(memory_space=vm), pl.BlockSpec(memory_space=vm)],
        out_specs=[far] * 3,
        scratch_shapes=[
            vm((512, 128), F32),
            vm((512, 128), F32),
            vm((blocks, 9, 64, 64), F32),
            pltpu.SemaphoreType.DMA((blocks + 4,)),
        ],
        compiler_params=pltpu.CompilerParams(vmem_limit_bytes=32 << 20),
    )(c, a, pieces, grad)


def local(c_guess, adjoint_guess, weights, biases, coarse_gain):
    c = c_guess.reshape(512, 128)
    a = adjoint_guess.reshape(512, 128)
    far = [
        pltpu.with_memory_space_constraint(x, pltpu.HBM)
        for x in (c, a, weights, biases, coarse_gain)
    ]
    pieces, grad = fused(*far)
    c_states, ends, weight_grad = unpack(far[0], far[1], pieces, grad)
    return (c_states.reshape(c_guess.shape), ends.reshape(c_guess.shape), weight_grad)


def solution(mesh):
    in_specs = (
        P("layer", None, None, "row", "col"),
        P("layer", None, None, "row", "col"),
        P("layer", None, None, None),
        P("layer", None),
        P("layer", None),
    )
    out_specs = (
        P("layer", None, None, "row", "col"),
        P("layer", None, None, "row", "col"),
        P("layer", None, None, None),
    )
    return jax.shard_map(local, mesh=mesh, in_specs=in_specs, out_specs=out_specs, check_vma=False)
```

```python
import jax
import jax.numpy as jnp
from jax import lax
from jax.experimental import pallas as pl
from jax.experimental.pallas import tpu as pltpu
from jax.sharding import PartitionSpec as P

HALO = 32
OWN = 64
SPLIT = 4
BF = jnp.bfloat16
F32 = jnp.float32
MESH = pl.DeviceIdType.MESH


def remote(src, dst, send, recv, where):
    return pltpu.make_async_remote_copy(
        src_ref=src,
        dst_ref=dst,
        send_sem=send,
        recv_sem=recv,
        device_id=where,
        device_id_type=MESH,
    )


def fused_kernel(
    c_hbm,
    a_hbm,
    w_hbm,
    b_hbm,
    gain_hbm,
    pieces_out,
    grad_out,
    snd,
    rcv,
    edge_snd,
    edge_rcv,
    tmp,
    gain_snd,
    gain_rcv,
    gain_pk,
    gain_own,
    w_ref,
    wt_ref,
    b_s,
    phi_ref,
    psi_ref,
    z_s,
    sl_s,
    p1_snd,
    p1_rcv,
    p2_snd,
    g_part,
    g_sib,
    g_half,
    g_chip,
    in_send,
    in_recv,
    gain_send,
    gain_recv,
    p1_send,
    p1_recv,
    p2_send,
    p2_recv,
    ga_send,
    ga_recv,
    gb_send,
    gb_recv,
    gc_send,
    gc_recv,
    gd_send,
    gd_recv,
    c_ref,
    a_ref,
    w_in,
    b_ref,
    gain_ref,
    load_sem,
    q_s,
):
    blocks = w_in.shape[0]
    layer = lax.axis_index("layer")
    row = lax.axis_index("row")
    col = lax.axis_index("col")
    layers = lax.axis_size("layer")
    cols = lax.axis_size("col")
    core = lax.rem(col, 2)
    chip = 2 * row + col // 2
    strip = 2 * col + row
    lane = lax.broadcasted_iota(jnp.int32, (64, 128), 1)
    lane32 = lax.broadcasted_iota(jnp.int32, (32, 128), 1)
    lane16 = lax.broadcasted_iota(jnp.int32, (16, 128), 1)
    column = strip * OWN - HALO + lane
    inside = jnp.where((column >= 0) & (column < 2 * cols * OWN), 1.0, 0.0).astype(F32)
    own = jnp.where((lane >= HALO) & (lane < HALO + OWN), 1.0, 0.0).astype(F32)
    top = row == 0

    loads = [
        pltpu.make_async_copy(src, dst, load_sem.at[n])
        for n, (src, dst) in enumerate(
            (
                (c_hbm, c_ref),
                (a_hbm, a_ref),
                (w_hbm, w_in),
                (b_hbm, b_ref),
                (gain_hbm, gain_ref),
            )
        )
    ]
    loads[0].start()

    barrier = pltpu.get_barrier_semaphore()

    pl.semaphore_signal(barrier, inc=1, device_id={"row": 1 - row}, device_id_type=MESH)
    for step in range(1, cols):
        for rho in range(2):
            pl.semaphore_signal(
                barrier,
                inc=1,
                device_id={"row": rho, "col": lax.rem(col + step, cols)},
                device_id_type=MESH,
            )
    for step in range(1, layers):
        for rho in range(2):
            pl.semaphore_signal(
                barrier,
                inc=1,
                device_id={"layer": lax.rem(layer + step, layers), "row": rho},
                device_id_type=MESH,
            )

    def pack(src, n):
        def one(h, carry):
            x = src[pl.ds(h, 64, stride=8), :]
            turned_by = jnp.where(top, 64, 0)
            middle = jnp.where(
                lane32 < 64,
                pltpu.roll(x[:32], turned_by, 1),
                pltpu.roll(x[32:], 64 - turned_by, 1),
            )
            flank = jnp.zeros((16, 128), F32)
            for g in range(4):
                part = pltpu.roll(
                    x[16 * g : 16 * g + 16],
                    jnp.where(top, (32 * g + 96) % 128, (32 * g + 64) % 128),
                    1,
                )
                flank = jnp.where(lane16 // 32 == g, part, flank)
            snd[n, h] = jnp.concatenate([middle, flank], axis=0).astype(BF)
            for side in range(2):
                edge = jnp.zeros((16, 128), F32)
                for g in range(4):
                    part = x[16 * g : 16 * g + 16]
                    shift = (32 * g + (32 if side == 0 else 0)) % 128
                    if shift:
                        part = pltpu.roll(part, shift, 1)
                    edge = jnp.where(lane16 // 32 == g, part, edge)
                edge_snd[side, n, h] = edge.astype(BF)
            return carry

        for h in range(8):
            one(h, 0)

    def exchange(n):
        yield remote(snd.at[n], rcv.at[n], in_send.at[n, 0], in_recv.at[n, 0], {"row": 1 - row})
        yield remote(
            edge_snd.at[0, n],
            edge_rcv.at[row, n],
            in_send.at[n, 1],
            in_recv.at[n, 1 + row],
            {"row": 0, "col": lax.rem(col + 1, cols)},
        )
        yield remote(
            edge_snd.at[1, n],
            edge_rcv.at[row, n],
            in_send.at[n, 2],
            in_recv.at[n, 1 + row],
            {"row": 1, "col": lax.rem(col + cols - 1, cols)},
        )

    def arrived(n):
        remote(snd.at[n], rcv.at[n], in_send.at[n, 0], in_recv.at[n, 0], {"row": 1 - row}).wait_recv()
        for rho in range(2):
            remote(
                edge_snd.at[0, n],
                edge_rcv.at[rho, n],
                in_send.at[n, 1],
                in_recv.at[n, 1 + rho],
                {"row": 1 - row},
            ).wait_recv()

    loads[0].wait()
    for load in loads[1:]:
        load.start()
    pack(c_ref, 0)
    pl.semaphore_wait(barrier, 2 * layers - 1 + 2 * (cols - 1))
    for copy in exchange(0):
        copy.start()
    loads[1].wait()
    pack(a_ref, 1)
    for copy in exchange(1):
        copy.start()

    def lay_weights(l, carry):
        for i in range(3):
            w_ref[l, 64 * i : 64 * i + 64, :] = jnp.concatenate(
                [w_in[l, 3 * i + j] * jnp.asarray(0.5, BF) for j in range(3)], axis=1
            )
            stack = w_in[l, 3 * i : 3 * i + 3].reshape(192, 64)
            wt_ref[l, 64 * i : 64 * i + 64, :] = (0.5 * stack.astype(F32)).T.astype(BF)
        return carry

    for load in loads[2:]:
        load.wait()
    lax.fori_loop(0, blocks, lay_weights, 0)
    tmp[...] = jnp.zeros_like(tmp)
    tmp[0:blocks, 0:64] = 0.5 * b_ref[...]
    tmp[blocks : blocks + 1, 0:64] = gain_ref[...]
    turned = tmp[...].T
    for l in range(blocks):
        b_s[l] = jnp.broadcast_to(turned[0:64, l : l + 1], (64, 128))
    gain_own[...] = jnp.broadcast_to(turned[0:64, blocks : blocks + 1], (64, 128))
    gain_snd[...] = tmp[blocks : blocks + 8, :]

    def holder(h):
        return 2 * lax.rem(h, 8) + row, h // 8

    rows_far_first = [
        8 * rho + lax.rem(layer // 2 + k, 8) for rho in (1 - row, row) for k in (5, 3, 4, 6, 2, 7, 1, 0)
    ]
    layers_far_first = [
        4 * lax.rem(layer // 4 + dx, 4) + lax.rem(layer + dz, 4)
        for dx, dz in (
            (2, 2), (2, 1), (2, 3), (1, 2), (3, 2), (1, 1), (3, 3), (1, 3), (3, 1),
            (2, 0), (0, 2), (1, 0), (3, 0), (0, 1), (0, 3),
        )
    ]

    def all_but_own(count, wait):
        for own_piece in (True, False):

            @pl.when((lax.rem(layer, 2) == row) == own_piece)
            def _():
                wait(count - 1 if own_piece else count)

    def stays(h):
        lam, rho = holder(h)
        return jnp.logical_and(lam == layer, rho == row)

    def gain_copy(h):
        lam, rho = holder(h)
        return remote(
            gain_snd,
            gain_rcv.at[layer],
            gain_send.at[0],
            gain_recv.at[0],
            {"layer": lam, "row": rho},
        )

    def p1_copy(n, h):
        lam, rho = holder(h)
        return remote(
            p1_snd.at[n, h],
            p1_rcv.at[n, layer],
            p1_send.at[n],
            p1_recv.at[n],
            {"layer": lam, "row": rho},
        )

    def start_unless_here(h, copy):
        @pl.when(jnp.logical_not(stays(h)))
        def _():
            copy.start()

    for h in rows_far_first:
        start_unless_here(h, gain_copy(h))

    @pl.when(lax.rem(layer, 2) == row)
    def _():
        gain_rcv[layer] = gain_snd[...]

    def spread(packed):
        return jnp.concatenate([pltpu.roll(packed, 32, 1), pltpu.roll(packed, 96, 1)], axis=0)

    def assemble(src, n, dst):
        shift = jnp.where(top, 32, 96)

        def halo(rho, h):
            packed = edge_rcv[rho, n, h].astype(F32)
            return jnp.concatenate(
                [
                    pltpu.roll(packed, jnp.where(top, (128 - 32 * g) % 128, (96 - 32 * g) % 128), 1)
                    for g in range(4)
                ],
                axis=0,
            )

        start = jnp.where(top, 0, 96)
        outer = (lane >= start) & (lane < start + 32)
        middle = (lane >= 32) & (lane < 96)

        def one(h, carry):
            x = src[pl.ds(h, 64, stride=8), :]
            dst[8 * row + h] = jnp.where(outer, halo(row, h), pltpu.roll(x, shift, 1)) * inside
            y = rcv[n, h].astype(F32)
            flank = jnp.concatenate(
                [
                    pltpu.roll(
                        y[32:48], jnp.where(top, (96 - 32 * g) % 128, (128 - 32 * g) % 128), 1
                    )
                    for g in range(4)
                ],
                axis=0,
            )
            dst[8 * (1 - row) + h] = (
                jnp.where(outer, halo(1 - row, h), jnp.where(middle, spread(y[:32]), flank))
                * inside
            )
            return carry

        for h in range(8):
            one(h, 0)

    arrived(0)
    assemble(c_ref, 0, phi_ref)

    zero = jnp.zeros((64, 128), BF)

    def forward(l, carry):
        w = w_ref[l]
        bias = b_s[l]
        z_s[l, 0] = zero
        z_s[l, 17] = zero
        later, last = None, None
        for m in range(8):
            pieces = []
            for h in (2 * m, 2 * m + 1):
                t = jnp.tanh(phi_ref[h]) * inside
                sl_s[l, h] = inside - t * t
                z_s[l, h + 1] = (t * own).astype(BF)
                pieces.append(
                    jnp.concatenate(
                        [
                            pltpu.roll(t, 1, 1).astype(BF),
                            t.astype(BF),
                            pltpu.roll(t, 127, 1).astype(BF),
                        ],
                        axis=0,
                    )
                )
            rhs = jnp.concatenate(pieces, axis=1)
            prod = jnp.dot(w, rhs, preferred_element_type=F32)
            p0, p1 = prod[:, :128], prod[:, 128:]
            if m > 0:
                phi_ref[2 * m - 1] = phi_ref[2 * m - 1] + bias + (later + p0[128:])
                first = last + p0[64:128] + p1[128:]
            else:
                first = p0[64:128] + p1[128:]
            phi_ref[2 * m] = phi_ref[2 * m] + bias + first
            later = p0[:64] + p1[64:128]
            last = p1[:64]
        phi_ref[15] = phi_ref[15] + bias + later
        return carry

    lax.fori_loop(0, blocks, forward, 0)

    def send_pieces(n, field, guess_own, keep):
        gain = gain_own[...] * keep
        shift = jnp.where(top, 32, 96)
        for u in range(8):
            for rho, guess in (
                (row, pltpu.roll(guess_own[pl.ds(u, 64, stride=8), :], shift, 1)),
                (1 - row, spread(rcv[n, u, 0:32, :].astype(F32))),
            ):
                r = field[8 * rho + u] - gain * guess
                p1_snd[n, 8 * rho + u] = jnp.where(
                    lane32 < 64, pltpu.roll(r[:32], 96, 1), pltpu.roll(r[32:], 32, 1)
                ).astype(BF)

        for h in rows_far_first:
            start_unless_here(h, p1_copy(n, h))

        @pl.when(lax.rem(layer, 2) == row)
        def _():
            p1_rcv[n, layer] = p1_snd[n, 8 * row + layer // 2]

    def p2_copy(n, e):
        return remote(
            p2_snd.at[n, e],
            pieces_out.at[n, layer],
            p2_send.at[n],
            p2_recv.at[n],
            {"layer": e},
        )

    def solve(n):
        first = 0 if n == 0 else layers - 1
        stride = 1 if n == 0 else -1

        all_but_own(
            16,
            lambda count: remote(
                p1_snd.at[n, pl.ds(0, count)],
                p1_rcv.at[n, pl.ds(0, count)],
                p1_send.at[n],
                p1_recv.at[n],
                {"row": 1 - row},
            ).wait_recv(),
        )
        state = jnp.zeros((32, 128), F32)
        for k in range(15):
            e = first + stride * k
            state = gain_pk[e] * state + p1_rcv[n, e].astype(F32)
            p2_snd[n, e + stride] = state.astype(BF)
        skipped = 0 if n == 0 else layers - 1

        for e in layers_far_first:

            @pl.when(e != skipped)
            def _():
                p2_copy(n, e).start()

        @pl.when(layer != skipped)
        def _():
            pieces_out[n, layer] = p2_snd[n, layer]

    send_pieces(0, phi_ref, c_ref, jnp.where(layer == 0, 0.0, 1.0))

    all_but_own(
        16,
        lambda count: remote(
            gain_rcv.at[pl.ds(0, count)],
            gain_rcv.at[pl.ds(0, count)],
            gain_send.at[0],
            gain_recv.at[0],
            {"row": 1 - row},
        ).wait_recv(),
    )
    for e in range(16):
        tmp[e : e + 1, :] = gain_rcv[e, 0:1, :]
    turned_all = tmp[...].T
    for e in range(16):
        gain_pk[e] = jnp.where(
            lane32 < 64,
            jnp.broadcast_to(turned_all[0:32, e : e + 1], (32, 128)),
            jnp.broadcast_to(turned_all[32:64, e : e + 1], (32, 128)),
        )

    half = pl.ds(pl.multiple_of(144 * core, 16), 144)
    other_half = pl.ds(pl.multiple_of(144 * (1 - core), 16), 144)
    beside = {"col": col + 1 - 2 * core}

    def ga_copy(l):
        return remote(g_part.at[l, other_half], g_sib.at[l], ga_send.at[l], ga_recv.at[l], beside)

    def at_chip(y):
        return {"row": y // 2, "col": 2 * lax.rem(y, 2) + core}

    def gb_copy(l):
        y = lax.rem(l, 4)
        return remote(
            g_half.at[l],
            g_chip.at[l // 4, chip],
            gb_send.at[l],
            gb_recv.at[l // 4, chip],
            at_chip(y),
        )

    def gc_copy(l, step):
        y = lax.rem(chip + step, 4)
        return remote(
            grad_out.at[l, half],
            grad_out.at[l, half],
            gc_send.at[l // 4, step - 1],
            gc_recv.at[l],
            at_chip(y),
        )

    def gd_copy(l):
        return remote(grad_out.at[l, half], grad_out.at[l, half], gd_send.at[l], gd_recv.at[l], beside)

    def to_owner(l):
        ga_copy(l).wait_recv()
        total = (g_part[l, half, :] + g_sib[l]).astype(BF)

        @pl.when(lax.rem(l, 4) == chip)
        def _():
            g_chip[l // 4, chip] = total

        @pl.when(lax.rem(l, 4) != chip)
        def _():
            g_half[l] = total
            gb_copy(l).start()

    def own_block(q):
        l = 4 * q + chip
        for step in range(1, 4):
            y = lax.rem(chip + step, 4)
            remote(
                g_half.at[l],
                g_chip.at[q, y],
                gb_send.at[l],
                gb_recv.at[q, y],
                at_chip(y),
            ).wait_recv()
        total = g_chip[q, 0].astype(F32) + g_chip[q, 1].astype(F32)
        total = total + g_chip[q, 2].astype(F32) + g_chip[q, 3].astype(F32)
        grad_out[l, half, :] = total.astype(BF)
        for step in range(1, 4):
            gc_copy(l, step).start()

    arrived(1)
    assemble(a_ref, 1, psi_ref)

    def keep_grad(l, grad):
        grad = 0.5 * grad
        g_part[l, 0:192, :] = grad[:, :128]
        g_part[l, 192:288, 0:64] = grad[:96, 128:192]
        g_part[l, 192:288, 64:128] = grad[96:, 128:192]
        ga_copy(l).start()

    def rows_of(l, first, last):
        return jnp.concatenate(
            [
                jnp.concatenate([z_s[l, h], z_s[l, h + 1], z_s[l, h + 2]], axis=0)
                for h in range(first, last)
            ],
            axis=1,
        )

    def backward(step, with_grad):
        l = blocks - 1 - step
        grad = jnp.zeros((192, 192), F32)
        wt = wt_ref[l]
        later, last = None, None
        for m in range(8):
            pieces = []
            for h in (2 * m, 2 * m + 1):
                a = psi_ref[h]
                pieces.append(
                    jnp.concatenate(
                        [
                            pltpu.roll(a, 127, 1).astype(BF),
                            a.astype(BF),
                            pltpu.roll(a, 1, 1).astype(BF),
                        ],
                        axis=0,
                    )
                )
            rhs = jnp.concatenate(pieces, axis=1)
            if with_grad:
                grad = grad + lax.dot_general(
                    rhs,
                    rows_of(l, 2 * m, 2 * m + 2),
                    (((1,), (1,)), ((), ())),
                    preferred_element_type=F32,
                )
            else:
                q_s[l, :, 256 * m : 256 * m + 256] = rhs
            prod = jnp.dot(wt, rhs, preferred_element_type=F32)
            p0, p1 = prod[:, :128], prod[:, 128:]
            if m > 0:
                psi_ref[2 * m - 1] = psi_ref[2 * m - 1] + sl_s[l, 2 * m - 1] * (later + p0[:64])
                first = last + p0[64:128] + p1[:64]
            else:
                first = p0[64:128] + p1[:64]
            psi_ref[2 * m] = psi_ref[2 * m] + sl_s[l, 2 * m] * first
            later = p0[128:] + p1[64:128]
            last = p1[128:]
        psi_ref[15] = psi_ref[15] + sl_s[l, 15] * later
        if with_grad:
            keep_grad(l, grad)

    def sweep_grads(step, carry):
        backward(step, True)

        @pl.when(step >= 2)
        def _():
            to_owner(blocks + 1 - step)

        return carry

    def sweep(step, carry):
        backward(step, False)
        return carry

    lax.fori_loop(0, SPLIT, sweep_grads, 0)
    lax.fori_loop(SPLIT, blocks, sweep, 0)
    send_pieces(1, psi_ref, a_ref, jnp.where(layer == layers - 1, 0.0, 1.0))

    def weight_grads(step, carry):
        l = blocks - 1 - step
        keep_grad(
            l,
            lax.dot_general(
                q_s[l], rows_of(l, 0, 16), (((1,), (1,)), ((), ())), preferred_element_type=F32
            ),
        )

        @pl.when(step >= SPLIT)
        def _():
            to_owner(l + 2)

        @pl.when(step == 5)
        def _():
            solve(0)

        return carry

    lax.fori_loop(SPLIT, blocks, weight_grads, 0)
    for l in (1, 0):
        to_owner(l)
    solve(1)
    own_block(1)
    own_block(0)

    def forward_half(k, carry):
        l = blocks - 1 - k

        @pl.when(lax.rem(l, 4) != chip)
        def _():
            remote(
                grad_out.at[l, half],
                grad_out.at[l, half],
                gc_send.at[0, 0],
                gc_recv.at[l],
                at_chip(lax.rem(l, 4)),
            ).wait_recv()

        gd_copy(l).start()
        return carry

    for n in range(2):
        for copy in exchange(n):
            copy.wait_send()

    def sent(count):
        remote(
            gain_rcv.at[pl.ds(0, count)],
            gain_rcv.at[pl.ds(0, count)],
            gain_send.at[0],
            gain_recv.at[0],
            {"row": 1 - row},
        ).wait_send()
        for n in range(2):
            remote(
                p1_snd.at[n, pl.ds(0, count)],
                p1_rcv.at[n, pl.ds(0, count)],
                p1_send.at[n],
                p1_recv.at[n],
                {"row": 1 - row},
            ).wait_send()

    all_but_own(16, sent)

    def drain_parts(l, carry):
        ga_copy(l).wait_send()

        @pl.when(lax.rem(l, 4) != chip)
        def _():
            gb_copy(l).wait_send()

        return carry

    lax.fori_loop(0, blocks, drain_parts, 0)
    lax.fori_loop(0, blocks, forward_half, 0)

    def p2_bytes(n, count):
        return remote(
            p2_snd.at[n, pl.ds(0, count)],
            pieces_out.at[n, pl.ds(0, count)],
            p2_send.at[n],
            p2_recv.at[n],
            {"row": 1 - row},
        )

    for n in range(2):
        skipped = 0 if n == 0 else layers - 1

        @pl.when(layer == skipped)
        def _():
            p2_bytes(n, 15).wait_send()

        @pl.when(layer != skipped)
        def _():
            p2_bytes(n, 14).wait_send()
            p2_bytes(n, 15).wait_recv()

    def drain_grads(l, carry):
        gd_copy(l).wait_send()
        remote(
            grad_out.at[l, other_half],
            grad_out.at[l, other_half],
            gd_send.at[l],
            gd_recv.at[l],
            beside,
        ).wait_recv()
        return carry

    lax.fori_loop(0, blocks, drain_grads, 0)
    for q in range(2):
        for step in range(1, 4):
            gc_copy(4 * q + chip, step).wait_send()


def fused(c, a, w, b, gain):
    blocks = w.shape[0]
    vm = pltpu.VMEM
    dma = pltpu.SemaphoreType.DMA
    return pl.pallas_call(
        fused_kernel,
        out_shape=(
            jax.ShapeDtypeStruct((2, 16, 32, 128), BF),
            jax.ShapeDtypeStruct((blocks, 288, 128), BF),
        ),
        in_specs=[pl.BlockSpec(memory_space=pltpu.HBM)] * 5,
        out_specs=[pl.BlockSpec(memory_space=vm)] * 2,
        scratch_shapes=[
            vm((2, 8, 48, 128), BF),
            vm((2, 8, 48, 128), BF),
            vm((2, 2, 8, 16, 128), BF),
            vm((2, 2, 8, 16, 128), BF),
            vm((128, 128), F32),
            vm((8, 128), F32),
            vm((16, 8, 128), F32),
            vm((16, 32, 128), F32),
            vm((64, 128), F32),
            vm((blocks, 192, 192), BF),
            vm((blocks, 192, 192), BF),
            vm((blocks, 64, 128), F32),
            vm((16, 64, 128), F32),
            vm((16, 64, 128), F32),
            vm((blocks, 18, 64, 128), BF),
            vm((blocks, 16, 64, 128), F32),
            vm((2, 16, 32, 128), BF),
            vm((2, 16, 32, 128), BF),
            vm((2, 16, 32, 128), BF),
            vm((blocks, 288, 128), F32),
            vm((blocks, 144, 128), F32),
            vm((blocks, 144, 128), BF),
            vm((2, 4, 144, 128), BF),
            dma((2, 3)),
            dma((2, 3)),
            dma((1,)),
            dma((1,)),
            dma((2,)),
            dma((2,)),
            dma((2,)),
            dma((2,)),
            dma((blocks,)),
            dma((blocks,)),
            dma((blocks,)),
            dma((2, 4)),
            dma((2, 3)),
            dma((blocks,)),
            dma((blocks,)),
            dma((blocks,)),
            vm(c.shape, F32),
            vm(a.shape, F32),
            vm(w.shape, BF),
            vm(b.shape, F32),
            vm(gain.shape, F32),
            dma((5,)),
            vm((blocks, 192, 2048), BF),
        ],
        compiler_params=pltpu.CompilerParams(
            vmem_limit_bytes=48 << 20, collective_id=0, has_side_effects=True
        ),
    )(c, a, w, b, gain)


def unpack_kernel(c_ref, a_ref, pieces_ref, grad_ref, c_out, a_out, g_out, c_s, a_s, g_s, sem):
    layer = lax.axis_index("layer")
    layers = lax.axis_size("layer")
    blocks = grad_ref.shape[0]
    lane32 = lax.broadcasted_iota(jnp.int32, (32, 128), 1)

    for n, whole, part, skipped in ((0, c_ref, c_s, 0), (1, a_ref, a_s, layers - 1)):

        @pl.when(layer == skipped)
        def _():
            pltpu.make_async_copy(whole, part, sem.at[blocks + 2 + n]).start()

    def states(n, whole, part, out, skipped):
        @pl.when(layer == skipped)
        def _():
            pltpu.make_async_copy(whole, part, sem.at[blocks + 2 + n]).wait()

        @pl.when(layer != skipped)
        def _():
            for u in range(8):
                left = pieces_ref[n, 2 * u].astype(F32)
                right = pieces_ref[n, 2 * u + 1].astype(F32)
                part[pl.ds(u, 32, stride=8), :] = jnp.where(
                    lane32 < 64, left, pltpu.roll(right, 64, 1)
                )
                part[pl.ds(256 + u, 32, stride=8), :] = jnp.where(
                    lane32 < 64, pltpu.roll(left, 64, 1), right
                )
        pltpu.make_async_copy(part, out, sem.at[blocks + n]).start()

    def one(l, carry):
        for j in range(3):
            g_s[l, j] = grad_ref[l, 64 * j : 64 * j + 64, 0:64].astype(F32)
            g_s[l, 3 + j] = grad_ref[l, 64 * j : 64 * j + 64, 64:128].astype(F32)
        g_s[l, 6] = grad_ref[l, 192:256, 0:64].astype(F32)
        g_s[l, 7, 0:32] = grad_ref[l, 256:288, 0:64].astype(F32)
        g_s[l, 7, 32:64] = grad_ref[l, 192:224, 64:128].astype(F32)
        g_s[l, 8] = grad_ref[l, 224:288, 64:128].astype(F32)
        pltpu.make_async_copy(g_s.at[l], g_out.at[l], sem.at[l]).start()
        return carry

    lax.fori_loop(0, blocks, one, 0)
    states(0, c_ref, c_s, c_out, 0)
    states(1, a_ref, a_s, a_out, layers - 1)
    for l in range(blocks):
        pltpu.make_async_copy(g_s.at[l], g_out.at[l], sem.at[l]).wait()
    pltpu.make_async_copy(c_s, c_out, sem.at[blocks]).wait()
    pltpu.make_async_copy(a_s, a_out, sem.at[blocks + 1]).wait()


def unpack(c, a, pieces, grad):
    blocks = grad.shape[0]
    vm = pltpu.VMEM
    far = pl.BlockSpec(memory_space=pltpu.HBM)
    return pl.pallas_call(
        unpack_kernel,
        out_shape=(
            jax.ShapeDtypeStruct((512, 128), F32),
            jax.ShapeDtypeStruct((512, 128), F32),
            jax.ShapeDtypeStruct((blocks, 9, 64, 64), F32),
        ),
        in_specs=[far, far, pl.BlockSpec(memory_space=vm), pl.BlockSpec(memory_space=vm)],
        out_specs=[far] * 3,
        scratch_shapes=[
            vm((512, 128), F32),
            vm((512, 128), F32),
            vm((blocks, 9, 64, 64), F32),
            pltpu.SemaphoreType.DMA((blocks + 4,)),
        ],
        compiler_params=pltpu.CompilerParams(vmem_limit_bytes=32 << 20),
    )(c, a, pieces, grad)


def local(c_guess, adjoint_guess, weights, biases, coarse_gain):
    c = c_guess.reshape(512, 128)
    a = adjoint_guess.reshape(512, 128)
    far = [
        pltpu.with_memory_space_constraint(x, pltpu.HBM)
        for x in (c, a, weights, biases, coarse_gain)
    ]
    pieces, grad = fused(*far)
    c_states, ends, weight_grad = unpack(far[0], far[1], pieces, grad)
    return (c_states.reshape(c_guess.shape), ends.reshape(c_guess.shape), weight_grad)


def solution(mesh):
    in_specs = (
        P("layer", None, None, "row", "col"),
        P("layer", None, None, "row", "col"),
        P("layer", None, None, None),
        P("layer", None),
        P("layer", None),
    )
    out_specs = (
        P("layer", None, None, "row", "col"),
        P("layer", None, None, "row", "col"),
        P("layer", None, None, None),
    )
    return jax.shard_map(local, mesh=mesh, in_specs=in_specs, out_specs=out_specs, check_vma=False)
```
